32 devices in a mesh: groups: 2 (over y), rows: 4 (over x, core), cols: 4 (over z).
Axes of the slice: x: 2, y: 2, z: 4, core: 2. Of those that a mesh axis runs over, the one named last changes fastest.
Arguments:
- q_fresh: bfloat16 [64, 128, 1536], P(('groups', 'rows'), 'cols'), parts along dimension 0, may hold values from -33 to 33
- k_fresh: bfloat16 [64, 128, 1536], P(('groups', 'rows'), 'cols'), parts along dimension 0, may hold values from -6.5 to 6.5
- v_fresh: bfloat16 [64, 128, 1536], P(('groups', 'rows'), 'cols'), parts along dimension 0, may hold values from -6 to 6
- k_stale: bfloat16 [64, 128, 1536], P(('groups', 'rows'), 'cols'), parts along dimension 0, may hold values from -6.375 to 6.375
- v_stale: bfloat16 [64, 128, 1536], P(('groups', 'rows'), 'cols'), parts along dimension 0, may hold values from -6 to 6
- text_k: bfloat16 [1024, 1536], P(('groups', 'rows', 'cols')), parts along dimension 0, may hold values from -6.375 to 6.375
- text_v: bfloat16 [1024, 1536], P(('groups', 'rows', 'cols')), parts along dimension 0, may hold values from -6 to 6
- conv_w: float32 [3, 3, 1536], replicated, may hold values from -0.8 to 0.8
- reads: int32 [8, 4, 2], P(('groups', 'rows'), 'cols'), parts along dimension 0, may hold values from 0 to 7, as said below
- pattern: int32 [16, 4, 2], P(('groups', 'rows'), 'cols'), parts along dimension 0, may hold values from 0 to 3, as said below
- text_blocks: int32 [16, 4, 2], P(('groups', 'rows'), 'cols'), parts along dimension 0, may hold values from 0 to 3, all different within a row
Outputs:
- attended: float32 [64, 128, 1536], P(('groups', 'rows'), 'cols'), parts along dimension 0
The draws below stay inside these ranges and needn't reach their ends.
There are 2 independent parts, one for each index of `groups`. The reference program is written for one: setup_inputs(seed, part) draws one part's arguments, and reference() takes and returns one part's arrays. A program takes and returns all parts, laid end to end along the dimension named above; an argument that names none is the same for every part. Nothing has to cross between parts.
Inputs may be any that keep to these rules, and one draw needn't show every extreme that they name: `reads`: entry f of device (r, c) names a block row of column strip c; the device row of that block row (the entry // 2) differs from r and from those of the device's other entries. `pattern`: each row lists 2 distinct slots; the row of block row i always lists slot i % 2, and every slot from 2 up is listed by some block of its device.
All inputs are finite; a program needn't handle non-finite values.
Results may differ from the reference program's by a relative error of at most 0.00075.
Values may be sent and summed in bfloat16 or wider, within the bound.
No kernel may reach another device: no remote copies, remote signals or barrier semaphores. Data moves between devices by JAX's collectives and lax.ppermute only.
A program may use at most 192 MiB of HBM per device.

```python
import math
import jax
import jax.numpy as jnp
from jax import lax

HEADS = 12
HEAD_DIM = 128
F = 1536
BLOCK_ROWS = 4
BLOCK_COLS = 32
TXT = 512
TXT_SEL = 2
GRID_R = 32
GRID_C = 128
BLK_DEV = 2
NBR = 8
TEXT_BLOCKS = 4
FETCH = 2
K_SEL = 2
N_ROWS = 4
N_COLS = 4


def query_key_pair(key):
    grid_shape = (GRID_R, GRID_C, HEADS * HEAD_DIM)
    key_keys, key_query = jax.random.split(jax.random.fold_in(key, 17), 2)
    key_values = 1.6 * jax.random.truncated_normal(key_keys, -4.0, 4.0, grid_shape, jnp.float32)
    query_values = 1.6 * jax.random.truncated_normal(key_query, -4.0, 4.0, grid_shape, jnp.float32)
    return (query_values, key_values)


def draw_q_fresh(key, part):
    return query_key_pair(key)[0].astype(jnp.bfloat16)


def draw_k_fresh(key, part):
    return query_key_pair(key)[1].astype(jnp.bfloat16)


def draw_reads(key, part):
    key_hot, key_noise, key_block = jax.random.split(jax.random.fold_in(key, 29), 3)
    reader = jnp.arange(N_ROWS, dtype=jnp.int32)[:, None, None]
    owner = jnp.arange(N_ROWS, dtype=jnp.int32)[None, None, :]
    hotness = jax.random.randint(key_hot, (1, N_COLS, N_ROWS), 0, 4)
    jitter = jax.random.randint(key_noise, (N_ROWS, N_COLS, N_ROWS), 0, 4096)
    ranking = (hotness * 4096 + jitter) * N_ROWS + owner
    forced = (reader == 0) & (owner == N_ROWS - 1) | (reader == N_ROWS - 1) & (owner == 0)
    ranking = jnp.where(forced, 5 * 4096 * N_ROWS + owner, ranking)
    ranking = jnp.where(reader == owner, -1, ranking)
    chosen = lax.top_k(ranking, FETCH)[1].astype(jnp.int32)
    block_pick = jax.random.randint(key_block, chosen.shape, 0, BLK_DEV)
    block_pick = jnp.where((reader == 0) & (chosen == N_ROWS - 1), BLK_DEV - 1, block_pick)
    block_pick = jnp.where((reader == N_ROWS - 1) & (chosen == 0), 0, block_pick)
    return (chosen * BLK_DEV + block_pick).astype(jnp.int32)


def draw_pattern(key, part):
    slot_count = BLK_DEV + FETCH
    key_turn, key_order = jax.random.split(jax.random.fold_in(key, 31), 2)
    own_slot = jnp.arange(NBR, dtype=jnp.int32)[:, None, None] % BLK_DEV
    slot_index = jnp.arange(slot_count, dtype=jnp.int32)[None, None, :]
    turn = jax.random.randint(key_turn, (N_ROWS, N_COLS, 1), 0, BLK_DEV).astype(jnp.int32)
    turn = jnp.repeat(turn, BLK_DEV, axis=0)
    covered = (slot_index - BLK_DEV + turn) % BLK_DEV == own_slot
    assigned = (slot_index == own_slot) | (slot_index >= BLK_DEV) & covered
    orders = jax.random.randint(key_order, (NBR, N_COLS, slot_count), 0, 4096).astype(jnp.int32) * slot_count + slot_index
    ranking = assigned.astype(jnp.int32) * (8192 * slot_count) + orders
    return lax.top_k(ranking, K_SEL)[1].astype(jnp.int32)


def block_levels(stream_key, shape, shards, least, high):
    loudness, own = 1.0, jax.random.fold_in(stream_key, 6)
    for dim, parts in shards:
        steps = jnp.exp(jax.random.uniform(jax.random.fold_in(own, dim), (parts,), jnp.float32, least / len(shards), high / len(shards)))
        loudness = loudness * jnp.repeat(steps, shape[dim] // parts).reshape([-1 if axis == dim else 1 for axis in range(len(shape))])
    return loudness


def choose_distinct(key, rows, count, top, lift):
    order = jax.random.permutation(jax.random.fold_in(key, 1), count)
    boost = order
    for power in range(3):
        boost = boost * boost // count
    boost = boost * lift // count
    chance = jax.random.randint(jax.random.fold_in(key, 2), (rows, count), 0, 4096) + boost
    holders = jax.random.permutation(jax.random.fold_in(key, 3), rows)[jnp.arange(count) % rows]
    chance = jnp.where(jnp.arange(rows)[:, None] == holders[None, :], 1 << 14, chance)
    merit = chance * count + jnp.arange(count)
    return lax.top_k(merit.astype(jnp.int32), top)[1].astype(jnp.int32)


def noise(key, shape, spread, most, cuts=(), held_as=jnp.bfloat16):
    entries = spread * jax.random.normal(key, shape, jnp.float32)
    if cuts:
        entries = entries * block_levels(key, shape, cuts, -0.22, 0.18)
    return jnp.clip(entries, -most, most).astype(held_as)


def setup_inputs(seed: int = 0, part: int = 0) -> dict:
    seeds = jax.random.split(jax.random.key(seed), 12)
    own_keys = jax.random.split(jax.random.fold_in(seeds[11], part), 12)
    return {
        "q_fresh": draw_q_fresh(jax.random.fold_in(jax.random.fold_in(seeds[11], part), 71), part),
        "k_fresh": draw_k_fresh(jax.random.fold_in(jax.random.fold_in(seeds[11], part), 71), part),
        "v_fresh": noise(own_keys[2], (GRID_R, GRID_C, F), 1.0, 6.0, ((0, 4), (1, 4))),
        "k_stale": noise(own_keys[3], (GRID_R, GRID_C, F), 1.6, 6.375, ((0, 4), (1, 4))),
        "v_stale": noise(own_keys[4], (GRID_R, GRID_C, F), 1.0, 6.0, ((0, 4), (1, 4))),
        "text_k": noise(own_keys[5], (TXT, F), 1.6, 6.375, ((0, 16),)),
        "text_v": noise(own_keys[6], (TXT, F), 1.0, 6.0, ((0, 16),)),
        "conv_w": noise(seeds[7], (3, 3, F), 0.2, 0.8, (), jnp.float32),
        "reads": draw_reads(jax.random.fold_in(jax.random.fold_in(seeds[11], part), 71), part),
        "pattern": draw_pattern(jax.random.fold_in(jax.random.fold_in(seeds[11], part), 71), part),
        "text_blocks": choose_distinct(own_keys[10], NBR * N_COLS, TEXT_BLOCKS, TXT_SEL, 0).reshape((NBR, N_COLS, TXT_SEL)),
    }


def blocks_of(grid_values):
    block_rows = grid_values.shape[0] // BLOCK_ROWS
    block_cols = grid_values.shape[1] // BLOCK_COLS
    feature_width = grid_values.shape[2]
    shaped = grid_values.reshape(block_rows, BLOCK_ROWS, block_cols, BLOCK_COLS, feature_width)
    return shaped.transpose(0, 2, 1, 3, 4).reshape(block_rows, block_cols, BLOCK_ROWS * BLOCK_COLS, feature_width)

def reference(q_fresh, k_fresh, v_fresh, k_stale, v_stale, text_k, text_v, conv_w, reads, pattern, text_blocks):
    per_block = BLOCK_ROWS * BLOCK_COLS
    feature_width = q_fresh.shape[2]
    query_blocks = blocks_of(q_fresh)
    fresh_keys = blocks_of(k_fresh)
    fresh_values = blocks_of(v_fresh)
    stale_keys = blocks_of(k_stale)
    stale_values = blocks_of(v_stale)
    text_key_blocks = text_k.reshape(TEXT_BLOCKS, per_block, feature_width)
    text_value_blocks = text_v.reshape(TEXT_BLOCKS, per_block, feature_width)

    def one_block(flat_index):
        block_row = flat_index // N_COLS
        block_col = flat_index % N_COLS
        slot_list = pattern[block_row, block_col]
        device_row = block_row // BLK_DEV
        is_fresh = slot_list < BLK_DEV
        fresh_row = device_row * BLK_DEV + jnp.minimum(slot_list, BLK_DEV - 1)
        stale_row = reads[device_row, block_col, jnp.clip(slot_list - BLK_DEV, 0, FETCH - 1)]
        key_rows = jnp.where(is_fresh[:, None, None], fresh_keys[fresh_row, block_col], stale_keys[stale_row, block_col])
        value_rows = jnp.where(is_fresh[:, None, None], fresh_values[fresh_row, block_col], stale_values[stale_row, block_col])
        text_pick = text_blocks[block_row, block_col]
        key_rows = jnp.concatenate([key_rows, text_key_blocks[text_pick]], axis=0).reshape(-1, HEADS, HEAD_DIM)
        value_rows = jnp.concatenate([value_rows, text_value_blocks[text_pick]], axis=0).reshape(-1, HEADS, HEAD_DIM)
        query_rows = query_blocks[block_row, block_col].reshape(per_block, HEADS, HEAD_DIM).astype(jnp.float32)
        scores = jnp.einsum('qhd,khd->hqk', query_rows, key_rows.astype(jnp.float32)) * (1.0 / math.sqrt(HEAD_DIM))
        row_peak = lax.optimization_barrier(jnp.max(scores, axis=-1, keepdims=True))
        weights = jnp.exp(scores - row_peak).astype(jnp.bfloat16)
        row_total = lax.optimization_barrier(jnp.sum(weights.astype(jnp.float32), axis=-1))
        mixed_rows = jnp.einsum('hqk,khd->qhd', weights.astype(jnp.float32), value_rows.astype(jnp.float32))
        return (mixed_rows / jnp.transpose(row_total)[:, :, None]).reshape(per_block, feature_width)
    per_block_out = lax.map(one_block, jnp.arange(NBR * N_COLS, dtype=jnp.int32))
    attention = per_block_out.reshape(NBR, N_COLS, BLOCK_ROWS, BLOCK_COLS, feature_width)
    attention = attention.transpose(0, 2, 1, 3, 4).reshape(GRID_R, GRID_C, feature_width)
    padded = jnp.pad(v_fresh.astype(jnp.float32), ((1, 1), (1, 1), (0, 0)))
    position_term = jnp.zeros((GRID_R, GRID_C, feature_width), jnp.float32)
    for row_tap in range(3):
        for col_tap in range(3):
            position_term = position_term + conv_w[row_tap, col_tap] * padded[row_tap:row_tap + GRID_R, col_tap:col_tap + GRID_C]
    return attention + position_term
```

```python
import functools
import math

import jax
import jax.numpy as jnp
from jax import lax
from jax.experimental import pallas as pl
from jax.experimental.pallas import tpu as pltpu
from jax.sharding import PartitionSpec as P

HEAD_DIM = 128
BLOCK_ROWS = 4
BLOCK_COLS = 32
PER_BLOCK = BLOCK_ROWS * BLOCK_COLS
SCORE_SCALE = 1.0 / math.sqrt(HEAD_DIM)
EXP2_SCALE = SCORE_SCALE * math.log2(math.e)
CHUNKS = 3
VMEM_LIMIT = 48 * 1024 * 1024


def extended(cells, sides, width):
    for axis, dim in sides:
        count = lax.axis_size(axis)
        ends = count - 1
        head = lax.slice_in_dim(cells, 0, width, axis=dim)
        tail = lax.slice_in_dim(cells, cells.shape[dim] - width, cells.shape[dim], axis=dim)
        cells = jnp.concatenate(
            [
                lax.ppermute(tail, axis, [(i, (i + 1) % count) for i in range(ends)]),
                cells,
                lax.ppermute(head, axis, [((i + 1) % count, i) for i in range(ends)]),
            ],
            axis=dim,
        )
    return cells


def position(v_fresh, conv_w):
    rows_here, cols_here, feature_width = v_fresh.shape
    rims = extended(v_fresh, (("rows", 0), ("cols", 1)), 1)
    position_term = jnp.zeros((rows_here, cols_here, feature_width), jnp.float32)
    for row_tap in range(3):
        for col_tap in range(3):
            position_term = position_term + conv_w[row_tap, col_tap] * rims[
                row_tap : row_tap + rows_here, col_tap : col_tap + cols_here
            ].astype(jnp.float32)
    return position_term


def split_heads(flat_rows):
    return flat_rows.reshape(flat_rows.shape[:-1] + (flat_rows.shape[-1] // HEAD_DIM, HEAD_DIM))


def attend(softmax_state, queries, key_blocks, value_blocks, allowed):
    old_peak, old_total, old_summed = softmax_state
    scores = (
        jnp.einsum(
            "bqhd,nkhd->bhqnk", queries, key_blocks, preferred_element_type=jnp.float32
        )
        * SCORE_SCALE
    )
    scores = jnp.where(allowed[:, None, None, :, None], scores, -1e30)
    new_peak = jnp.maximum(old_peak, jnp.max(scores, axis=(3, 4)))
    weights = jnp.exp(scores - new_peak[:, :, :, None, None]).astype(jnp.bfloat16)
    factor = jnp.exp(old_peak - new_peak)
    new_total = old_total * factor + jnp.sum(weights.astype(jnp.float32), axis=(3, 4))
    product = jnp.einsum(
        "bhqnk,nkhd->bqhd", weights, value_blocks, preferred_element_type=jnp.float32
    )
    new_summed = old_summed * jnp.transpose(factor, (0, 2, 1))[:, :, :, None] + product
    return (new_peak, new_total, new_summed)


def general_body(
    q_fresh, k_fresh, v_fresh, k_stale, v_stale, text_k, text_v, conv_w, reads, pattern, text_blocks
):
    rows_here, cols_here, feature_width = q_fresh.shape
    blocks_here = rows_here // BLOCK_ROWS
    head_count = feature_width // HEAD_DIM

    def as_blocks(grid_values):
        return split_heads(grid_values.reshape(blocks_here, PER_BLOCK, feature_width))

    queries = as_blocks(q_fresh)
    text_keys, text_values = (
        lax.all_gather(text_k, ("rows", "cols"), axis=0, tiled=True),
        lax.all_gather(text_v, ("rows", "cols"), axis=0, tiled=True),
    )
    text_count = text_keys.shape[0] // PER_BLOCK
    text_keys = split_heads(text_keys.reshape(text_count, PER_BLOCK, feature_width))
    text_values = split_heads(text_values.reshape(text_count, PER_BLOCK, feature_width))
    wanted = pattern[:, 0, :]
    fetch_rows = reads[0, 0, :]
    fetch_count = fetch_rows.shape[0]
    slot_count = blocks_here + fetch_count
    slot_mask = jnp.any(
        wanted[:, :, None] == jnp.arange(slot_count, dtype=jnp.int32)[None, None, :], axis=1
    )
    text_mask = jnp.any(
        text_blocks[:, 0, :, None] == jnp.arange(text_count, dtype=jnp.int32)[None, None, :], axis=1
    )
    softmax_state = (
        jnp.full((blocks_here, head_count, PER_BLOCK), -1e30, jnp.float32),
        jnp.zeros((blocks_here, head_count, PER_BLOCK), jnp.float32),
        jnp.zeros((blocks_here, PER_BLOCK, head_count, HEAD_DIM), jnp.float32),
    )
    softmax_state = attend(
        softmax_state,
        queries,
        jnp.concatenate([as_blocks(k_fresh), text_keys], axis=0),
        jnp.concatenate([as_blocks(v_fresh), text_values], axis=0),
        jnp.concatenate([slot_mask[:, :blocks_here], text_mask], axis=1),
    )
    chosen = jnp.where(
        wanted >= blocks_here, fetch_rows[jnp.clip(wanted - blocks_here, 0, fetch_count - 1)], -1
    )
    piece_keys = lax.all_gather(as_blocks(k_stale), "rows", axis=0, tiled=True)
    piece_values = lax.all_gather(as_blocks(v_stale), "rows", axis=0, tiled=True)
    block_rows = jnp.arange(piece_keys.shape[0], dtype=jnp.int32)
    piece_mask = jnp.any(chosen[:, :, None] == block_rows[None, None, :], axis=1)
    softmax_state = attend(softmax_state, queries, piece_keys, piece_values, piece_mask)
    _, final_total, final_summed = softmax_state
    mixed_rows = final_summed / jnp.transpose(final_total, (0, 2, 1))[:, :, :, None]
    attention = mixed_rows.reshape(rows_here, cols_here, feature_width)
    return attention + position(v_fresh, conv_w)


def head_scores(queries, keys):
    return lax.dot_general(
        queries, keys, (((1,), (1,)), ((), ())), preferred_element_type=jnp.float32
    )


def near_kernel(
    text_ref,
    q_ref,
    k_hbm,
    v_hbm,
    *rest,
):
    pieces = rest[:10]
    sum_ref, stat_ref, keys, values, sems = rest[10:]
    heads = q_ref.shape[1] // HEAD_DIM
    row = lax.axis_index("rows")
    col = lax.axis_index("cols")
    across, core = row // 2, row % 2
    shard = pieces[0].shape[0] // 4

    def start(source, first, target, block, at, count, which):
        pltpu.make_async_copy(
            source.at[pl.ds(first, count)], target.at[block, pl.ds(at, count)], sems.at[which, block]
        ).start()

    for block in range(2):
        start(k_hbm, block * PER_BLOCK, keys, block, 0, PER_BLOCK, 0)
        start(v_hbm, block * PER_BLOCK, values, block, 0, PER_BLOCK, 1)
        for turn in range(2):
            chosen = text_ref[block, 0, turn]
            first = pl.multiple_of(jnp.where(chosen // 2 == across, 0, 2 * shard), 2 * shard)
            at = PER_BLOCK * (1 + turn)

            def fetch(group):
                def one(source, step):
                    start(source, first, keys, block, at + step * shard, shard, 0)
                    start(source, first + shard, values, block, at + step * shard, shard, 1)

                for step in range(3):
                    one(group[step], step)

                @pl.when(col >= 2)
                def _():
                    one(group[3], 3)

                @pl.when(col < 2)
                def _():
                    one(group[4], 3)

            @pl.when(chosen % 2 == core)
            def _():
                fetch(pieces[:5])

            @pl.when(chosen % 2 != core)
            def _():
                fetch(pieces[5:])

    lane = lax.broadcasted_iota(jnp.int32, (PER_BLOCK, 128), 1)
    for block in range(2):
        rows = pl.ds(block * PER_BLOCK, PER_BLOCK)
        pltpu.make_async_copy(keys.at[block], keys.at[block], sems.at[0, block]).wait()
        pltpu.make_async_copy(values.at[block], values.at[block], sems.at[1, block]).wait()
        stats = jnp.zeros((PER_BLOCK, 128), jnp.float32)
        for head in range(heads):
            part = pl.ds(head * HEAD_DIM, HEAD_DIM)
            scores = head_scores(q_ref[rows, part], keys[block, :, part])
            peak = jnp.max(scores, axis=1, keepdims=True) * EXP2_SCALE
            weights = jnp.exp2(scores * EXP2_SCALE - peak).astype(jnp.bfloat16)
            total = jnp.sum(weights.astype(jnp.float32), axis=1, keepdims=True)
            sum_ref[rows, part] = jnp.dot(
                weights, values[block, :, part], preferred_element_type=jnp.float32
            )
            stats = jnp.where(lane == head, peak, stats)
            stats = jnp.where(lane == head + heads, total, stats)
        stat_ref[rows, :] = stats


def far_kernel(
    chunk, heads, reads_ref, pattern_ref, q_ref, sum_ref, stat_ref, term_ref, mate, across_, both, _, out_ref,
    keys, values, sems,
):
    row = lax.axis_index("rows")
    across, core = row // 2, row % 2
    half = mate.shape[0] // 2
    for block in range(2):
        slot = pattern_ref[block, 0, 0] + pattern_ref[block, 0, 1] - block - 2
        wanted = reads_ref[0, 0, slot]
        owner = wanted // 2
        first = pl.multiple_of((wanted % 2) * PER_BLOCK, PER_BLOCK)

        def fetch(source):
            pltpu.make_async_copy(
                source.at[pl.ds(first, PER_BLOCK)], keys.at[block], sems.at[0, block]
            ).start()
            pltpu.make_async_copy(
                source.at[pl.ds(half + first, PER_BLOCK)], values.at[block], sems.at[1, block]
            ).start()

        @pl.when(owner // 2 == across)
        def _():
            fetch(mate)

        @pl.when((owner // 2 != across) & (owner % 2 == core))
        def _():
            fetch(across_)

        @pl.when((owner // 2 != across) & (owner % 2 != core))
        def _():
            fetch(both)

    here = q_ref.shape[1] // HEAD_DIM
    for block in range(2):
        rows = pl.ds(block * PER_BLOCK, PER_BLOCK)
        pltpu.make_async_copy(keys.at[block], keys.at[block], sems.at[0, block]).wait()
        pltpu.make_async_copy(values.at[block], values.at[block], sems.at[1, block]).wait()
        for head in range(here):
            part = pl.ds(head * HEAD_DIM, HEAD_DIM)
            at = chunk * here + head
            old_peak = stat_ref[rows, at : at + 1]
            old_total = stat_ref[rows, at + heads : at + heads + 1]
            scores = head_scores(q_ref[rows, part], keys[block, :, part])
            peak = jnp.maximum(old_peak, jnp.max(scores, axis=1, keepdims=True) * EXP2_SCALE)
            weights = jnp.exp2(scores * EXP2_SCALE - peak).astype(jnp.bfloat16)
            factor = jnp.exp2(old_peak - peak)
            total = old_total * factor + jnp.sum(
                weights.astype(jnp.float32), axis=1, keepdims=True
            )
            product = jnp.dot(weights, values[block, :, part], preferred_element_type=jnp.float32)
            out_ref[rows, part] = (sum_ref[rows, part] * factor + product) / total + term_ref[
                rows, part
            ]


def body(
    q_fresh, k_fresh, v_fresh, k_stale, v_stale, text_k, text_v, conv_w, reads, pattern, text_blocks
):
    rows_here, cols_here, width = q_fresh.shape
    tokens = rows_here * cols_here
    heads = width // HEAD_DIM
    shard = text_k.shape[0]
    swap = [(r, (r + 2) % 4) for r in range(4)]
    mates = [(r, r ^ 1) for r in range(4)]

    def flat(grid_values):
        return grid_values.reshape(tokens, width)

    def to_mate(values):
        return lax.ppermute(values, "rows", mates)

    q, k, v = flat(q_fresh), flat(k_fresh), flat(v_fresh)
    k_old, v_old = flat(k_stale), flat(v_stale)

    across_k = lax.ppermute(text_k, "rows", swap)
    across_v = lax.ppermute(text_v, "rows", swap)
    step = width // CHUNKS
    packed = [
        jnp.concatenate(
            [k_old[:, i * step : (i + 1) * step], v_old[:, i * step : (i + 1) * step]], axis=0
        )
        for i in range(CHUNKS)
    ]
    far = [lax.ppermute(p, "rows", swap) for p in packed]

    text = jnp.concatenate([text_k, text_v, across_k, across_v], axis=0)
    left = lax.ppermute(text, "cols", [(i, (i + 1) % 4) for i in range(4)])
    right = lax.ppermute(text, "cols", [((i + 1) % 4, i) for i in range(4)])
    upper = lax.ppermute(left, "cols", [(1, 2), (2, 3)])
    lower = lax.ppermute(right, "cols", [(1, 0), (2, 1)])
    pieces = [text, left, right, upper, lower]
    pieces = pieces + [to_mate(p) for p in pieces]
    term = position(v_fresh, conv_w).reshape(tokens, width)

    any_space = pl.BlockSpec(memory_space=pl.ANY)
    params = pltpu.CompilerParams(vmem_limit_bytes=VMEM_LIMIT)
    key_count = PER_BLOCK * 3
    summed, stats = pl.pallas_call(
        near_kernel,
        out_shape=(
            jax.ShapeDtypeStruct((tokens, width), jnp.float32),
            jax.ShapeDtypeStruct((tokens, 128), jnp.float32),
        ),
        grid_spec=pltpu.PrefetchScalarGridSpec(
            num_scalar_prefetch=1,
            grid=(1,),
            in_specs=[pl.BlockSpec((tokens, width), lambda i, *_: (0, 0))] + [any_space] * 12,
            out_specs=(
                pl.BlockSpec((tokens, width), lambda i, *_: (0, 0)),
                pl.BlockSpec((tokens, 128), lambda i, *_: (0, 0)),
            ),
            scratch_shapes=[
                pltpu.VMEM((2, key_count, width), jnp.bfloat16),
                pltpu.VMEM((2, key_count, width), jnp.bfloat16),
                pltpu.SemaphoreType.DMA((2, 2)),
            ],
        ),
        compiler_params=params,
        name="near",
    )(text_blocks, q, k, v, *pieces)

    out = None
    for chunk in range(CHUNKS):
        arrived = [to_mate(packed[chunk]), far[chunk], to_mate(far[chunk])]
        part = pl.BlockSpec((tokens, step), lambda i, *_, chunk=chunk: (0, chunk))
        out = pl.pallas_call(
            functools.partial(far_kernel, chunk, heads)
            if out is not None
            else lambda *refs: far_kernel(0, heads, *refs[:9], None, *refs[9:]),
            out_shape=jax.ShapeDtypeStruct((tokens, width), jnp.float32),
            grid_spec=pltpu.PrefetchScalarGridSpec(
                num_scalar_prefetch=2,
                grid=(1,),
                in_specs=[
                    part,
                    part,
                    pl.BlockSpec((tokens, 128), lambda i, *_: (0, 0)),
                    part,
                    any_space,
                    any_space,
                    any_space,
                ]
                + ([any_space] if out is not None else []),
                out_specs=part,
                scratch_shapes=[
                    pltpu.VMEM((2, PER_BLOCK, step), jnp.bfloat16),
                    pltpu.VMEM((2, PER_BLOCK, step), jnp.bfloat16),
                    pltpu.SemaphoreType.DMA((2, 2)),
                ],
            ),
            input_output_aliases={9: 0} if out is not None else {},
            compiler_params=params,
            name=f"far{chunk}",
        )(reads, pattern, q, summed, stats, term, *arrived, *([out] if out is not None else []))
    return out.reshape(rows_here, cols_here, width)


def fits(mesh, reads, pattern, text_k):
    sizes = dict(mesh.shape)
    return (
        sizes["rows"] == 4
        and sizes["cols"] == 4
        and reads.shape[-1] == 2
        and pattern.shape[-1] == 2
        and pattern.shape[0] == 2 * sizes["groups"] * 4
        and text_k.shape[0] == sizes["groups"] * 4 * PER_BLOCK
    )


def solution(mesh):
    grid = P(("groups", "rows"), "cols", None)
    text = P(("groups", "rows", "cols"), None)
    in_specs = (grid, grid, grid, grid, grid, text, text, P(), grid, grid, grid)

    def program(*args):
        chosen = body if fits(mesh, args[8], args[9], args[5]) else general_body
        return jax.shard_map(
            chosen, mesh=mesh, in_specs=in_specs, out_specs=grid, check_vma=False
        )(*args)

    return program
```

```python
import functools
import math

import jax
import jax.numpy as jnp
from jax import lax
from jax.experimental import pallas as pl
from jax.experimental.pallas import tpu as pltpu
from jax.sharding import PartitionSpec as P

HEAD_DIM = 128
BLOCK_ROWS = 4
BLOCK_COLS = 32
PER_BLOCK = BLOCK_ROWS * BLOCK_COLS
SCORE_SCALE = 1.0 / math.sqrt(HEAD_DIM)
EXP2_SCALE = SCORE_SCALE * math.log2(math.e)
CHUNK_HEADS = (4, 5, 3)
GROUP = 8
VMEM_LIMIT = 24 * 1024 * 1024


def extended(cells, sides, width):
    for axis, dim in sides:
        count = lax.axis_size(axis)
        ends = count - 1
        head = lax.slice_in_dim(cells, 0, width, axis=dim)
        tail = lax.slice_in_dim(cells, cells.shape[dim] - width, cells.shape[dim], axis=dim)
        cells = jnp.concatenate(
            [
                lax.ppermute(tail, axis, [(i, (i + 1) % count) for i in range(ends)]),
                cells,
                lax.ppermute(head, axis, [((i + 1) % count, i) for i in range(ends)]),
            ],
            axis=dim,
        )
    return cells


def position(v_fresh, conv_w):
    rows_here, cols_here, feature_width = v_fresh.shape
    rims = extended(v_fresh, (("rows", 0), ("cols", 1)), 1)
    position_term = jnp.zeros((rows_here, cols_here, feature_width), jnp.float32)
    for row_tap in range(3):
        for col_tap in range(3):
            position_term = position_term + conv_w[row_tap, col_tap] * rims[
                row_tap : row_tap + rows_here, col_tap : col_tap + cols_here
            ].astype(jnp.float32)
    return position_term


def split_heads(flat_rows):
    return flat_rows.reshape(flat_rows.shape[:-1] + (flat_rows.shape[-1] // HEAD_DIM, HEAD_DIM))


def attend(softmax_state, queries, key_blocks, value_blocks, allowed):
    old_peak, old_total, old_summed = softmax_state
    scores = (
        jnp.einsum(
            "bqhd,nkhd->bhqnk", queries, key_blocks, preferred_element_type=jnp.float32
        )
        * SCORE_SCALE
    )
    scores = jnp.where(allowed[:, None, None, :, None], scores, -1e30)
    new_peak = jnp.maximum(old_peak, jnp.max(scores, axis=(3, 4)))
    weights = jnp.exp(scores - new_peak[:, :, :, None, None]).astype(jnp.bfloat16)
    factor = jnp.exp(old_peak - new_peak)
    new_total = old_total * factor + jnp.sum(weights.astype(jnp.float32), axis=(3, 4))
    product = jnp.einsum(
        "bhqnk,nkhd->bqhd", weights, value_blocks, preferred_element_type=jnp.float32
    )
    new_summed = old_summed * jnp.transpose(factor, (0, 2, 1))[:, :, :, None] + product
    return (new_peak, new_total, new_summed)


def general_body(
    q_fresh, k_fresh, v_fresh, k_stale, v_stale, text_k, text_v, conv_w, reads, pattern, text_blocks
):
    rows_here, cols_here, feature_width = q_fresh.shape
    blocks_here = rows_here // BLOCK_ROWS
    head_count = feature_width // HEAD_DIM

    def as_blocks(grid_values):
        return split_heads(grid_values.reshape(blocks_here, PER_BLOCK, feature_width))

    queries = as_blocks(q_fresh)
    text_keys, text_values = (
        lax.all_gather(text_k, ("rows", "cols"), axis=0, tiled=True),
        lax.all_gather(text_v, ("rows", "cols"), axis=0, tiled=True),
    )
    text_count = text_keys.shape[0] // PER_BLOCK
    text_keys = split_heads(text_keys.reshape(text_count, PER_BLOCK, feature_width))
    text_values = split_heads(text_values.reshape(text_count, PER_BLOCK, feature_width))
    wanted = pattern[:, 0, :]
    fetch_rows = reads[0, 0, :]
    fetch_count = fetch_rows.shape[0]
    slot_count = blocks_here + fetch_count
    slot_mask = jnp.any(
        wanted[:, :, None] == jnp.arange(slot_count, dtype=jnp.int32)[None, None, :], axis=1
    )
    text_mask = jnp.any(
        text_blocks[:, 0, :, None] == jnp.arange(text_count, dtype=jnp.int32)[None, None, :], axis=1
    )
    softmax_state = (
        jnp.full((blocks_here, head_count, PER_BLOCK), -1e30, jnp.float32),
        jnp.zeros((blocks_here, head_count, PER_BLOCK), jnp.float32),
        jnp.zeros((blocks_here, PER_BLOCK, head_count, HEAD_DIM), jnp.float32),
    )
    softmax_state = attend(
        softmax_state,
        queries,
        jnp.concatenate([as_blocks(k_fresh), text_keys], axis=0),
        jnp.concatenate([as_blocks(v_fresh), text_values], axis=0),
        jnp.concatenate([slot_mask[:, :blocks_here], text_mask], axis=1),
    )
    chosen = jnp.where(
        wanted >= blocks_here, fetch_rows[jnp.clip(wanted - blocks_here, 0, fetch_count - 1)], -1
    )
    piece_keys = lax.all_gather(as_blocks(k_stale), "rows", axis=0, tiled=True)
    piece_values = lax.all_gather(as_blocks(v_stale), "rows", axis=0, tiled=True)
    block_rows = jnp.arange(piece_keys.shape[0], dtype=jnp.int32)
    piece_mask = jnp.any(chosen[:, :, None] == block_rows[None, None, :], axis=1)
    softmax_state = attend(softmax_state, queries, piece_keys, piece_values, piece_mask)
    _, final_total, final_summed = softmax_state
    mixed_rows = final_summed / jnp.transpose(final_total, (0, 2, 1))[:, :, :, None]
    attention = mixed_rows.reshape(rows_here, cols_here, feature_width)
    return attention + position(v_fresh, conv_w)


def head_scores(queries, keys):
    return lax.dot_general(
        queries, keys, (((1,), (1,)), ((), ())), preferred_element_type=jnp.float32
    )


def pack_far_kernel(k_hbm, v_hbm, *refs):
    outs, sems = refs[:-1], refs[-1]
    tokens = k_hbm.shape[0]
    copies = []
    first = 0
    for index, out in enumerate(outs):
        part = pl.ds(first, out.shape[1])
        first += out.shape[1]
        for which, source in enumerate((k_hbm, v_hbm)):
            copies.append(
                pltpu.make_async_copy(
                    source.at[:, part], out.at[pl.ds(which * tokens, tokens)], sems.at[index, which]
                )
            )
    for copy in copies:
        copy.start()
    for copy in copies:
        copy.wait()


def above_below(beside, diagonal):
    first_core = lax.axis_index("rows") % 2 == 0
    return (
        jnp.where(first_core, diagonal, beside),
        jnp.where(first_core, beside, diagonal),
    )


def pack_text_kernel(text_k, text_v, across_k, across_v, cells, beside, diagonal, plus, minus):
    shard = text_k.shape[0]
    rows_here, cols_here, width = cells.shape
    for index, source in enumerate((text_k, text_v, across_k, across_v)):
        part = pl.ds(index * shard, shard)
        value = source[...]
        plus[part, :] = value
        minus[part, :] = value
    above, below = above_below(beside[...], diagonal[...])
    rows = [above] + [cells[i] for i in range(rows_here)] + [below]
    rows = [row.astype(jnp.float32) for row in rows]
    spare = jnp.zeros((16 - len(rows), width), jnp.float32)
    for target, at in ((plus, cols_here - 1), (minus, 0)):
        edge = jnp.concatenate([row[at : at + 1] for row in rows] + [spare], axis=0)
        target[pl.ds(4 * shard, 16), :] = edge.astype(target.dtype)


def term_kernel(cells, beside, diagonal, left, right, weights, out):
    rows_here, cols_here, width = cells.shape
    col = lax.axis_index("cols")
    edge_at = left.shape[0] - 16
    place = lax.broadcasted_iota(jnp.int32, (cols_here, HEAD_DIM), 0)
    for lane in range(width // HEAD_DIM):
        part = pl.ds(lane * HEAD_DIM, HEAD_DIM)
        above, below = above_below(beside[:, part], diagonal[:, part])
        lefts = left[pl.ds(edge_at, 16), part].astype(jnp.float32)
        rights = right[pl.ds(edge_at, 16), part].astype(jnp.float32)
        lefts = jnp.where(col > 0, lefts, 0.0)
        rights = jnp.where(col < 3, rights, 0.0)
        taps = []
        for row in range(rows_here + 2):
            if row == 0:
                centre = above
            elif row == rows_here + 1:
                centre = below
            else:
                centre = cells[row - 1, :, part]
            centre = centre.astype(jnp.float32)
            before = jnp.where(place == 0, lefts[row : row + 1], pltpu.roll(centre, 1, 0))
            after = jnp.where(
                place == cols_here - 1, rights[row : row + 1], pltpu.roll(centre, cols_here - 1, 0)
            )
            taps.append((before, centre, after))
        for row in range(rows_here):
            total = None
            for row_tap in range(3):
                for col_tap in range(3):
                    piece = weights[row_tap, col_tap : col_tap + 1, part] * taps[row + row_tap][col_tap]
                    total = piece if total is None else total + piece
            out[pl.ds(row * cols_here, cols_here), part] = total


def attend_kernel(first_head, reads_ref, pattern_ref, text_ref, q, k, v, *refs):
    pieces, (mate_k, mate_v, across_kv, both_kv, term) = refs[:10], refs[10:15]
    out = refs[-1]
    row, col = lax.axis_index("rows"), lax.axis_index("cols")
    across, core = row // 2, row % 2
    shard = (pieces[0].shape[0] - 16) // 4
    half = across_kv.shape[0] // 2
    head_count = across_kv.shape[1] // HEAD_DIM

    def lanes(head):
        return pl.ds((first_head + head) * HEAD_DIM, HEAD_DIM)

    def text_part(chosen, head, which):
        from_own = chosen % 2 == core
        first = jnp.where(chosen // 2 == across, 0, 2 * shard) + which * shard
        rows = pl.ds(pl.multiple_of(first, shard), shard)
        part = lanes(head)

        def one(own, other):
            return jnp.where(from_own, own[rows, part], other[rows, part])

        last = jnp.where(col >= 2, one(pieces[3], pieces[8]), one(pieces[4], pieces[9]))
        return [one(pieces[i], pieces[i + 5]) for i in range(3)] + [last]

    def far_part(block, head, which):
        slot = pattern_ref[block, 0, 0] + pattern_ref[block, 0, 1] - block - 2
        wanted = reads_ref[0, 0, slot]
        owner = wanted // 2
        first = (wanted % 2) * PER_BLOCK
        rows = pl.ds(pl.multiple_of(first, PER_BLOCK), PER_BLOCK)
        packed = pl.ds(pl.multiple_of(first + which * half, PER_BLOCK), PER_BLOCK)
        mate = (mate_k, mate_v)[which][rows, lanes(head)]
        here = pl.ds(head * HEAD_DIM, HEAD_DIM)
        straight, crossed = across_kv[packed, here], both_kv[packed, here]
        arrived = jnp.where(owner % 2 == core, straight, crossed)
        return jnp.where(owner // 2 == across, mate, arrived)

    def gathered(block, head, which):
        own = (k, v)[which][pl.ds(block * PER_BLOCK, PER_BLOCK), lanes(head)]
        parts = [own]
        for turn in range(2):
            parts += text_part(text_ref[block, 0, turn], head, which)
        return jnp.concatenate(parts + [far_part(block, head, which)], axis=0)

    jobs = [(block, head) for head in range(head_count) for block in range(2)]
    for at in range(0, len(jobs), GROUP):
        group = jobs[at : at + GROUP]
        scores = [
            head_scores(
                q[pl.ds(block * PER_BLOCK, PER_BLOCK), lanes(head)], gathered(block, head, 0)
            )
            for block, head in group
        ]
        peaks = [jnp.max(s, axis=1, keepdims=True) * EXP2_SCALE for s in scores]
        weights = [
            jnp.exp2(s * EXP2_SCALE - peak).astype(jnp.bfloat16) for s, peak in zip(scores, peaks)
        ]
        totals = [jnp.sum(w.astype(jnp.float32), axis=1, keepdims=True) for w in weights]
        products = [
            jnp.dot(w, gathered(block, head, 1), preferred_element_type=jnp.float32)
            for w, (block, head) in zip(weights, group)
        ]
        for product, total, (block, head) in zip(products, totals, group):
            rows = pl.ds(block * PER_BLOCK, PER_BLOCK)
            out[rows, pl.ds(head * HEAD_DIM, HEAD_DIM)] = product / total + term[rows, lanes(head)]


def body(
    q_fresh, k_fresh, v_fresh, k_stale, v_stale, text_k, text_v, conv_w, reads, pattern, text_blocks
):
    rows_here, cols_here, width = q_fresh.shape
    tokens = rows_here * cols_here
    shard = text_k.shape[0]
    swap = [(r, (r + 2) % 4) for r in range(4)]
    mates = [(r, r ^ 1) for r in range(4)]
    row = lax.axis_index("rows")
    in_vmem = pl.BlockSpec(memory_space=pltpu.VMEM)
    anywhere = pl.BlockSpec(memory_space=pl.ANY)
    params = pltpu.CompilerParams(vmem_limit_bytes=VMEM_LIMIT)
    bf16 = jnp.bfloat16

    def flat(grid_values):
        return grid_values.reshape(tokens, width)

    def to_mate(values):
        return lax.ppermute(values, "rows", mates)

    across_k = lax.ppermute(text_k, "rows", swap)
    across_v = lax.ppermute(text_v, "rows", swap)
    beside = to_mate(jnp.where(row % 2 == 0, v_fresh[rows_here - 1], v_fresh[0]))
    diagonal = lax.ppermute(
        jnp.where(row < 2, v_fresh[rows_here - 1], v_fresh[0]), "rows", [(1, 2), (2, 1)]
    )
    packed = pl.pallas_call(
        pack_far_kernel,
        out_shape=tuple(
            jax.ShapeDtypeStruct((2 * tokens, n * HEAD_DIM), bf16) for n in CHUNK_HEADS
        ),
        in_specs=[anywhere] * 2,
        out_specs=(in_vmem,) * len(CHUNK_HEADS),
        scratch_shapes=[pltpu.SemaphoreType.DMA((len(CHUNK_HEADS), 2))],
        compiler_params=params,
        name="pack_far",
    )(flat(k_stale), flat(v_stale))
    far = [lax.ppermute(p, "rows", swap) for p in packed]
    mate_k, mate_v = to_mate(flat(k_stale)), to_mate(flat(v_stale))

    plus, minus = pl.pallas_call(
        pack_text_kernel,
        out_shape=(jax.ShapeDtypeStruct((4 * shard + 16, width), bf16),) * 2,
        in_specs=[in_vmem] * 7,
        out_specs=(in_vmem,) * 2,
        compiler_params=params,
        name="pack_text",
    )(text_k, text_v, across_k, across_v, v_fresh, beside, diagonal)
    left = lax.ppermute(plus, "cols", [(i, (i + 1) % 4) for i in range(4)])
    right = lax.ppermute(minus, "cols", [((i + 1) % 4, i) for i in range(4)])
    upper = lax.ppermute(left, "cols", [(1, 2), (2, 3)])
    lower = lax.ppermute(right, "cols", [(1, 0), (2, 1)])
    pieces = [plus, left, right, upper, lower]
    pieces = pieces + [to_mate(p) for p in pieces]

    term = pl.pallas_call(
        term_kernel,
        out_shape=jax.ShapeDtypeStruct((tokens, width), jnp.float32),
        in_specs=[in_vmem] * 6,
        out_specs=in_vmem,
        compiler_params=params,
        name="term",
    )(v_fresh, beside, diagonal, left, right, conv_w)

    out = None
    first_head = 0
    for chunk, head_count in enumerate(CHUNK_HEADS):
        block = pl.BlockSpec(
            (pl.Element(tokens), pl.Element(head_count * HEAD_DIM)),
            lambda i, *_, at=first_head * HEAD_DIM: (0, at),
        )
        out = pl.pallas_call(
            functools.partial(attend_kernel, first_head),
            out_shape=jax.ShapeDtypeStruct((tokens, width), jnp.float32),
            grid_spec=pltpu.PrefetchScalarGridSpec(
                num_scalar_prefetch=3,
                grid=(1,),
                in_specs=[in_vmem] * 18 + [anywhere] * (out is not None),
                out_specs=block,
            ),
            input_output_aliases={21: 0} if out is not None else {},
            compiler_params=params,
            name=f"attend{chunk}",
        )(
            reads, pattern, text_blocks, flat(q_fresh), flat(k_fresh), flat(v_fresh), *pieces,
            mate_k, mate_v, far[chunk], to_mate(far[chunk]), term, *([out] if out is not None else []),
        )
        first_head += head_count
    return out.reshape(rows_here, cols_here, width)


def fits(mesh, reads, pattern, text_k):
    sizes = dict(mesh.shape)
    return (
        sizes["rows"] == 4
        and sizes["cols"] == 4
        and reads.shape[-1] == 2
        and pattern.shape[-1] == 2
        and pattern.shape[0] == 2 * sizes["groups"] * 4
        and text_k.shape[0] == sizes["groups"] * 4 * PER_BLOCK
    )


def solution(mesh):
    grid = P(("groups", "rows"), "cols", None)
    text = P(("groups", "rows", "cols"), None)
    in_specs = (grid, grid, grid, grid, grid, text, text, P(), grid, grid, grid)

    def program(*args):
        chosen = body if fits(mesh, args[8], args[9], args[5]) else general_body
        return jax.shard_map(
            chosen, mesh=mesh, in_specs=in_specs, out_specs=grid, check_vma=False
        )(*args)

    return program
```

```python
import functools
import math

import jax
import jax.numpy as jnp
from jax import lax
from jax.experimental import pallas as pl
from jax.experimental.pallas import tpu as pltpu
from jax.sharding import PartitionSpec as P

HEAD_DIM = 128
BLOCK_ROWS = 4
BLOCK_COLS = 32
PER_BLOCK = BLOCK_ROWS * BLOCK_COLS
SCORE_SCALE = 1.0 / math.sqrt(HEAD_DIM)
EXP2_SCALE = SCORE_SCALE * math.log2(math.e)
CHUNK_HEADS = (9, 3)
GROUP = 8
VMEM_LIMIT = 24 * 1024 * 1024


def extended(cells, sides, width):
    for axis, dim in sides:
        count = lax.axis_size(axis)
        ends = count - 1
        head = lax.slice_in_dim(cells, 0, width, axis=dim)
        tail = lax.slice_in_dim(cells, cells.shape[dim] - width, cells.shape[dim], axis=dim)
        cells = jnp.concatenate(
            [
                lax.ppermute(tail, axis, [(i, (i + 1) % count) for i in range(ends)]),
                cells,
                lax.ppermute(head, axis, [((i + 1) % count, i) for i in range(ends)]),
            ],
            axis=dim,
        )
    return cells


def position(v_fresh, conv_w):
    rows_here, cols_here, feature_width = v_fresh.shape
    rims = extended(v_fresh, (("rows", 0), ("cols", 1)), 1)
    position_term = jnp.zeros((rows_here, cols_here, feature_width), jnp.float32)
    for row_tap in range(3):
        for col_tap in range(3):
            position_term = position_term + conv_w[row_tap, col_tap] * rims[
                row_tap : row_tap + rows_here, col_tap : col_tap + cols_here
            ].astype(jnp.float32)
    return position_term


def split_heads(flat_rows):
    return flat_rows.reshape(flat_rows.shape[:-1] + (flat_rows.shape[-1] // HEAD_DIM, HEAD_DIM))


def attend(softmax_state, queries, key_blocks, value_blocks, allowed):
    old_peak, old_total, old_summed = softmax_state
    scores = (
        jnp.einsum(
            "bqhd,nkhd->bhqnk", queries, key_blocks, preferred_element_type=jnp.float32
        )
        * SCORE_SCALE
    )
    scores = jnp.where(allowed[:, None, None, :, None], scores, -1e30)
    new_peak = jnp.maximum(old_peak, jnp.max(scores, axis=(3, 4)))
    weights = jnp.exp(scores - new_peak[:, :, :, None, None]).astype(jnp.bfloat16)
    factor = jnp.exp(old_peak - new_peak)
    new_total = old_total * factor + jnp.sum(weights.astype(jnp.float32), axis=(3, 4))
    product = jnp.einsum(
        "bhqnk,nkhd->bqhd", weights, value_blocks, preferred_element_type=jnp.float32
    )
    new_summed = old_summed * jnp.transpose(factor, (0, 2, 1))[:, :, :, None] + product
    return (new_peak, new_total, new_summed)


def general_body(
    q_fresh, k_fresh, v_fresh, k_stale, v_stale, text_k, text_v, conv_w, reads, pattern, text_blocks
):
    rows_here, cols_here, feature_width = q_fresh.shape
    blocks_here = rows_here // BLOCK_ROWS
    head_count = feature_width // HEAD_DIM

    def as_blocks(grid_values):
        return split_heads(grid_values.reshape(blocks_here, PER_BLOCK, feature_width))

    queries = as_blocks(q_fresh)
    text_keys, text_values = (
        lax.all_gather(text_k, ("rows", "cols"), axis=0, tiled=True),
        lax.all_gather(text_v, ("rows", "cols"), axis=0, tiled=True),
    )
    text_count = text_keys.shape[0] // PER_BLOCK
    text_keys = split_heads(text_keys.reshape(text_count, PER_BLOCK, feature_width))
    text_values = split_heads(text_values.reshape(text_count, PER_BLOCK, feature_width))
    wanted = pattern[:, 0, :]
    fetch_rows = reads[0, 0, :]
    fetch_count = fetch_rows.shape[0]
    slot_count = blocks_here + fetch_count
    slot_mask = jnp.any(
        wanted[:, :, None] == jnp.arange(slot_count, dtype=jnp.int32)[None, None, :], axis=1
    )
    text_mask = jnp.any(
        text_blocks[:, 0, :, None] == jnp.arange(text_count, dtype=jnp.int32)[None, None, :], axis=1
    )
    softmax_state = (
        jnp.full((blocks_here, head_count, PER_BLOCK), -1e30, jnp.float32),
        jnp.zeros((blocks_here, head_count, PER_BLOCK), jnp.float32),
        jnp.zeros((blocks_here, PER_BLOCK, head_count, HEAD_DIM), jnp.float32),
    )
    softmax_state = attend(
        softmax_state,
        queries,
        jnp.concatenate([as_blocks(k_fresh), text_keys], axis=0),
        jnp.concatenate([as_blocks(v_fresh), text_values], axis=0),
        jnp.concatenate([slot_mask[:, :blocks_here], text_mask], axis=1),
    )
    chosen = jnp.where(
        wanted >= blocks_here, fetch_rows[jnp.clip(wanted - blocks_here, 0, fetch_count - 1)], -1
    )
    piece_keys = lax.all_gather(as_blocks(k_stale), "rows", axis=0, tiled=True)
    piece_values = lax.all_gather(as_blocks(v_stale), "rows", axis=0, tiled=True)
    block_rows = jnp.arange(piece_keys.shape[0], dtype=jnp.int32)
    piece_mask = jnp.any(chosen[:, :, None] == block_rows[None, None, :], axis=1)
    softmax_state = attend(softmax_state, queries, piece_keys, piece_values, piece_mask)
    _, final_total, final_summed = softmax_state
    mixed_rows = final_summed / jnp.transpose(final_total, (0, 2, 1))[:, :, :, None]
    attention = mixed_rows.reshape(rows_here, cols_here, feature_width)
    return attention + position(v_fresh, conv_w)


def head_scores(queries, keys):
    return lax.dot_general(
        queries, keys, (((1,), (1,)), ((), ())), preferred_element_type=jnp.float32
    )


def pack_kernel(k_hbm, v_hbm, cells, text_k, text_v, passed, diagonal, text, *refs):
    outs, sems = refs[:-1], refs[-1]
    tokens, shard = k_hbm.shape[0], text_k.shape[0]
    row = lax.axis_index("rows")
    end, edges = cells.shape[0] - 1, pl.ds(2 * tokens, cells.shape[1])
    copies = []
    for which, source in enumerate((text_k, text_v)):
        copies.append((source, text.at[pl.ds(which * shard, shard)]))
    first = 0
    for out in outs:
        part = pl.ds(first, out.shape[1])
        first += out.shape[1]
        for which, source in enumerate((k_hbm, v_hbm)):
            copies.append((source.at[:, part], out.at[pl.ds(which * tokens, tokens)]))
    for which, source in enumerate((k_hbm, v_hbm)):
        copies.append((source, passed.at[pl.ds(which * tokens, tokens)]))
    copies.append((cells.at[jnp.where(row % 2 == 0, end, 0)], passed.at[edges]))
    copies.append((cells.at[jnp.where(row < 2, end, 0)], diagonal))
    copies = [pltpu.make_async_copy(*pair, sems.at[i]) for i, pair in enumerate(copies)]
    for copy in copies:
        copy.start()
    for copy in copies:
        copy.wait()


def bundle_kernel(*refs):
    out = refs[-1]
    at = 0
    for ref in refs[:-1]:
        out[pl.ds(at, ref.shape[0]), :] = ref[...]
        at += ref.shape[0]


def choose_kernel(upper, lower, out):
    out[...] = jnp.where(lax.axis_index("cols") >= 2, upper[...], lower[...])


def edge_kernel(cells, passed, diagonal, last, first):
    rows_here, cols_here, width = cells.shape
    beside = passed[pl.ds(passed.shape[0] - cols_here, cols_here), :]
    above, below = above_below(beside, diagonal[...])
    rows = [above] + [cells[i] for i in range(rows_here)] + [below]
    rows = [row.astype(jnp.float32) for row in rows]
    spare = jnp.zeros((16 - len(rows), width), jnp.float32)
    for target, at in ((last, cols_here - 1), (first, 0)):
        edge = jnp.concatenate([row[at : at + 1] for row in rows] + [spare], axis=0)
        target[...] = edge.astype(target.dtype)


def above_below(beside, diagonal):
    first_core = lax.axis_index("rows") % 2 == 0
    return (
        jnp.where(first_core, diagonal, beside),
        jnp.where(first_core, beside, diagonal),
    )


def term_kernel(cells, passed, diagonal, left, right, weights, out):
    rows_here, cols_here, width = cells.shape
    col = lax.axis_index("cols")
    place = lax.broadcasted_iota(jnp.int32, (cols_here, HEAD_DIM), 0)
    for lane in range(width // HEAD_DIM):
        part = pl.ds(lane * HEAD_DIM, HEAD_DIM)
        above, below = above_below(
            passed[pl.ds(passed.shape[0] - cols_here, cols_here), part], diagonal[:, part]
        )
        lefts = left[:, part].astype(jnp.float32)
        rights = right[:, part].astype(jnp.float32)
        lefts = jnp.where(col > 0, lefts, 0.0)
        rights = jnp.where(col < 3, rights, 0.0)
        taps = []
        for row in range(rows_here + 2):
            if row == 0:
                centre = above
            elif row == rows_here + 1:
                centre = below
            else:
                centre = cells[row - 1, :, part]
            centre = centre.astype(jnp.float32)
            before = jnp.where(place == 0, lefts[row : row + 1], pltpu.roll(centre, 1, 0))
            after = jnp.where(
                place == cols_here - 1, rights[row : row + 1], pltpu.roll(centre, cols_here - 1, 0)
            )
            taps.append((before, centre, after))
        for row in range(rows_here):
            total = None
            for row_tap in range(3):
                for col_tap in range(3):
                    piece = weights[row_tap, col_tap : col_tap + 1, part] * taps[row + row_tap][col_tap]
                    total = piece if total is None else total + piece
            out[pl.ds(row * cols_here, cols_here), part] = total


def attend_kernel(first_head, reads_ref, pattern_ref, text_ref, q, k, v, *refs):
    near, last, near_mate, last_mate, passed, across_kv, both_kv, term = refs[:8]
    out = refs[-1]
    row, col = lax.axis_index("rows"), lax.axis_index("cols")
    across, core = row // 2, row % 2
    shard = last.shape[0] // 4
    half = across_kv.shape[0] // 2
    head_count = across_kv.shape[1] // HEAD_DIM

    def lanes(head):
        return pl.ds((first_head + head) * HEAD_DIM, HEAD_DIM)

    def text_part(chosen, head, which):
        from_own = chosen % 2 == core
        first = jnp.where(chosen // 2 == across, 0, 2 * shard) + which * shard
        part = lanes(head)

        def one(own, other, at):
            rows = pl.ds(pl.multiple_of(first + at, shard), shard)
            return jnp.where(from_own, own[rows, part], other[rows, part])

        return [one(near, near_mate, 4 * shard * i) for i in range(3)] + [one(last, last_mate, 0)]

    def far_part(block, head, which):
        slot = pattern_ref[block, 0, 0] + pattern_ref[block, 0, 1] - block - 2
        wanted = reads_ref[0, 0, slot]
        owner = wanted // 2
        first = (wanted % 2) * PER_BLOCK
        packed = pl.ds(pl.multiple_of(first + which * half, PER_BLOCK), PER_BLOCK)
        mate = passed[packed, lanes(head)]
        here = pl.ds(head * HEAD_DIM, HEAD_DIM)
        straight, crossed = across_kv[packed, here], both_kv[packed, here]
        arrived = jnp.where(owner % 2 == core, straight, crossed)
        return jnp.where(owner // 2 == across, mate, arrived)

    def gathered(block, head, which):
        own = (k, v)[which][pl.ds(block * PER_BLOCK, PER_BLOCK), lanes(head)]
        parts = [own]
        for turn in range(2):
            parts += text_part(text_ref[block, 0, turn], head, which)
        return jnp.concatenate(parts + [far_part(block, head, which)], axis=0)

    jobs = [(block, head) for head in range(head_count) for block in range(2)]
    size = -(-len(jobs) // -(-len(jobs) // GROUP))
    for at in range(0, len(jobs), size):
        group = jobs[at : at + size]
        scores = [
            head_scores(
                q[pl.ds(block * PER_BLOCK, PER_BLOCK), lanes(head)], gathered(block, head, 0)
            )
            for block, head in group
        ]
        peaks = [jnp.max(s, axis=1, keepdims=True) * EXP2_SCALE for s in scores]
        weights = [
            jnp.exp2(s * EXP2_SCALE - peak).astype(jnp.bfloat16) for s, peak in zip(scores, peaks)
        ]
        totals = [jnp.sum(w.astype(jnp.float32), axis=1, keepdims=True) for w in weights]
        products = [
            jnp.dot(w, gathered(block, head, 1), preferred_element_type=jnp.float32)
            for w, (block, head) in zip(weights, group)
        ]
        for product, total, (block, head) in zip(products, totals, group):
            rows = pl.ds(block * PER_BLOCK, PER_BLOCK)
            out[rows, pl.ds(head * HEAD_DIM, HEAD_DIM)] = product / total + term[rows, lanes(head)]


def body(
    q_fresh, k_fresh, v_fresh, k_stale, v_stale, text_k, text_v, conv_w, reads, pattern, text_blocks
):
    rows_here, cols_here, width = q_fresh.shape
    tokens = rows_here * cols_here
    shard = text_k.shape[0]
    swap = [(r, (r + 2) % 4) for r in range(4)]
    mates = [(r, r ^ 1) for r in range(4)]
    in_vmem = pl.BlockSpec(memory_space=pltpu.VMEM)
    in_hbm = pl.BlockSpec(memory_space=pltpu.HBM)
    params = pltpu.CompilerParams(vmem_limit_bytes=VMEM_LIMIT)
    cost = pl.CostEstimate(flops=1 << 20, transcendentals=0, bytes_accessed=1 << 16)

    def after(value, *others):
        return lax.optimization_barrier((value, *others))[0]

    def flat(grid_values):
        return grid_values.reshape(tokens, width)

    def to_mate(values):
        return lax.ppermute(values, "rows", mates)

    def rows_of(*counts):
        shapes = tuple(jax.ShapeDtypeStruct((n, width), jnp.bfloat16) for n in counts)
        return shapes if len(shapes) > 1 else shapes[0]

    def local(kernel, name, shapes, *args, specs=None, scratch=()):
        many = isinstance(shapes, tuple)
        return pl.pallas_call(
            kernel,
            out_shape=shapes,
            in_specs=specs or [in_vmem] * len(args),
            out_specs=(in_vmem,) * len(shapes) if many else in_vmem,
            scratch_shapes=scratch,
            compiler_params=params,
            cost_estimate=cost,
            name=name,
        )(*args)

    chunks = tuple(
        jax.ShapeDtypeStruct((2 * tokens, n * HEAD_DIM), jnp.bfloat16) for n in CHUNK_HEADS
    )
    in_place = [
        pltpu.with_memory_space_constraint(value, pltpu.HBM)
        for value in (flat(k_stale), flat(v_stale), v_fresh, text_k, text_v)
    ]
    passed, diagonal, text, *packed = local(
        pack_kernel,
        "pack",
        rows_of(2 * tokens + cols_here, cols_here, 2 * shard) + chunks,
        *in_place,
        specs=[in_hbm] * 5,
        scratch=[pltpu.SemaphoreType.DMA((6 + 2 * len(CHUNK_HEADS),))],
    )
    across = lax.ppermute(text, "rows", swap)
    diagonal = lax.ppermute(diagonal, "rows", [(1, 2), (2, 1)])
    far = [lax.ppermute(after(packed[0], across, diagonal), "rows", swap)]
    passed = to_mate(passed)

    text = local(bundle_kernel, "join", rows_of(4 * shard), text, across)
    left = lax.ppermute(text, "cols", [(i, (i + 1) % 4) for i in range(4)])
    right = lax.ppermute(text, "cols", [((i + 1) % 4, i) for i in range(4)])
    far.append(lax.ppermute(after(packed[1], passed), "rows", swap))
    upper = lax.ppermute(left, "cols", [(1, 2), (2, 3)])
    lower = lax.ppermute(right, "cols", [(1, 0), (2, 1)])

    last, first = local(edge_kernel, "edge", rows_of(16, 16), v_fresh, passed, diagonal)
    last = lax.ppermute(last, "cols", [(i, i + 1) for i in range(3)])
    first = lax.ppermute(first, "cols", [(i + 1, i) for i in range(3)])
    near = local(bundle_kernel, "bundle", rows_of(12 * shard), text, left, right)
    near_mate = to_mate(near)
    term = local(
        term_kernel,
        "term",
        jax.ShapeDtypeStruct((tokens, width), jnp.float32),
        v_fresh, passed, diagonal, after(last, near), first, conv_w,
    )
    rest = local(choose_kernel, "choose", rows_of(4 * shard), upper, lower)
    rest_mate = to_mate(rest)
    far[0] = after(far[0], term, rest)

    out = None
    first_head = 0
    for chunk, head_count in enumerate(CHUNK_HEADS):
        if out is not None:
            far[chunk] = after(far[chunk], out)
        far_mate = to_mate(far[chunk])
        block = pl.BlockSpec(
            (pl.Element(tokens), pl.Element(head_count * HEAD_DIM)),
            lambda i, *_, at=first_head * HEAD_DIM: (0, at),
        )
        out = pl.pallas_call(
            functools.partial(attend_kernel, first_head),
            out_shape=jax.ShapeDtypeStruct((tokens, width), jnp.float32),
            grid_spec=pltpu.PrefetchScalarGridSpec(
                num_scalar_prefetch=3,
                grid=(1,),
                in_specs=[in_vmem] * 11 + [in_hbm] * (out is not None),
                out_specs=block,
            ),
            input_output_aliases={14: 0} if out is not None else {},
            compiler_params=params,
            cost_estimate=cost,
            name=f"attend{chunk}",
        )(
            reads, pattern, text_blocks, flat(q_fresh), flat(k_fresh), flat(v_fresh),
            near, rest, near_mate, rest_mate, passed, far[chunk], far_mate, term,
            *([out] if out is not None else []),
        )
        first_head += head_count
    return out.reshape(rows_here, cols_here, width)


def fits(mesh, reads, pattern, text_k):
    sizes = dict(mesh.shape)
    return (
        sizes["rows"] == 4
        and sizes["cols"] == 4
        and reads.shape[-1] == 2
        and pattern.shape[-1] == 2
        and pattern.shape[0] == 2 * sizes["groups"] * 4
        and text_k.shape[0] == sizes["groups"] * 4 * PER_BLOCK
    )


def solution(mesh):
    grid = P(("groups", "rows"), "cols", None)
    text = P(("groups", "rows", "cols"), None)
    in_specs = (grid, grid, grid, grid, grid, text, text, P(), grid, grid, grid)

    def program(*args):
        chosen = body if fits(mesh, args[8], args[9], args[5]) else general_body
        return jax.shard_map(
            chosen, mesh=mesh, in_specs=in_specs, out_specs=grid, check_vma=False
        )(*args)

    return program
```

```python
import functools
import math

import jax
import jax.numpy as jnp
from jax import lax
from jax.experimental import pallas as pl
from jax.experimental.pallas import tpu as pltpu
from jax.sharding import PartitionSpec as P

HEAD_DIM = 128
BLOCK_ROWS = 4
BLOCK_COLS = 32
PER_BLOCK = BLOCK_ROWS * BLOCK_COLS
SCORE_SCALE = 1.0 / math.sqrt(HEAD_DIM)
EXP2_SCALE = SCORE_SCALE * math.log2(math.e)
CHUNK_HEADS = (9, 3)
CHUNK_SPARE = (0, 16)
GROUP = 8
VMEM_LIMIT = 24 * 1024 * 1024


def extended(cells, sides, width):
    for axis, dim in sides:
        count = lax.axis_size(axis)
        ends = count - 1
        head = lax.slice_in_dim(cells, 0, width, axis=dim)
        tail = lax.slice_in_dim(cells, cells.shape[dim] - width, cells.shape[dim], axis=dim)
        cells = jnp.concatenate(
            [
                lax.ppermute(tail, axis, [(i, (i + 1) % count) for i in range(ends)]),
                cells,
                lax.ppermute(head, axis, [((i + 1) % count, i) for i in range(ends)]),
            ],
            axis=dim,
        )
    return cells


def position(v_fresh, conv_w):
    rows_here, cols_here, feature_width = v_fresh.shape
    rims = extended(v_fresh, (("rows", 0), ("cols", 1)), 1)
    position_term = jnp.zeros((rows_here, cols_here, feature_width), jnp.float32)
    for row_tap in range(3):
        for col_tap in range(3):
            position_term = position_term + conv_w[row_tap, col_tap] * rims[
                row_tap : row_tap + rows_here, col_tap : col_tap + cols_here
            ].astype(jnp.float32)
    return position_term


def split_heads(flat_rows):
    return flat_rows.reshape(flat_rows.shape[:-1] + (flat_rows.shape[-1] // HEAD_DIM, HEAD_DIM))


def attend(softmax_state, queries, key_blocks, value_blocks, allowed):
    old_peak, old_total, old_summed = softmax_state
    scores = (
        jnp.einsum(
            "bqhd,nkhd->bhqnk", queries, key_blocks, preferred_element_type=jnp.float32
        )
        * SCORE_SCALE
    )
    scores = jnp.where(allowed[:, None, None, :, None], scores, -1e30)
    new_peak = jnp.maximum(old_peak, jnp.max(scores, axis=(3, 4)))
    weights = jnp.exp(scores - new_peak[:, :, :, None, None]).astype(jnp.bfloat16)
    factor = jnp.exp(old_peak - new_peak)
    new_total = old_total * factor + jnp.sum(weights.astype(jnp.float32), axis=(3, 4))
    product = jnp.einsum(
        "bhqnk,nkhd->bqhd", weights, value_blocks, preferred_element_type=jnp.float32
    )
    new_summed = old_summed * jnp.transpose(factor, (0, 2, 1))[:, :, :, None] + product
    return (new_peak, new_total, new_summed)


def general_body(
    q_fresh, k_fresh, v_fresh, k_stale, v_stale, text_k, text_v, conv_w, reads, pattern, text_blocks
):
    rows_here, cols_here, feature_width = q_fresh.shape
    blocks_here = rows_here // BLOCK_ROWS
    head_count = feature_width // HEAD_DIM

    def as_blocks(grid_values):
        return split_heads(grid_values.reshape(blocks_here, PER_BLOCK, feature_width))

    queries = as_blocks(q_fresh)
    text_keys, text_values = (
        lax.all_gather(text_k, ("rows", "cols"), axis=0, tiled=True),
        lax.all_gather(text_v, ("rows", "cols"), axis=0, tiled=True),
    )
    text_count = text_keys.shape[0] // PER_BLOCK
    text_keys = split_heads(text_keys.reshape(text_count, PER_BLOCK, feature_width))
    text_values = split_heads(text_values.reshape(text_count, PER_BLOCK, feature_width))
    wanted = pattern[:, 0, :]
    fetch_rows = reads[0, 0, :]
    fetch_count = fetch_rows.shape[0]
    slot_count = blocks_here + fetch_count
    slot_mask = jnp.any(
        wanted[:, :, None] == jnp.arange(slot_count, dtype=jnp.int32)[None, None, :], axis=1
    )
    text_mask = jnp.any(
        text_blocks[:, 0, :, None] == jnp.arange(text_count, dtype=jnp.int32)[None, None, :], axis=1
    )
    softmax_state = (
        jnp.full((blocks_here, head_count, PER_BLOCK), -1e30, jnp.float32),
        jnp.zeros((blocks_here, head_count, PER_BLOCK), jnp.float32),
        jnp.zeros((blocks_here, PER_BLOCK, head_count, HEAD_DIM), jnp.float32),
    )
    softmax_state = attend(
        softmax_state,
        queries,
        jnp.concatenate([as_blocks(k_fresh), text_keys], axis=0),
        jnp.concatenate([as_blocks(v_fresh), text_values], axis=0),
        jnp.concatenate([slot_mask[:, :blocks_here], text_mask], axis=1),
    )
    chosen = jnp.where(
        wanted >= blocks_here, fetch_rows[jnp.clip(wanted - blocks_here, 0, fetch_count - 1)], -1
    )
    piece_keys = lax.all_gather(as_blocks(k_stale), "rows", axis=0, tiled=True)
    piece_values = lax.all_gather(as_blocks(v_stale), "rows", axis=0, tiled=True)
    block_rows = jnp.arange(piece_keys.shape[0], dtype=jnp.int32)
    piece_mask = jnp.any(chosen[:, :, None] == block_rows[None, None, :], axis=1)
    softmax_state = attend(softmax_state, queries, piece_keys, piece_values, piece_mask)
    _, final_total, final_summed = softmax_state
    mixed_rows = final_summed / jnp.transpose(final_total, (0, 2, 1))[:, :, :, None]
    attention = mixed_rows.reshape(rows_here, cols_here, feature_width)
    return attention + position(v_fresh, conv_w)


def head_scores(queries, keys):
    return lax.dot_general(
        queries, keys, (((1,), (1,)), ((), ())), preferred_element_type=jnp.float32
    )


def run_copies(copies, sems):
    copies = [pltpu.make_async_copy(*pair, sems.at[i]) for i, pair in enumerate(copies)]
    for copy in copies:
        copy.start()
    for copy in copies:
        copy.wait()


def pack_kernel(cells, text_k, text_v, beside, diagonal, text, sems):
    shard = text_k.shape[0]
    row = lax.axis_index("rows")
    end = cells.shape[0] - 1
    copies = []
    for which, source in enumerate((text_k, text_v)):
        copies.append((source, text.at[pl.ds(which * shard, shard)]))
    copies.append((cells.at[jnp.where(row % 2 == 0, end, 0)], beside))
    copies.append((cells.at[jnp.where(row < 2, end, 0)], diagonal))
    run_copies(copies, sems)


def send_kernel(wanted, k_hbm, v_hbm, passed_k, passed_v, *refs):
    outs, sems = refs[:-1], refs[-1]
    row = lax.axis_index("rows")

    def block_of(owner):
        found = 0
        for turn in range(2):
            entry = wanted[0, 0, turn]
            found = jnp.where(entry // 2 == owner, entry % 2, found)
        return pl.multiple_of(found * PER_BLOCK, PER_BLOCK)

    own, other = block_of(row), block_of(row + 1 - 2 * (row % 2))
    copies = []
    first = 0
    for out in outs:
        part = pl.ds(first, out.shape[1])
        first += out.shape[1]
        for which, (source, passed) in enumerate(((k_hbm, passed_k), (v_hbm, passed_v))):
            at = 2 * PER_BLOCK * which
            copies.append(
                (source.at[pl.ds(own, PER_BLOCK), part], out.at[pl.ds(at, PER_BLOCK)])
            )
            copies.append(
                (
                    passed.at[pl.ds(other, PER_BLOCK), part],
                    out.at[pl.ds(at + PER_BLOCK, PER_BLOCK)],
                )
            )
    for out, spare in zip(outs, CHUNK_SPARE):
        if spare:
            rows = pl.ds(out.shape[0] - spare, spare)
            out[rows, :] = jnp.zeros((spare, out.shape[1]), out.dtype)
    run_copies(copies, sems)


def bundle_kernel(*refs):
    out = refs[-1]
    at = 0
    for ref in refs[:-1]:
        out[pl.ds(at, ref.shape[0]), :] = ref[...]
        at += ref.shape[0]


def choose_kernel(upper, lower, out):
    out[...] = jnp.where(lax.axis_index("cols") >= 2, upper[...], lower[...])


def edge_kernel(cells, beside, diagonal, last, first):
    rows_here, cols_here, width = cells.shape
    above, below = above_below(beside[...], diagonal[...])
    rows = [above] + [cells[i] for i in range(rows_here)] + [below]
    rows = [row.astype(jnp.float32) for row in rows]
    spare = jnp.zeros((16 - len(rows), width), jnp.float32)
    for target, at in ((last, cols_here - 1), (first, 0)):
        edge = jnp.concatenate([row[at : at + 1] for row in rows] + [spare], axis=0)
        target[...] = edge.astype(target.dtype)


def above_below(beside, diagonal):
    first_core = lax.axis_index("rows") % 2 == 0
    return (
        jnp.where(first_core, diagonal, beside),
        jnp.where(first_core, beside, diagonal),
    )


def term_kernel(cells, beside, diagonal, left, right, weights, out):
    rows_here, cols_here, width = cells.shape
    col = lax.axis_index("cols")
    place = lax.broadcasted_iota(jnp.int32, (cols_here, HEAD_DIM), 0)
    for lane in range(width // HEAD_DIM):
        part = pl.ds(lane * HEAD_DIM, HEAD_DIM)
        above, below = above_below(beside[:, part], diagonal[:, part])
        lefts = left[:, part].astype(jnp.float32)
        rights = right[:, part].astype(jnp.float32)
        lefts = jnp.where(col > 0, lefts, 0.0)
        rights = jnp.where(col < 3, rights, 0.0)
        taps = []
        for row in range(rows_here + 2):
            if row == 0:
                centre = above
            elif row == rows_here + 1:
                centre = below
            else:
                centre = cells[row - 1, :, part]
            centre = centre.astype(jnp.float32)
            before = jnp.where(place == 0, lefts[row : row + 1], pltpu.roll(centre, 1, 0))
            after = jnp.where(
                place == cols_here - 1, rights[row : row + 1], pltpu.roll(centre, cols_here - 1, 0)
            )
            taps.append((before, centre, after))
        for row in range(rows_here):
            total = None
            for row_tap in range(3):
                for col_tap in range(3):
                    piece = weights[row_tap, col_tap : col_tap + 1, part] * taps[row + row_tap][col_tap]
                    total = piece if total is None else total + piece
            out[pl.ds(row * cols_here, cols_here), part] = total


def attend_kernel(first_head, reads_ref, pattern_ref, text_ref, q, k, v, *refs):
    near, last, near_mate, last_mate, passed_k, passed_v, arrived, term = refs[:8]
    out = refs[-1]
    row, col = lax.axis_index("rows"), lax.axis_index("cols")
    across, core = row // 2, row % 2
    shard = last.shape[0] // 4
    half = 2 * PER_BLOCK
    head_count = arrived.shape[1] // HEAD_DIM

    def lanes(head):
        return pl.ds((first_head + head) * HEAD_DIM, HEAD_DIM)

    def text_part(chosen, head, which):
        from_own = chosen % 2 == core
        first = jnp.where(chosen // 2 == across, 0, 2 * shard) + which * shard
        part = lanes(head)

        def one(own, other, at):
            rows = pl.ds(pl.multiple_of(first + at, shard), shard)
            return jnp.where(from_own, own[rows, part], other[rows, part])

        return [one(near, near_mate, 4 * shard * i) for i in range(3)] + [one(last, last_mate, 0)]

    def far_part(block, head, which):
        slot = pattern_ref[block, 0, 0] + pattern_ref[block, 0, 1] - block - 2
        wanted = reads_ref[0, 0, slot]
        owner = wanted // 2
        mate_at = (wanted % 2) * PER_BLOCK
        far_at = jnp.where(owner % 2 == core, 0, PER_BLOCK) + which * half
        passed = (passed_k, passed_v)[which]
        mate = passed[pl.ds(pl.multiple_of(mate_at, PER_BLOCK), PER_BLOCK), lanes(head)]
        here = pl.ds(head * HEAD_DIM, HEAD_DIM)
        far = arrived[pl.ds(pl.multiple_of(far_at, PER_BLOCK), PER_BLOCK), here]
        return jnp.where(owner // 2 == across, mate, far)

    def gathered(block, head, which):
        own = (k, v)[which][pl.ds(block * PER_BLOCK, PER_BLOCK), lanes(head)]
        parts = [own]
        for turn in range(2):
            parts += text_part(text_ref[block, 0, turn], head, which)
        return jnp.concatenate(parts + [far_part(block, head, which)], axis=0)

    jobs = [(block, head) for head in range(head_count) for block in range(2)]
    size = -(-len(jobs) // -(-len(jobs) // GROUP))
    for at in range(0, len(jobs), size):
        group = jobs[at : at + size]
        scores = [
            head_scores(
                q[pl.ds(block * PER_BLOCK, PER_BLOCK), lanes(head)], gathered(block, head, 0)
            )
            for block, head in group
        ]
        peaks = [jnp.max(s, axis=1, keepdims=True) * EXP2_SCALE for s in scores]
        weights = [
            jnp.exp2(s * EXP2_SCALE - peak).astype(jnp.bfloat16) for s, peak in zip(scores, peaks)
        ]
        totals = [jnp.sum(w.astype(jnp.float32), axis=1, keepdims=True) for w in weights]
        products = [
            jnp.dot(w, gathered(block, head, 1), preferred_element_type=jnp.float32)
            for w, (block, head) in zip(weights, group)
        ]
        for product, total, (block, head) in zip(products, totals, group):
            rows = pl.ds(block * PER_BLOCK, PER_BLOCK)
            out[rows, pl.ds(head * HEAD_DIM, HEAD_DIM)] = product / total + term[rows, lanes(head)]


def body(
    q_fresh, k_fresh, v_fresh, k_stale, v_stale, text_k, text_v, conv_w, reads, pattern, text_blocks
):
    rows_here, cols_here, width = q_fresh.shape
    tokens = rows_here * cols_here
    shard = text_k.shape[0]
    swap = [(r, (r + 2) % 4) for r in range(4)]
    mates = [(r, r ^ 1) for r in range(4)]
    in_vmem = pl.BlockSpec(memory_space=pltpu.VMEM)
    in_hbm = pl.BlockSpec(memory_space=pltpu.HBM)
    params = pltpu.CompilerParams(vmem_limit_bytes=VMEM_LIMIT)
    cost = pl.CostEstimate(flops=1 << 20, transcendentals=0, bytes_accessed=1 << 16)

    def after(value, *others):
        return lax.optimization_barrier((value, *others))[0]

    def flat(grid_values):
        return grid_values.reshape(tokens, width)

    def to_mate(values):
        return lax.ppermute(values, "rows", mates)

    def rows_of(*counts):
        shapes = tuple(jax.ShapeDtypeStruct((n, width), jnp.bfloat16) for n in counts)
        return shapes if len(shapes) > 1 else shapes[0]

    def local(kernel, name, shapes, *args, specs=None, scratch=()):
        many = isinstance(shapes, tuple)
        return pl.pallas_call(
            kernel,
            out_shape=shapes,
            in_specs=specs or [in_vmem] * len(args),
            out_specs=(in_vmem,) * len(shapes) if many else in_vmem,
            scratch_shapes=scratch,
            compiler_params=params,
            cost_estimate=cost,
            name=name,
        )(*args)

    chunks = tuple(
        jax.ShapeDtypeStruct((2 * tokens + spare, n * HEAD_DIM), jnp.bfloat16)
        for n, spare in zip(CHUNK_HEADS, CHUNK_SPARE)
    )
    in_place = [
        pltpu.with_memory_space_constraint(value, pltpu.HBM)
        for value in (flat(k_stale), flat(v_stale), v_fresh, text_k, text_v)
    ]
    wanted = lax.ppermute(reads, "rows", swap)
    beside, diagonal, text = local(
        pack_kernel,
        "pack",
        rows_of(cols_here, cols_here, 2 * shard),
        *in_place[2:],
        specs=[in_hbm] * 3,
        scratch=[pltpu.SemaphoreType.DMA((4,))],
    )
    across = lax.ppermute(text, "rows", swap)
    diagonal = lax.ppermute(diagonal, "rows", [(1, 2), (2, 1)])
    beside = to_mate(beside)
    passed = [to_mate(value) for value in in_place[:2]]
    packed = local(
        send_kernel,
        "send",
        chunks,
        wanted,
        *in_place[:2],
        *passed,
        specs=[pl.BlockSpec(memory_space=pltpu.SMEM)] + [in_hbm] * 2 + [in_vmem] * 2,
        scratch=[pltpu.SemaphoreType.DMA((4 * len(CHUNK_HEADS),))],
    )
    far = [lax.ppermute(chunk, "rows", swap) for chunk in packed]

    text = local(
        bundle_kernel, "join", rows_of(4 * shard), after(text, diagonal, packed[0], beside), across
    )
    left = lax.ppermute(text, "cols", [(i, (i + 1) % 4) for i in range(4)])
    right = lax.ppermute(text, "cols", [((i + 1) % 4, i) for i in range(4)])
    last, first = local(edge_kernel, "edge", rows_of(16, 16), v_fresh, beside, diagonal)
    last = lax.ppermute(last, "cols", [(i, i + 1) for i in range(3)])
    first = lax.ppermute(first, "cols", [(i + 1, i) for i in range(3)])
    upper = lax.ppermute(left, "cols", [(1, 2), (2, 3)])
    lower = lax.ppermute(right, "cols", [(1, 0), (2, 1)])

    near = local(bundle_kernel, "bundle", rows_of(12 * shard), text, left, right)
    near_mate = to_mate(near)
    term = local(
        term_kernel,
        "term",
        jax.ShapeDtypeStruct((tokens, width), jnp.float32),
        v_fresh, beside, diagonal, last, first, conv_w,
    )
    rest = local(choose_kernel, "choose", rows_of(4 * shard), after(upper, far[0], term), lower)
    rest_mate = to_mate(rest)
    out = None
    first_head = 0
    for chunk, head_count in enumerate(CHUNK_HEADS):
        if out is not None:
            far[chunk] = after(far[chunk], out)
        block = pl.BlockSpec(
            (pl.Element(tokens), pl.Element(head_count * HEAD_DIM)),
            lambda i, *_, at=first_head * HEAD_DIM: (0, at),
        )
        out = pl.pallas_call(
            functools.partial(attend_kernel, first_head),
            out_shape=jax.ShapeDtypeStruct((tokens, width), jnp.float32),
            grid_spec=pltpu.PrefetchScalarGridSpec(
                num_scalar_prefetch=3,
                grid=(1,),
                in_specs=[in_vmem] * 11 + [in_hbm] * (out is not None),
                out_specs=block,
            ),
            input_output_aliases={14: 0} if out is not None else {},
            compiler_params=params,
            cost_estimate=cost,
            name=f"attend{chunk}",
        )(
            reads, pattern, text_blocks, flat(q_fresh), flat(k_fresh), flat(v_fresh),
            near, rest, near_mate, rest_mate, *passed, far[chunk], term,
            *([out] if out is not None else []),
        )
        first_head += head_count
    return out.reshape(rows_here, cols_here, width)


def fits(mesh, reads, pattern, text_k):
    sizes = dict(mesh.shape)
    return (
        sizes["rows"] == 4
        and sizes["cols"] == 4
        and reads.shape[-1] == 2
        and pattern.shape[-1] == 2
        and pattern.shape[0] == 2 * sizes["groups"] * 4
        and text_k.shape[0] == sizes["groups"] * 4 * PER_BLOCK
    )


def solution(mesh):
    grid = P(("groups", "rows"), "cols", None)
    text = P(("groups", "rows", "cols"), None)
    in_specs = (grid, grid, grid, grid, grid, text, text, P(), grid, grid, grid)

    def program(*args):
        chosen = body if fits(mesh, args[8], args[9], args[5]) else general_body
        return jax.shard_map(
            chosen, mesh=mesh, in_specs=in_specs, out_specs=grid, check_vma=False
        )(*args)

    return program
```

```python
import functools
import math

import jax
import jax.numpy as jnp
from jax import lax
from jax.experimental import pallas as pl
from jax.experimental.pallas import tpu as pltpu
from jax.sharding import PartitionSpec as P

HEAD_DIM = 128
BLOCK_ROWS = 4
BLOCK_COLS = 32
PER_BLOCK = BLOCK_ROWS * BLOCK_COLS
SCORE_SCALE = 1.0 / math.sqrt(HEAD_DIM)
EXP2_SCALE = SCORE_SCALE * math.log2(math.e)
CHUNK_HEADS = (9, 3)
CHUNK_SPARE = (0, 0)
GROUP = 8
VMEM_LIMIT = 24 * 1024 * 1024


def extended(cells, sides, width):
    for axis, dim in sides:
        count = lax.axis_size(axis)
        ends = count - 1
        head = lax.slice_in_dim(cells, 0, width, axis=dim)
        tail = lax.slice_in_dim(cells, cells.shape[dim] - width, cells.shape[dim], axis=dim)
        cells = jnp.concatenate(
            [
                lax.ppermute(tail, axis, [(i, (i + 1) % count) for i in range(ends)]),
                cells,
                lax.ppermute(head, axis, [((i + 1) % count, i) for i in range(ends)]),
            ],
            axis=dim,
        )
    return cells


def position(v_fresh, conv_w):
    rows_here, cols_here, feature_width = v_fresh.shape
    rims = extended(v_fresh, (("rows", 0), ("cols", 1)), 1)
    position_term = jnp.zeros((rows_here, cols_here, feature_width), jnp.float32)
    for row_tap in range(3):
        for col_tap in range(3):
            position_term = position_term + conv_w[row_tap, col_tap] * rims[
                row_tap : row_tap + rows_here, col_tap : col_tap + cols_here
            ].astype(jnp.float32)
    return position_term


def split_heads(flat_rows):
    return flat_rows.reshape(flat_rows.shape[:-1] + (flat_rows.shape[-1] // HEAD_DIM, HEAD_DIM))


def attend(softmax_state, queries, key_blocks, value_blocks, allowed):
    old_peak, old_total, old_summed = softmax_state
    scores = (
        jnp.einsum(
            "bqhd,nkhd->bhqnk", queries, key_blocks, preferred_element_type=jnp.float32
        )
        * SCORE_SCALE
    )
    scores = jnp.where(allowed[:, None, None, :, None], scores, -1e30)
    new_peak = jnp.maximum(old_peak, jnp.max(scores, axis=(3, 4)))
    weights = jnp.exp(scores - new_peak[:, :, :, None, None]).astype(jnp.bfloat16)
    factor = jnp.exp(old_peak - new_peak)
    new_total = old_total * factor + jnp.sum(weights.astype(jnp.float32), axis=(3, 4))
    product = jnp.einsum(
        "bhqnk,nkhd->bqhd", weights, value_blocks, preferred_element_type=jnp.float32
    )
    new_summed = old_summed * jnp.transpose(factor, (0, 2, 1))[:, :, :, None] + product
    return (new_peak, new_total, new_summed)


def general_body(
    q_fresh, k_fresh, v_fresh, k_stale, v_stale, text_k, text_v, conv_w, reads, pattern, text_blocks
):
    rows_here, cols_here, feature_width = q_fresh.shape
    blocks_here = rows_here // BLOCK_ROWS
    head_count = feature_width // HEAD_DIM

    def as_blocks(grid_values):
        return split_heads(grid_values.reshape(blocks_here, PER_BLOCK, feature_width))

    queries = as_blocks(q_fresh)
    text_keys, text_values = (
        lax.all_gather(text_k, ("rows", "cols"), axis=0, tiled=True),
        lax.all_gather(text_v, ("rows", "cols"), axis=0, tiled=True),
    )
    text_count = text_keys.shape[0] // PER_BLOCK
    text_keys = split_heads(text_keys.reshape(text_count, PER_BLOCK, feature_width))
    text_values = split_heads(text_values.reshape(text_count, PER_BLOCK, feature_width))
    wanted = pattern[:, 0, :]
    fetch_rows = reads[0, 0, :]
    fetch_count = fetch_rows.shape[0]
    slot_count = blocks_here + fetch_count
    slot_mask = jnp.any(
        wanted[:, :, None] == jnp.arange(slot_count, dtype=jnp.int32)[None, None, :], axis=1
    )
    text_mask = jnp.any(
        text_blocks[:, 0, :, None] == jnp.arange(text_count, dtype=jnp.int32)[None, None, :], axis=1
    )
    softmax_state = (
        jnp.full((blocks_here, head_count, PER_BLOCK), -1e30, jnp.float32),
        jnp.zeros((blocks_here, head_count, PER_BLOCK), jnp.float32),
        jnp.zeros((blocks_here, PER_BLOCK, head_count, HEAD_DIM), jnp.float32),
    )
    softmax_state = attend(
        softmax_state,
        queries,
        jnp.concatenate([as_blocks(k_fresh), text_keys], axis=0),
        jnp.concatenate([as_blocks(v_fresh), text_values], axis=0),
        jnp.concatenate([slot_mask[:, :blocks_here], text_mask], axis=1),
    )
    chosen = jnp.where(
        wanted >= blocks_here, fetch_rows[jnp.clip(wanted - blocks_here, 0, fetch_count - 1)], -1
    )
    piece_keys = lax.all_gather(as_blocks(k_stale), "rows", axis=0, tiled=True)
    piece_values = lax.all_gather(as_blocks(v_stale), "rows", axis=0, tiled=True)
    block_rows = jnp.arange(piece_keys.shape[0], dtype=jnp.int32)
    piece_mask = jnp.any(chosen[:, :, None] == block_rows[None, None, :], axis=1)
    softmax_state = attend(softmax_state, queries, piece_keys, piece_values, piece_mask)
    _, final_total, final_summed = softmax_state
    mixed_rows = final_summed / jnp.transpose(final_total, (0, 2, 1))[:, :, :, None]
    attention = mixed_rows.reshape(rows_here, cols_here, feature_width)
    return attention + position(v_fresh, conv_w)


def head_scores(queries, keys):
    return lax.dot_general(
        queries, keys, (((1,), (1,)), ((), ())), preferred_element_type=jnp.float32
    )


def run_copies(copies, sems):
    copies = [pltpu.make_async_copy(*pair, sems.at[i]) for i, pair in enumerate(copies)]
    for copy in copies:
        copy.start()
    for copy in copies:
        copy.wait()


def pack_kernel(k_hbm, v_hbm, cells, text_k, text_v, stale, ends, text, sems):
    tokens, shard = k_hbm.shape[0], text_k.shape[0]
    copies = []
    for which, source in enumerate((text_k, text_v)):
        copies.append((source, text.at[pl.ds(which * shard, shard)]))
    for which, source in enumerate((k_hbm, v_hbm)):
        copies.append((source, stale.at[pl.ds(which * tokens, tokens)]))
    for which, at in enumerate((0, cells.shape[0] - 1)):
        copies.append((cells.at[at], ends.at[pl.ds(which * cells.shape[1], cells.shape[1])]))
    run_copies(copies, sems)


def send_kernel(wanted, stale, passed, *outs):
    row = lax.axis_index("rows")
    tokens = stale.shape[0] // 2

    def block_of(owner):
        found = 0
        for turn in range(2):
            entry = wanted[0, 0, turn]
            found = jnp.where(entry // 2 == owner, entry % 2, found)
        return found * PER_BLOCK

    starts = block_of(row), block_of(row + 1 - 2 * (row % 2))
    first = 0
    for out, spare in zip(outs, CHUNK_SPARE):
        part = pl.ds(first, out.shape[1])
        first += out.shape[1]
        for which in range(2):
            for slot, source in enumerate((stale, passed)):
                rows = pl.ds(pl.multiple_of(which * tokens + starts[slot], PER_BLOCK), PER_BLOCK)
                at = (2 * which + slot) * PER_BLOCK
                out[pl.ds(at, PER_BLOCK), :] = source[rows, part]
        if spare:
            rows = pl.ds(out.shape[0] - spare, spare)
            out[rows, :] = jnp.zeros((spare, out.shape[1]), out.dtype)


def bundle_kernel(*refs):
    out = refs[-1]
    count = out.shape[0] // (len(refs) - 1)
    for index, ref in enumerate(refs[:-1]):
        out[pl.ds(index * count, count), :] = ref[pl.ds(0, count), :]


def crop_kernel(source, out):
    out[...] = source[pl.ds(0, out.shape[0]), :]


def choose_kernel(upper, lower, *outs):
    upwards = lax.axis_index("cols") >= 2
    for index, out in enumerate(outs):
        rows = pl.ds(index * out.shape[0], out.shape[0])
        out[...] = jnp.where(upwards, upper[rows, :], lower[rows, :])


def offer_kernel(text, ends_mate, out):
    count = ends_mate.shape[0] // 2
    out[pl.ds(0, text.shape[0]), :] = text[...]
    first_core = lax.axis_index("rows") % 2 == 0
    out[pl.ds(text.shape[0], count), :] = jnp.where(
        first_core, ends_mate[pl.ds(count, count), :], ends_mate[pl.ds(0, count), :]
    )


def above_below(ends_mate, across, part):
    count = ends_mate.shape[0] // 2
    row = lax.axis_index("rows")
    beside_first, beside_last = (ends_mate[pl.ds(at, count), part] for at in (0, count))
    passed = across[pl.ds(across.shape[0] - count, count), part]
    passed = jnp.where((row > 0) & (row < 3), passed, jnp.zeros_like(passed))
    first_core = row % 2 == 0
    return (
        jnp.where(first_core, passed, beside_last),
        jnp.where(first_core, beside_first, passed),
    )


def join_kernel(text, across, cells, ends_mate, plus, minus):
    half = text.shape[0]
    rows_here, cols_here, width = cells.shape
    above, below = above_below(ends_mate, across, slice(None))
    rows = [above] + [cells[i] for i in range(rows_here)] + [below]
    rows = [row.astype(jnp.float32) for row in rows]
    spare = jnp.zeros((16 - len(rows), width), jnp.float32)
    for target, at in ((plus, cols_here - 1), (minus, 0)):
        target[pl.ds(0, half), :] = text[...]
        target[pl.ds(half, half), :] = across[pl.ds(0, half), :]
        edge = jnp.concatenate([row[at : at + 1] for row in rows] + [spare], axis=0)
        target[pl.ds(2 * half, 16), :] = edge.astype(target.dtype)


def term_kernel(cells, ends_mate, across, left, right, weights, out):
    rows_here, cols_here, width = cells.shape
    col = lax.axis_index("cols")
    edges = pl.ds(left.shape[0] - 16, 16)
    place = lax.broadcasted_iota(jnp.int32, (cols_here, HEAD_DIM), 0)
    for lane in range(width // HEAD_DIM):
        part = pl.ds(lane * HEAD_DIM, HEAD_DIM)
        above, below = above_below(ends_mate, across, part)
        lefts = left[edges, part].astype(jnp.float32)
        rights = right[edges, part].astype(jnp.float32)
        lefts = jnp.where(col > 0, lefts, 0.0)
        rights = jnp.where(col < 3, rights, 0.0)
        taps = []
        for row in range(rows_here + 2):
            if row == 0:
                centre = above
            elif row == rows_here + 1:
                centre = below
            else:
                centre = cells[row - 1, :, part]
            centre = centre.astype(jnp.float32)
            before = jnp.where(place == 0, lefts[row : row + 1], pltpu.roll(centre, 1, 0))
            after = jnp.where(
                place == cols_here - 1, rights[row : row + 1], pltpu.roll(centre, cols_here - 1, 0)
            )
            taps.append((before, centre, after))
        for row in range(rows_here):
            total = None
            for row_tap in range(3):
                for col_tap in range(3):
                    piece = weights[row_tap, col_tap : col_tap + 1, part] * taps[row + row_tap][col_tap]
                    total = piece if total is None else total + piece
            out[pl.ds(row * cols_here, cols_here), part] = total


def attend_kernel(first_head, reads_ref, pattern_ref, text_ref, q, k, v, *refs):
    home, home_mate, near, near_mate, passed, arrived, term = refs[:7]
    last, last_mate = refs[7:9], refs[9:11]
    out = refs[-1]
    row, col = lax.axis_index("rows"), lax.axis_index("cols")
    across, core = row // 2, row % 2
    shard = last[0].shape[0] // 2
    half = 2 * PER_BLOCK
    head_count = arrived.shape[1] // HEAD_DIM

    def lanes(head):
        return pl.ds((first_head + head) * HEAD_DIM, HEAD_DIM)

    def text_part(chosen, head, which):
        from_own = chosen % 2 == core
        from_side = chosen // 2 == across
        part = lanes(head)
        first = jnp.where(from_side, 0, 2 * shard) + which * shard
        rows = pl.ds(which * shard, shard)

        def one(own, other, at):
            spot = pl.ds(pl.multiple_of(first + at, shard), shard)
            return jnp.where(from_own, own[spot, part], other[spot, part])

        sides = [
            jnp.where(from_own, own[rows, part], other[rows, part])
            for own, other in zip(last, last_mate)
        ]
        return [
            one(home, home_mate, 0),
            one(near, near_mate, 0),
            one(near, near_mate, 4 * shard),
            jnp.where(from_side, *sides),
        ]

    def far_part(block, head, which):
        slot = pattern_ref[block, 0, 0] + pattern_ref[block, 0, 1] - block - 2
        wanted = reads_ref[0, 0, slot]
        owner = wanted // 2
        mate_at = (wanted % 2) * PER_BLOCK + which * half
        far_at = jnp.where(owner % 2 == core, 0, PER_BLOCK) + which * half
        mate = passed[pl.ds(pl.multiple_of(mate_at, PER_BLOCK), PER_BLOCK), lanes(head)]
        here = pl.ds(head * HEAD_DIM, HEAD_DIM)
        far = arrived[pl.ds(pl.multiple_of(far_at, PER_BLOCK), PER_BLOCK), here]
        return jnp.where(owner // 2 == across, mate, far)

    def gathered(block, head, which):
        own = (k, v)[which][pl.ds(block * PER_BLOCK, PER_BLOCK), lanes(head)]
        parts = [own]
        for turn in range(2):
            parts += text_part(text_ref[block, 0, turn], head, which)
        return jnp.concatenate(parts + [far_part(block, head, which)], axis=0)

    jobs = [(block, head) for head in range(head_count) for block in range(2)]
    size = -(-len(jobs) // -(-len(jobs) // GROUP))
    for at in range(0, len(jobs), size):
        group = jobs[at : at + size]
        scores = [
            head_scores(
                q[pl.ds(block * PER_BLOCK, PER_BLOCK), lanes(head)], gathered(block, head, 0)
            )
            for block, head in group
        ]
        peaks = [jnp.max(s, axis=1, keepdims=True) * EXP2_SCALE for s in scores]
        weights = [
            jnp.exp2(s * EXP2_SCALE - peak).astype(jnp.bfloat16) for s, peak in zip(scores, peaks)
        ]
        totals = [jnp.sum(w.astype(jnp.float32), axis=1, keepdims=True) for w in weights]
        products = [
            jnp.dot(w, gathered(block, head, 1), preferred_element_type=jnp.float32)
            for w, (block, head) in zip(weights, group)
        ]
        for product, total, (block, head) in zip(products, totals, group):
            rows = pl.ds(block * PER_BLOCK, PER_BLOCK)
            out[rows, pl.ds(head * HEAD_DIM, HEAD_DIM)] = product / total + term[rows, lanes(head)]


def body(
    q_fresh, k_fresh, v_fresh, k_stale, v_stale, text_k, text_v, conv_w, reads, pattern, text_blocks
):
    rows_here, cols_here, width = q_fresh.shape
    tokens = rows_here * cols_here
    shard = text_k.shape[0]
    swap = [(r, (r + 2) % 4) for r in range(4)]
    mates = [(r, r ^ 1) for r in range(4)]
    in_vmem = pl.BlockSpec(memory_space=pltpu.VMEM)
    in_hbm = pl.BlockSpec(memory_space=pltpu.HBM)
    params = pltpu.CompilerParams(vmem_limit_bytes=VMEM_LIMIT)
    cost = pl.CostEstimate(flops=1 << 20, transcendentals=0, bytes_accessed=1 << 16)

    def after(value, *others):
        return lax.optimization_barrier((value, *others))[0]

    def flat(grid_values):
        return grid_values.reshape(tokens, width)

    def to_mate(values):
        return lax.ppermute(values, "rows", mates)

    def rows_of(*counts):
        shapes = tuple(jax.ShapeDtypeStruct((n, width), jnp.bfloat16) for n in counts)
        return shapes if len(shapes) > 1 else shapes[0]

    def local(kernel, name, shapes, *args, specs=None, scratch=()):
        many = isinstance(shapes, tuple)
        return pl.pallas_call(
            kernel,
            out_shape=shapes,
            in_specs=specs or [in_vmem] * len(args),
            out_specs=(in_vmem,) * len(shapes) if many else in_vmem,
            scratch_shapes=scratch,
            compiler_params=params,
            cost_estimate=cost,
            name=name,
        )(*args)

    chunks = tuple(
        jax.ShapeDtypeStruct((2 * tokens + spare, n * HEAD_DIM), jnp.bfloat16)
        for n, spare in zip(CHUNK_HEADS, CHUNK_SPARE)
    )
    in_place = [
        pltpu.with_memory_space_constraint(value, pltpu.HBM)
        for value in (flat(k_stale), flat(v_stale), v_fresh, text_k, text_v)
    ]
    wanted = lax.ppermute(reads, "rows", swap)
    stale, ends, text = local(
        pack_kernel,
        "pack",
        rows_of(2 * tokens, 2 * cols_here, 2 * shard),
        *in_place,
        specs=[in_hbm] * 5,
        scratch=[pltpu.SemaphoreType.DMA((6,))],
    )
    ends_mate = to_mate(ends)
    offer = local(offer_kernel, "offer", rows_of(2 * shard + cols_here), text, ends_mate)
    across = lax.ppermute(after(offer, wanted), "rows", swap)
    passed = to_mate(stale)
    packed = local(
        send_kernel,
        "send",
        chunks,
        wanted,
        stale,
        passed,
        specs=[pl.BlockSpec(memory_space=pltpu.SMEM)] + [in_vmem] * 2,
    )
    far = [lax.ppermute(chunk, "rows", swap) for chunk in packed]

    plus, minus = local(
        join_kernel,
        "join",
        rows_of(4 * shard + 16, 4 * shard + 16),
        after(text, packed[0]),
        across,
        v_fresh,
        ends_mate,
    )
    left = lax.ppermute(plus, "cols", [(i, (i + 1) % 4) for i in range(4)])
    right = lax.ppermute(minus, "cols", [((i + 1) % 4, i) for i in range(4)])
    upper = lax.ppermute(local(crop_kernel, "crop", rows_of(4 * shard), left), "cols", [(1, 2), (2, 3)])
    lower = lax.ppermute(local(crop_kernel, "crop", rows_of(4 * shard), right), "cols", [(1, 0), (2, 1)])
    near = local(bundle_kernel, "bundle", rows_of(8 * shard), left, right)
    near_mate, plus_mate = to_mate(near), to_mate(plus)
    term = local(
        term_kernel,
        "term",
        jax.ShapeDtypeStruct((tokens, width), jnp.float32),
        v_fresh, ends_mate, across, left, right, conv_w,
    )
    rest = local(choose_kernel, "choose", rows_of(2 * shard, 2 * shard), after(upper, far[0], term), lower)
    rest_mate = [to_mate(part) for part in rest]

    out = None
    first_head = 0
    for chunk, head_count in enumerate(CHUNK_HEADS):
        if out is not None:
            far[chunk] = after(far[chunk], out)
        block = pl.BlockSpec(
            (pl.Element(tokens), pl.Element(head_count * HEAD_DIM)),
            lambda i, *_, at=first_head * HEAD_DIM: (0, at),
        )
        out = pl.pallas_call(
            functools.partial(attend_kernel, first_head),
            out_shape=jax.ShapeDtypeStruct((tokens, width), jnp.float32),
            grid_spec=pltpu.PrefetchScalarGridSpec(
                num_scalar_prefetch=3,
                grid=(1,),
                in_specs=[in_vmem] * 14 + [in_hbm] * (out is not None),
                out_specs=block,
            ),
            input_output_aliases={17: 0} if out is not None else {},
            compiler_params=params,
            cost_estimate=cost,
            name=f"attend{chunk}",
        )(
            reads, pattern, text_blocks, flat(q_fresh), flat(k_fresh), flat(v_fresh),
            plus, plus_mate, near, near_mate, passed, far[chunk], term, *rest, *rest_mate,
            *([out] if out is not None else []),
        )
        first_head += head_count
    return out.reshape(rows_here, cols_here, width)


def fits(mesh, reads, pattern, text_k):
    sizes = dict(mesh.shape)
    return (
        sizes["rows"] == 4
        and sizes["cols"] == 4
        and reads.shape[-1] == 2
        and pattern.shape[-1] == 2
        and pattern.shape[0] == 2 * sizes["groups"] * 4
        and text_k.shape[0] == sizes["groups"] * 4 * PER_BLOCK
    )


def solution(mesh):
    grid = P(("groups", "rows"), "cols", None)
    text = P(("groups", "rows", "cols"), None)
    in_specs = (grid, grid, grid, grid, grid, text, text, P(), grid, grid, grid)

    def program(*args):
        chosen = body if fits(mesh, args[8], args[9], args[5]) else general_body
        return jax.shard_map(
            chosen, mesh=mesh, in_specs=in_specs, out_specs=grid, check_vma=False
        )(*args)

    return program
```

```python
import functools
import math

import jax
import jax.numpy as jnp
from jax import lax
from jax.experimental import pallas as pl
from jax.experimental.pallas import tpu as pltpu
from jax.sharding import PartitionSpec as P

HEAD_DIM = 128
BLOCK_ROWS = 4
BLOCK_COLS = 32
PER_BLOCK = BLOCK_ROWS * BLOCK_COLS
SCORE_SCALE = 1.0 / math.sqrt(HEAD_DIM)
EXP2_SCALE = SCORE_SCALE * math.log2(math.e)
CHUNK_HEADS = (9, 3)
GROUP = 8
VMEM_LIMIT = 24 * 1024 * 1024


def extended(cells, sides, width):
    for axis, dim in sides:
        count = lax.axis_size(axis)
        ends = count - 1
        head = lax.slice_in_dim(cells, 0, width, axis=dim)
        tail = lax.slice_in_dim(cells, cells.shape[dim] - width, cells.shape[dim], axis=dim)
        cells = jnp.concatenate(
            [
                lax.ppermute(tail, axis, [(i, (i + 1) % count) for i in range(ends)]),
                cells,
                lax.ppermute(head, axis, [((i + 1) % count, i) for i in range(ends)]),
            ],
            axis=dim,
        )
    return cells


def position(v_fresh, conv_w):
    rows_here, cols_here, feature_width = v_fresh.shape
    rims = extended(v_fresh, (("rows", 0), ("cols", 1)), 1)
    position_term = jnp.zeros((rows_here, cols_here, feature_width), jnp.float32)
    for row_tap in range(3):
        for col_tap in range(3):
            position_term = position_term + conv_w[row_tap, col_tap] * rims[
                row_tap : row_tap + rows_here, col_tap : col_tap + cols_here
            ].astype(jnp.float32)
    return position_term


def split_heads(flat_rows):
    return flat_rows.reshape(flat_rows.shape[:-1] + (flat_rows.shape[-1] // HEAD_DIM, HEAD_DIM))


def attend(softmax_state, queries, key_blocks, value_blocks, allowed):
    old_peak, old_total, old_summed = softmax_state
    scores = (
        jnp.einsum(
            "bqhd,nkhd->bhqnk", queries, key_blocks, preferred_element_type=jnp.float32
        )
        * SCORE_SCALE
    )
    scores = jnp.where(allowed[:, None, None, :, None], scores, -1e30)
    new_peak = jnp.maximum(old_peak, jnp.max(scores, axis=(3, 4)))
    weights = jnp.exp(scores - new_peak[:, :, :, None, None]).astype(jnp.bfloat16)
    factor = jnp.exp(old_peak - new_peak)
    new_total = old_total * factor + jnp.sum(weights.astype(jnp.float32), axis=(3, 4))
    product = jnp.einsum(
        "bhqnk,nkhd->bqhd", weights, value_blocks, preferred_element_type=jnp.float32
    )
    new_summed = old_summed * jnp.transpose(factor, (0, 2, 1))[:, :, :, None] + product
    return (new_peak, new_total, new_summed)


def general_body(
    q_fresh, k_fresh, v_fresh, k_stale, v_stale, text_k, text_v, conv_w, reads, pattern, text_blocks
):
    rows_here, cols_here, feature_width = q_fresh.shape
    blocks_here = rows_here // BLOCK_ROWS
    head_count = feature_width // HEAD_DIM

    def as_blocks(grid_values):
        return split_heads(grid_values.reshape(blocks_here, PER_BLOCK, feature_width))

    queries = as_blocks(q_fresh)
    text_keys, text_values = (
        lax.all_gather(text_k, ("rows", "cols"), axis=0, tiled=True),
        lax.all_gather(text_v, ("rows", "cols"), axis=0, tiled=True),
    )
    text_count = text_keys.shape[0] // PER_BLOCK
    text_keys = split_heads(text_keys.reshape(text_count, PER_BLOCK, feature_width))
    text_values = split_heads(text_values.reshape(text_count, PER_BLOCK, feature_width))
    wanted = pattern[:, 0, :]
    fetch_rows = reads[0, 0, :]
    fetch_count = fetch_rows.shape[0]
    slot_count = blocks_here + fetch_count
    slot_mask = jnp.any(
        wanted[:, :, None] == jnp.arange(slot_count, dtype=jnp.int32)[None, None, :], axis=1
    )
    text_mask = jnp.any(
        text_blocks[:, 0, :, None] == jnp.arange(text_count, dtype=jnp.int32)[None, None, :], axis=1
    )
    softmax_state = (
        jnp.full((blocks_here, head_count, PER_BLOCK), -1e30, jnp.float32),
        jnp.zeros((blocks_here, head_count, PER_BLOCK), jnp.float32),
        jnp.zeros((blocks_here, PER_BLOCK, head_count, HEAD_DIM), jnp.float32),
    )
    softmax_state = attend(
        softmax_state,
        queries,
        jnp.concatenate([as_blocks(k_fresh), text_keys], axis=0),
        jnp.concatenate([as_blocks(v_fresh), text_values], axis=0),
        jnp.concatenate([slot_mask[:, :blocks_here], text_mask], axis=1),
    )
    chosen = jnp.where(
        wanted >= blocks_here, fetch_rows[jnp.clip(wanted - blocks_here, 0, fetch_count - 1)], -1
    )
    piece_keys = lax.all_gather(as_blocks(k_stale), "rows", axis=0, tiled=True)
    piece_values = lax.all_gather(as_blocks(v_stale), "rows", axis=0, tiled=True)
    block_rows = jnp.arange(piece_keys.shape[0], dtype=jnp.int32)
    piece_mask = jnp.any(chosen[:, :, None] == block_rows[None, None, :], axis=1)
    softmax_state = attend(softmax_state, queries, piece_keys, piece_values, piece_mask)
    _, final_total, final_summed = softmax_state
    mixed_rows = final_summed / jnp.transpose(final_total, (0, 2, 1))[:, :, :, None]
    attention = mixed_rows.reshape(rows_here, cols_here, feature_width)
    return attention + position(v_fresh, conv_w)


def head_scores(queries, keys):
    return lax.dot_general(
        queries, keys, (((1,), (1,)), ((), ())), preferred_element_type=jnp.float32
    )


def run_copies(copies, sems):
    copies = [pltpu.make_async_copy(*pair, sems.at[i]) for i, pair in enumerate(copies)]
    for copy in copies:
        copy.start()
    for copy in copies:
        copy.wait()


def pack_kernel(k_hbm, v_hbm, cells, text_k, text_v, stale, ends, text, sems):
    tokens, shard = k_hbm.shape[0], text_k.shape[0]
    copies = []
    for which, source in enumerate((text_k, text_v)):
        copies.append((source, text.at[pl.ds(which * shard, shard)]))
    for which, source in enumerate((k_hbm, v_hbm)):
        copies.append((source, stale.at[pl.ds(which * tokens, tokens)]))
    for which, at in enumerate((0, cells.shape[0] - 1)):
        copies.append((cells.at[at], ends.at[pl.ds(which * cells.shape[1], cells.shape[1])]))
    run_copies(copies, sems)


def offer_kernel(reads_ref, text, ends_mate, out):
    both, width = text.shape
    count = ends_mate.shape[0] // 2
    row = lax.axis_index("rows")
    partner = (row + 2) % 4

    def flag(owner):
        found = 0
        for turn in range(2):
            entry = reads_ref[0, 0, turn]
            found = jnp.where(entry // 2 == owner, entry % 2, found)
        return jnp.full((8, width // 2), found.astype(jnp.float32), jnp.float32)

    flags = [flag(owner) for owner in (partner, partner + 1 - 2 * (partner % 2))]
    out[pl.ds(0, both), :] = text[...]
    out[pl.ds(both, count), :] = jnp.where(
        row % 2 == 0, ends_mate[pl.ds(count, count), :], ends_mate[pl.ds(0, count), :]
    )
    out[pl.ds(both + count, 8), :] = jnp.concatenate(flags, axis=1).astype(out.dtype)


def send_kernel(across, stale, passed, *outs):
    tokens, width = stale.shape[0] // 2, stale.shape[1]

    def block_of(slot):
        lanes = pl.ds(slot * (width // 2), HEAD_DIM)
        flag = jnp.max(across[pl.ds(across.shape[0] - 8, 8), lanes].astype(jnp.float32))
        return jnp.where(flag > 0.5, PER_BLOCK, 0)

    starts = block_of(0), block_of(1)
    first = 0
    for out in outs:
        part = pl.ds(first, out.shape[1])
        first += out.shape[1]
        for which in range(2):
            for slot, source in enumerate((stale, passed)):
                rows = pl.ds(pl.multiple_of(which * tokens + starts[slot], PER_BLOCK), PER_BLOCK)
                at = (2 * which + slot) * PER_BLOCK
                out[pl.ds(at, PER_BLOCK), :] = source[rows, part]


def bundle_kernel(*refs):
    out = refs[-1]
    count = out.shape[0] // (len(refs) - 1)
    for index, ref in enumerate(refs[:-1]):
        out[pl.ds(index * count, count), :] = ref[pl.ds(0, count), :]


def above_below(ends_mate, across, part):
    count = ends_mate.shape[0] // 2
    row = lax.axis_index("rows")
    beside_first, beside_last = (ends_mate[pl.ds(at, count), part] for at in (0, count))
    passed = across[pl.ds(across.shape[0] - 8 - count, count), part]
    passed = jnp.where((row > 0) & (row < 3), passed, jnp.zeros_like(passed))
    first_core = row % 2 == 0
    return (
        jnp.where(first_core, passed, beside_last),
        jnp.where(first_core, beside_first, passed),
    )


def join_kernel(across, cells, ends_mate, peer, plus, minus):
    shard = peer.shape[0] // 2
    rows_here, cols_here, width = cells.shape
    above, below = above_below(ends_mate, across, slice(None))
    rows = [above] + [cells[i] for i in range(rows_here)] + [below]
    rows = [row.astype(jnp.float32) for row in rows]
    spare = jnp.zeros((16 - len(rows), width), jnp.float32)
    for target in (peer, plus, minus):
        target[pl.ds(0, 2 * shard), :] = across[pl.ds(0, 2 * shard), :]
    for target, at in ((plus, cols_here - 1), (minus, 0)):
        edge = jnp.concatenate([row[at : at + 1] for row in rows] + [spare], axis=0)
        target[pl.ds(2 * shard, 16), :] = edge.astype(target.dtype)


def term_kernel(cells, ends_mate, across, left, right, weights, out):
    rows_here, cols_here, width = cells.shape
    col = lax.axis_index("cols")
    edges = pl.ds(left.shape[0] - 16, 16)
    place = lax.broadcasted_iota(jnp.int32, (cols_here, HEAD_DIM), 0)
    for lane in range(width // HEAD_DIM):
        part = pl.ds(lane * HEAD_DIM, HEAD_DIM)
        above, below = above_below(ends_mate, across, part)
        lefts = left[edges, part].astype(jnp.float32)
        rights = right[edges, part].astype(jnp.float32)
        lefts = jnp.where(col > 0, lefts, 0.0)
        rights = jnp.where(col < 3, rights, 0.0)
        taps = []
        for row in range(rows_here + 2):
            if row == 0:
                centre = above
            elif row == rows_here + 1:
                centre = below
            else:
                centre = cells[row - 1, :, part]
            centre = centre.astype(jnp.float32)
            before = jnp.where(place == 0, lefts[row : row + 1], pltpu.roll(centre, 1, 0))
            after = jnp.where(
                place == cols_here - 1, rights[row : row + 1], pltpu.roll(centre, cols_here - 1, 0)
            )
            taps.append((before, centre, after))
        for row in range(rows_here):
            total = None
            for row_tap in range(3):
                for col_tap in range(3):
                    piece = weights[row_tap, col_tap : col_tap + 1, part] * taps[row + row_tap][col_tap]
                    total = piece if total is None else total + piece
            out[pl.ds(row * cols_here, cols_here), part] = total


def attend_kernel(first_head, reads_ref, pattern_ref, text_ref, q, k, v, *refs):
    near, near_mate, passed, arrived, term = refs[:5]
    side, side_mate = refs[5:9], refs[9:13]
    out = refs[-1]
    row, col = lax.axis_index("rows"), lax.axis_index("cols")
    across, core = row // 2, row % 2
    shard = near.shape[0] // 8
    half = 2 * PER_BLOCK
    head_count = arrived.shape[1] // HEAD_DIM

    def lanes(head):
        return pl.ds((first_head + head) * HEAD_DIM, HEAD_DIM)

    def text_part(chosen, head, which):
        from_own = chosen % 2 == core
        from_near = chosen // 2 == across
        part = lanes(head)

        def one(piece):
            rows = pl.ds((2 * piece + which) * shard, shard)
            here = pl.ds(which * shard, shard)
            return jnp.where(
                from_near,
                jnp.where(from_own, near[rows, part], near_mate[rows, part]),
                jnp.where(from_own, side[piece][here, part], side_mate[piece][here, part]),
            )

        return [one(piece) for piece in range(4)]

    def far_part(block, head, which):
        slot = pattern_ref[block, 0, 0] + pattern_ref[block, 0, 1] - block - 2
        wanted = reads_ref[0, 0, slot]
        owner = wanted // 2
        mate_at = (wanted % 2) * PER_BLOCK + which * half
        far_at = jnp.where(owner % 2 == core, 0, PER_BLOCK) + which * half
        mate = passed[pl.ds(pl.multiple_of(mate_at, PER_BLOCK), PER_BLOCK), lanes(head)]
        here = pl.ds(head * HEAD_DIM, HEAD_DIM)
        far = arrived[pl.ds(pl.multiple_of(far_at, PER_BLOCK), PER_BLOCK), here]
        return jnp.where(owner // 2 == across, mate, far)

    def gathered(block, head, which):
        own = (k, v)[which][pl.ds(block * PER_BLOCK, PER_BLOCK), lanes(head)]
        parts = [own]
        for turn in range(2):
            parts += text_part(text_ref[block, 0, turn], head, which)
        return jnp.concatenate(parts + [far_part(block, head, which)], axis=0)

    jobs = [(block, head) for head in range(head_count) for block in range(2)]
    size = -(-len(jobs) // -(-len(jobs) // GROUP))
    for at in range(0, len(jobs), size):
        group = jobs[at : at + size]
        scores = [
            head_scores(
                q[pl.ds(block * PER_BLOCK, PER_BLOCK), lanes(head)], gathered(block, head, 0)
            )
            for block, head in group
        ]
        peaks = [jnp.max(s, axis=1, keepdims=True) * EXP2_SCALE for s in scores]
        weights = [
            jnp.exp2(s * EXP2_SCALE - peak).astype(jnp.bfloat16) for s, peak in zip(scores, peaks)
        ]
        totals = [jnp.sum(w.astype(jnp.float32), axis=1, keepdims=True) for w in weights]
        products = [
            jnp.dot(w, gathered(block, head, 1), preferred_element_type=jnp.float32)
            for w, (block, head) in zip(weights, group)
        ]
        for product, total, (block, head) in zip(products, totals, group):
            rows = pl.ds(block * PER_BLOCK, PER_BLOCK)
            out[rows, pl.ds(head * HEAD_DIM, HEAD_DIM)] = product / total + term[rows, lanes(head)]


def body(
    q_fresh, k_fresh, v_fresh, k_stale, v_stale, text_k, text_v, conv_w, reads, pattern, text_blocks
):
    rows_here, cols_here, width = q_fresh.shape
    tokens = rows_here * cols_here
    shard = text_k.shape[0]
    swap = [(r, (r + 2) % 4) for r in range(4)]
    mates = [(r, r ^ 1) for r in range(4)]
    in_vmem = pl.BlockSpec(memory_space=pltpu.VMEM)
    in_hbm = pl.BlockSpec(memory_space=pltpu.HBM)
    params = pltpu.CompilerParams(vmem_limit_bytes=VMEM_LIMIT)
    cost = pl.CostEstimate(flops=1 << 20, transcendentals=0, bytes_accessed=1 << 16)

    def after(value, *others):
        return lax.optimization_barrier((value, *others))[0]

    def flat(grid_values):
        return grid_values.reshape(tokens, width)

    def to_mate(values):
        return lax.ppermute(values, "rows", mates)

    def rows_of(*counts):
        shapes = tuple(jax.ShapeDtypeStruct((n, width), jnp.bfloat16) for n in counts)
        return shapes if len(shapes) > 1 else shapes[0]

    def local(kernel, name, shapes, *args, specs=None, scratch=()):
        many = isinstance(shapes, tuple)
        return pl.pallas_call(
            kernel,
            out_shape=shapes,
            in_specs=specs or [in_vmem] * len(args),
            out_specs=(in_vmem,) * len(shapes) if many else in_vmem,
            scratch_shapes=scratch,
            compiler_params=params,
            cost_estimate=cost,
            name=name,
        )(*args)

    chunks = tuple(
        jax.ShapeDtypeStruct((2 * tokens, n * HEAD_DIM), jnp.bfloat16) for n in CHUNK_HEADS
    )
    in_place = [
        pltpu.with_memory_space_constraint(value, pltpu.HBM)
        for value in (flat(k_stale), flat(v_stale), v_fresh, text_k, text_v)
    ]
    stale, ends, text = local(
        pack_kernel,
        "pack",
        rows_of(2 * tokens, 2 * cols_here, 2 * shard),
        *in_place,
        specs=[in_hbm] * 5,
        scratch=[pltpu.SemaphoreType.DMA((6,))],
    )
    forward = [(i, (i + 1) % 4) for i in range(4)]
    backward = [(i, (i + 3) % 4) for i in range(4)]
    opposite = [(i, (i + 2) % 4) for i in range(4)]

    near_parts = [text] + [lax.ppermute(text, "cols", p) for p in (forward, backward, opposite)]
    ends_mate = to_mate(ends)
    offer = local(
        offer_kernel,
        "offer",
        rows_of(2 * shard + cols_here + 8),
        reads,
        text,
        ends_mate,
        specs=[pl.BlockSpec(memory_space=pltpu.SMEM)] + [in_vmem] * 2,
    )
    across = lax.ppermute(offer, "rows", swap)
    passed = to_mate(stale)
    packed = local(send_kernel, "send", chunks, across, stale, passed)
    far = [lax.ppermute(chunk, "rows", swap) for chunk in packed]

    peer, plus, minus = local(
        join_kernel,
        "join",
        rows_of(2 * shard, 2 * shard + 16, 2 * shard + 16),
        after(across, packed[0]),
        v_fresh,
        ends_mate,
    )
    left = lax.ppermute(plus, "cols", forward)
    right = lax.ppermute(minus, "cols", backward)
    side_parts = [peer, left, right, lax.ppermute(peer, "cols", opposite)]
    near_parts[0] = after(near_parts[0], packed[0])
    near = local(bundle_kernel, "bundle", rows_of(8 * shard), *near_parts)
    near_mate = to_mate(near)
    side_parts[3] = after(side_parts[3], near_mate)
    side_mate = [to_mate(part) for part in side_parts]
    term = local(
        term_kernel,
        "term",
        jax.ShapeDtypeStruct((tokens, width), jnp.float32),
        v_fresh, ends_mate, across, left, right, conv_w,
    )

    out = None
    first_head = 0
    for chunk, head_count in enumerate(CHUNK_HEADS):
        if out is not None:
            far[chunk] = after(far[chunk], out)
        block = pl.BlockSpec(
            (pl.Element(tokens), pl.Element(head_count * HEAD_DIM)),
            lambda i, *_, at=first_head * HEAD_DIM: (0, at),
        )
        out = pl.pallas_call(
            functools.partial(attend_kernel, first_head),
            out_shape=jax.ShapeDtypeStruct((tokens, width), jnp.float32),
            grid_spec=pltpu.PrefetchScalarGridSpec(
                num_scalar_prefetch=3,
                grid=(1,),
                in_specs=[in_vmem] * 16 + [in_hbm] * (out is not None),
                out_specs=block,
            ),
            input_output_aliases={19: 0} if out is not None else {},
            compiler_params=params,
            cost_estimate=cost,
            name=f"attend{chunk}",
        )(
            reads, pattern, text_blocks, flat(q_fresh), flat(k_fresh), flat(v_fresh),
            near, near_mate, passed, far[chunk], term, *side_parts, *side_mate,
            *([out] if out is not None else []),
        )
        first_head += head_count
    return out.reshape(rows_here, cols_here, width)


def fits(mesh, reads, pattern, text_k):
    sizes = dict(mesh.shape)
    return (
        sizes["rows"] == 4
        and sizes["cols"] == 4
        and reads.shape[-1] == 2
        and pattern.shape[-1] == 2
        and pattern.shape[0] == 2 * sizes["groups"] * 4
        and text_k.shape[0] == sizes["groups"] * 4 * PER_BLOCK
    )


def solution(mesh):
    grid = P(("groups", "rows"), "cols", None)
    text = P(("groups", "rows", "cols"), None)
    in_specs = (grid, grid, grid, grid, grid, text, text, P(), grid, grid, grid)

    def program(*args):
        chosen = body if fits(mesh, args[8], args[9], args[5]) else general_body
        return jax.shard_map(
            chosen, mesh=mesh, in_specs=in_specs, out_specs=grid, check_vma=False
        )(*args)

    return program
```

```python
import functools
import math

import jax
import jax.numpy as jnp
from jax import lax
from jax.experimental import pallas as pl
from jax.experimental.pallas import tpu as pltpu
from jax.sharding import PartitionSpec as P

HEAD_DIM = 128
BLOCK_ROWS = 4
BLOCK_COLS = 32
PER_BLOCK = BLOCK_ROWS * BLOCK_COLS
SCORE_SCALE = 1.0 / math.sqrt(HEAD_DIM)
EXP2_SCALE = SCORE_SCALE * math.log2(math.e)
CHUNK_HEADS = (9, 3)
GROUP = 8
VMEM_LIMIT = 24 * 1024 * 1024


def extended(cells, sides, width):
    for axis, dim in sides:
        count = lax.axis_size(axis)
        ends = count - 1
        head = lax.slice_in_dim(cells, 0, width, axis=dim)
        tail = lax.slice_in_dim(cells, cells.shape[dim] - width, cells.shape[dim], axis=dim)
        cells = jnp.concatenate(
            [
                lax.ppermute(tail, axis, [(i, (i + 1) % count) for i in range(ends)]),
                cells,
                lax.ppermute(head, axis, [((i + 1) % count, i) for i in range(ends)]),
            ],
            axis=dim,
        )
    return cells


def position(v_fresh, conv_w):
    rows_here, cols_here, feature_width = v_fresh.shape
    rims = extended(v_fresh, (("rows", 0), ("cols", 1)), 1)
    position_term = jnp.zeros((rows_here, cols_here, feature_width), jnp.float32)
    for row_tap in range(3):
        for col_tap in range(3):
            position_term = position_term + conv_w[row_tap, col_tap] * rims[
                row_tap : row_tap + rows_here, col_tap : col_tap + cols_here
            ].astype(jnp.float32)
    return position_term


def split_heads(flat_rows):
    return flat_rows.reshape(flat_rows.shape[:-1] + (flat_rows.shape[-1] // HEAD_DIM, HEAD_DIM))


def attend(softmax_state, queries, key_blocks, value_blocks, allowed):
    old_peak, old_total, old_summed = softmax_state
    scores = (
        jnp.einsum(
            "bqhd,nkhd->bhqnk", queries, key_blocks, preferred_element_type=jnp.float32
        )
        * SCORE_SCALE
    )
    scores = jnp.where(allowed[:, None, None, :, None], scores, -1e30)
    new_peak = jnp.maximum(old_peak, jnp.max(scores, axis=(3, 4)))
    weights = jnp.exp(scores - new_peak[:, :, :, None, None]).astype(jnp.bfloat16)
    factor = jnp.exp(old_peak - new_peak)
    new_total = old_total * factor + jnp.sum(weights.astype(jnp.float32), axis=(3, 4))
    product = jnp.einsum(
        "bhqnk,nkhd->bqhd", weights, value_blocks, preferred_element_type=jnp.float32
    )
    new_summed = old_summed * jnp.transpose(factor, (0, 2, 1))[:, :, :, None] + product
    return (new_peak, new_total, new_summed)


def general_body(
    q_fresh, k_fresh, v_fresh, k_stale, v_stale, text_k, text_v, conv_w, reads, pattern, text_blocks
):
    rows_here, cols_here, feature_width = q_fresh.shape
    blocks_here = rows_here // BLOCK_ROWS
    head_count = feature_width // HEAD_DIM

    def as_blocks(grid_values):
        return split_heads(grid_values.reshape(blocks_here, PER_BLOCK, feature_width))

    queries = as_blocks(q_fresh)
    text_keys, text_values = (
        lax.all_gather(text_k, ("rows", "cols"), axis=0, tiled=True),
        lax.all_gather(text_v, ("rows", "cols"), axis=0, tiled=True),
    )
    text_count = text_keys.shape[0] // PER_BLOCK
    text_keys = split_heads(text_keys.reshape(text_count, PER_BLOCK, feature_width))
    text_values = split_heads(text_values.reshape(text_count, PER_BLOCK, feature_width))
    wanted = pattern[:, 0, :]
    fetch_rows = reads[0, 0, :]
    fetch_count = fetch_rows.shape[0]
    slot_count = blocks_here + fetch_count
    slot_mask = jnp.any(
        wanted[:, :, None] == jnp.arange(slot_count, dtype=jnp.int32)[None, None, :], axis=1
    )
    text_mask = jnp.any(
        text_blocks[:, 0, :, None] == jnp.arange(text_count, dtype=jnp.int32)[None, None, :], axis=1
    )
    softmax_state = (
        jnp.full((blocks_here, head_count, PER_BLOCK), -1e30, jnp.float32),
        jnp.zeros((blocks_here, head_count, PER_BLOCK), jnp.float32),
        jnp.zeros((blocks_here, PER_BLOCK, head_count, HEAD_DIM), jnp.float32),
    )
    softmax_state = attend(
        softmax_state,
        queries,
        jnp.concatenate([as_blocks(k_fresh), text_keys], axis=0),
        jnp.concatenate([as_blocks(v_fresh), text_values], axis=0),
        jnp.concatenate([slot_mask[:, :blocks_here], text_mask], axis=1),
    )
    chosen = jnp.where(
        wanted >= blocks_here, fetch_rows[jnp.clip(wanted - blocks_here, 0, fetch_count - 1)], -1
    )
    piece_keys = lax.all_gather(as_blocks(k_stale), "rows", axis=0, tiled=True)
    piece_values = lax.all_gather(as_blocks(v_stale), "rows", axis=0, tiled=True)
    block_rows = jnp.arange(piece_keys.shape[0], dtype=jnp.int32)
    piece_mask = jnp.any(chosen[:, :, None] == block_rows[None, None, :], axis=1)
    softmax_state = attend(softmax_state, queries, piece_keys, piece_values, piece_mask)
    _, final_total, final_summed = softmax_state
    mixed_rows = final_summed / jnp.transpose(final_total, (0, 2, 1))[:, :, :, None]
    attention = mixed_rows.reshape(rows_here, cols_here, feature_width)
    return attention + position(v_fresh, conv_w)


def head_scores(queries, keys):
    return lax.dot_general(
        queries, keys, (((1,), (1,)), ((), ())), preferred_element_type=jnp.float32
    )


def run_copies(copies, sems):
    copies = [pltpu.make_async_copy(*pair, sems.at[i]) for i, pair in enumerate(copies)]
    for copy in copies:
        copy.start()
    for copy in copies:
        copy.wait()


def pack_kernel(k_hbm, v_hbm, cells, text_k, text_v, stale, ends, text, sems):
    tokens, shard = k_hbm.shape[0], text_k.shape[0]
    copies = []
    for which, source in enumerate((text_k, text_v)):
        copies.append((source, text.at[pl.ds(which * shard, shard)]))
    for which, source in enumerate((k_hbm, v_hbm)):
        copies.append((source, stale.at[pl.ds(which * tokens, tokens)]))
    for which, at in enumerate((0, cells.shape[0] - 1)):
        copies.append((cells.at[at], ends.at[pl.ds(which * cells.shape[1], cells.shape[1])]))
    run_copies(copies, sems)


def offer_kernel(reads_ref, text, ends_mate, out):
    both, width = text.shape
    count = ends_mate.shape[0] // 2
    row = lax.axis_index("rows")
    partner = (row + 2) % 4

    def flag(owner):
        found = 0
        for turn in range(2):
            entry = reads_ref[0, 0, turn]
            found = jnp.where(entry // 2 == owner, entry % 2, found)
        return jnp.full((8, width // 2), found.astype(jnp.float32), jnp.float32)

    flags = [flag(owner) for owner in (partner, partner + 1 - 2 * (partner % 2))]
    out[pl.ds(0, both), :] = text[...]
    out[pl.ds(both, count), :] = jnp.where(
        row % 2 == 0, ends_mate[pl.ds(count, count), :], ends_mate[pl.ds(0, count), :]
    )
    out[pl.ds(both + count, 8), :] = jnp.concatenate(flags, axis=1).astype(out.dtype)


def send_kernel(across, stale, passed, *outs):
    tokens, width = stale.shape[0] // 2, stale.shape[1]

    def block_of(slot):
        lanes = pl.ds(slot * (width // 2), HEAD_DIM)
        flag = jnp.max(across[pl.ds(across.shape[0] - 8, 8), lanes].astype(jnp.float32))
        return jnp.where(flag > 0.5, PER_BLOCK, 0)

    starts = block_of(0), block_of(1)
    first = 0
    for out in outs:
        part = pl.ds(first, out.shape[1])
        first += out.shape[1]
        for which in range(2):
            for slot, source in enumerate((stale, passed)):
                rows = pl.ds(pl.multiple_of(which * tokens + starts[slot], PER_BLOCK), PER_BLOCK)
                at = (2 * which + slot) * PER_BLOCK
                out[pl.ds(at, PER_BLOCK), :] = source[rows, part]


def bundle_kernel(*refs):
    out = refs[-1]
    count = out.shape[0] // (len(refs) - 1)
    for index, ref in enumerate(refs[:-1]):
        out[pl.ds(index * count, count), :] = ref[pl.ds(0, count), :]


def above_below(ends_mate, across, part):
    count = ends_mate.shape[0] // 2
    row = lax.axis_index("rows")
    beside_first, beside_last = (ends_mate[pl.ds(at, count), part] for at in (0, count))
    passed = across[pl.ds(across.shape[0] - 8 - count, count), part]
    passed = jnp.where((row > 0) & (row < 3), passed, jnp.zeros_like(passed))
    first_core = row % 2 == 0
    return (
        jnp.where(first_core, passed, beside_last),
        jnp.where(first_core, beside_first, passed),
    )


def join_kernel(across, cells, ends_mate, peer, plus, minus):
    shard = peer.shape[0] // 2
    rows_here, cols_here, width = cells.shape
    above, below = above_below(ends_mate, across, slice(None))
    rows = [above] + [cells[i] for i in range(rows_here)] + [below]
    rows = [row.astype(jnp.float32) for row in rows]
    spare = jnp.zeros((16 - len(rows), width), jnp.float32)
    for target in (peer, plus, minus):
        target[pl.ds(0, 2 * shard), :] = across[pl.ds(0, 2 * shard), :]
    for target, at in ((plus, cols_here - 1), (minus, 0)):
        edge = jnp.concatenate([row[at : at + 1] for row in rows] + [spare], axis=0)
        target[pl.ds(2 * shard, 16), :] = edge.astype(target.dtype)


def term_kernel(cells, ends_mate, across, left, right, weights, out):
    rows_here, cols_here, width = cells.shape
    col = lax.axis_index("cols")
    edges = pl.ds(left.shape[0] - 16, 16)
    place = lax.broadcasted_iota(jnp.int32, (cols_here, HEAD_DIM), 0)
    for lane in range(width // HEAD_DIM):
        part = pl.ds(lane * HEAD_DIM, HEAD_DIM)
        above, below = above_below(ends_mate, across, part)
        lefts = left[edges, part].astype(jnp.float32)
        rights = right[edges, part].astype(jnp.float32)
        lefts = jnp.where(col > 0, lefts, 0.0)
        rights = jnp.where(col < 3, rights, 0.0)
        taps = []
        for row in range(rows_here + 2):
            if row == 0:
                centre = above
            elif row == rows_here + 1:
                centre = below
            else:
                centre = cells[row - 1, :, part]
            centre = centre.astype(jnp.float32)
            before = jnp.where(place == 0, lefts[row : row + 1], pltpu.roll(centre, 1, 0))
            after = jnp.where(
                place == cols_here - 1, rights[row : row + 1], pltpu.roll(centre, cols_here - 1, 0)
            )
            taps.append((before, centre, after))
        for row in range(rows_here):
            total = None
            for row_tap in range(3):
                for col_tap in range(3):
                    piece = weights[row_tap, col_tap : col_tap + 1, part] * taps[row + row_tap][col_tap]
                    total = piece if total is None else total + piece
            out[pl.ds(row * cols_here, cols_here), part] = total


def attend_kernel(first_head, reads_ref, pattern_ref, text_ref, q, k, v, *refs):
    home, home_mate, near, near_mate, passed, arrived, term = refs[:7]
    side, side_mate = refs[7:11], refs[11:15]
    out = refs[-1]
    row, col = lax.axis_index("rows"), lax.axis_index("cols")
    across, core = row // 2, row % 2
    shard = home.shape[0] // 2
    half = 2 * PER_BLOCK
    head_count = arrived.shape[1] // HEAD_DIM

    def lanes(head):
        return pl.ds((first_head + head) * HEAD_DIM, HEAD_DIM)

    def text_part(chosen, head, which):
        from_own = chosen % 2 == core
        from_near = chosen // 2 == across
        part = lanes(head)

        def one(piece):
            here = pl.ds(which * shard, shard)
            rows = here if piece == 0 else pl.ds((2 * piece - 2 + which) * shard, shard)
            own, other = (home, home_mate) if piece == 0 else (near, near_mate)
            return jnp.where(
                from_near,
                jnp.where(from_own, own[rows, part], other[rows, part]),
                jnp.where(from_own, side[piece][here, part], side_mate[piece][here, part]),
            )

        return [one(piece) for piece in range(4)]

    def far_part(block, head, which):
        slot = pattern_ref[block, 0, 0] + pattern_ref[block, 0, 1] - block - 2
        wanted = reads_ref[0, 0, slot]
        owner = wanted // 2
        mate_at = (wanted % 2) * PER_BLOCK + which * half
        far_at = jnp.where(owner % 2 == core, 0, PER_BLOCK) + which * half
        mate = passed[pl.ds(pl.multiple_of(mate_at, PER_BLOCK), PER_BLOCK), lanes(head)]
        here = pl.ds(head * HEAD_DIM, HEAD_DIM)
        far = arrived[pl.ds(pl.multiple_of(far_at, PER_BLOCK), PER_BLOCK), here]
        return jnp.where(owner // 2 == across, mate, far)

    def gathered(block, head, which):
        own = (k, v)[which][pl.ds(block * PER_BLOCK, PER_BLOCK), lanes(head)]
        parts = [own]
        for turn in range(2):
            parts += text_part(text_ref[block, 0, turn], head, which)
        return jnp.concatenate(parts + [far_part(block, head, which)], axis=0)

    jobs = [(block, head) for head in range(head_count) for block in range(2)]
    size = -(-len(jobs) // -(-len(jobs) // GROUP))
    for at in range(0, len(jobs), size):
        group = jobs[at : at + size]
        scores = [
            head_scores(
                q[pl.ds(block * PER_BLOCK, PER_BLOCK), lanes(head)], gathered(block, head, 0)
            )
            for block, head in group
        ]
        peaks = [jnp.max(s, axis=1, keepdims=True) * EXP2_SCALE for s in scores]
        weights = [
            jnp.exp2(s * EXP2_SCALE - peak).astype(jnp.bfloat16) for s, peak in zip(scores, peaks)
        ]
        totals = [jnp.sum(w.astype(jnp.float32), axis=1, keepdims=True) for w in weights]
        products = [
            jnp.dot(w, gathered(block, head, 1), preferred_element_type=jnp.float32)
            for w, (block, head) in zip(weights, group)
        ]
        for product, total, (block, head) in zip(products, totals, group):
            rows = pl.ds(block * PER_BLOCK, PER_BLOCK)
            out[rows, pl.ds(head * HEAD_DIM, HEAD_DIM)] = product / total + term[rows, lanes(head)]


def body(
    q_fresh, k_fresh, v_fresh, k_stale, v_stale, text_k, text_v, conv_w, reads, pattern, text_blocks
):
    rows_here, cols_here, width = q_fresh.shape
    tokens = rows_here * cols_here
    shard = text_k.shape[0]
    swap = [(r, (r + 2) % 4) for r in range(4)]
    mates = [(r, r ^ 1) for r in range(4)]
    in_vmem = pl.BlockSpec(memory_space=pltpu.VMEM)
    in_hbm = pl.BlockSpec(memory_space=pltpu.HBM)
    params = pltpu.CompilerParams(vmem_limit_bytes=VMEM_LIMIT)
    cost = pl.CostEstimate(flops=1 << 20, transcendentals=0, bytes_accessed=1 << 16)

    def after(value, *others):
        return lax.optimization_barrier((value, *others))[0]

    def flat(grid_values):
        return grid_values.reshape(tokens, width)

    def to_mate(values):
        return lax.ppermute(values, "rows", mates)

    def rows_of(*counts):
        shapes = tuple(jax.ShapeDtypeStruct((n, width), jnp.bfloat16) for n in counts)
        return shapes if len(shapes) > 1 else shapes[0]

    def local(kernel, name, shapes, *args, specs=None, scratch=()):
        many = isinstance(shapes, tuple)
        return pl.pallas_call(
            kernel,
            out_shape=shapes,
            in_specs=specs or [in_vmem] * len(args),
            out_specs=(in_vmem,) * len(shapes) if many else in_vmem,
            scratch_shapes=scratch,
            compiler_params=params,
            cost_estimate=cost,
            name=name,
        )(*args)

    chunks = tuple(
        jax.ShapeDtypeStruct((2 * tokens, n * HEAD_DIM), jnp.bfloat16) for n in CHUNK_HEADS
    )
    in_place = [
        pltpu.with_memory_space_constraint(value, pltpu.HBM)
        for value in (flat(k_stale), flat(v_stale), v_fresh, text_k, text_v)
    ]
    stale, ends, text = local(
        pack_kernel,
        "pack",
        rows_of(2 * tokens, 2 * cols_here, 2 * shard),
        *in_place,
        specs=[in_hbm] * 5,
        scratch=[pltpu.SemaphoreType.DMA((6,))],
    )
    forward = [(i, (i + 1) % 4) for i in range(4)]
    backward = [(i, (i + 3) % 4) for i in range(4)]
    opposite = [(i, (i + 2) % 4) for i in range(4)]

    near_parts = [lax.ppermute(text, "cols", p) for p in (forward, backward, opposite)]
    ends_mate = to_mate(ends)
    offer = local(
        offer_kernel,
        "offer",
        rows_of(2 * shard + cols_here + 8),
        reads,
        text,
        ends_mate,
        specs=[pl.BlockSpec(memory_space=pltpu.SMEM)] + [in_vmem] * 2,
    )
    across = lax.ppermute(offer, "rows", swap)
    passed = to_mate(after(stale, ends_mate))
    packed = local(send_kernel, "send", chunks, across, stale, passed)
    far = [lax.ppermute(chunk, "rows", swap) for chunk in packed]

    text_mate = to_mate(text)
    peer, plus, minus = local(
        join_kernel,
        "join",
        rows_of(2 * shard, 2 * shard + 16, 2 * shard + 16),
        after(across, packed[0], text_mate),
        v_fresh,
        ends_mate,
    )
    near_parts[0] = after(near_parts[0], packed[0])
    near = local(bundle_kernel, "bundle", rows_of(6 * shard), *near_parts)
    near_mate = to_mate(near)
    left = lax.ppermute(plus, "cols", forward)
    right = lax.ppermute(after(minus, near_mate), "cols", backward)
    side_parts = [peer, left, right, lax.ppermute(peer, "cols", opposite)]
    side_mate = [to_mate(part) for part in side_parts]
    term = local(
        term_kernel,
        "term",
        jax.ShapeDtypeStruct((tokens, width), jnp.float32),
        v_fresh, ends_mate, across, left, right, conv_w,
    )

    out = None
    first_head = 0
    for chunk, head_count in enumerate(CHUNK_HEADS):
        if out is not None:
            far[chunk] = after(far[chunk], out)
        block = pl.BlockSpec(
            (pl.Element(tokens), pl.Element(head_count * HEAD_DIM)),
            lambda i, *_, at=first_head * HEAD_DIM: (0, at),
        )
        out = pl.pallas_call(
            functools.partial(attend_kernel, first_head),
            out_shape=jax.ShapeDtypeStruct((tokens, width), jnp.float32),
            grid_spec=pltpu.PrefetchScalarGridSpec(
                num_scalar_prefetch=3,
                grid=(1,),
                in_specs=[in_vmem] * 18 + [in_hbm] * (out is not None),
                out_specs=block,
            ),
            input_output_aliases={21: 0} if out is not None else {},
            compiler_params=params,
            cost_estimate=cost,
            name=f"attend{chunk}",
        )(
            reads, pattern, text_blocks, flat(q_fresh), flat(k_fresh), flat(v_fresh),
            text, text_mate, near, near_mate, passed, far[chunk], term, *side_parts, *side_mate,
            *([out] if out is not None else []),
        )
        first_head += head_count
    return out.reshape(rows_here, cols_here, width)


def fits(mesh, reads, pattern, text_k):
    sizes = dict(mesh.shape)
    return (
        sizes["rows"] == 4
        and sizes["cols"] == 4
        and reads.shape[-1] == 2
        and pattern.shape[-1] == 2
        and pattern.shape[0] == 2 * sizes["groups"] * 4
        and text_k.shape[0] == sizes["groups"] * 4 * PER_BLOCK
    )


def solution(mesh):
    grid = P(("groups", "rows"), "cols", None)
    text = P(("groups", "rows", "cols"), None)
    in_specs = (grid, grid, grid, grid, grid, text, text, P(), grid, grid, grid)

    def program(*args):
        chosen = body if fits(mesh, args[8], args[9], args[5]) else general_body
        return jax.shard_map(
            chosen, mesh=mesh, in_specs=in_specs, out_specs=grid, check_vma=False
        )(*args)

    return program
```

```python
import functools
import math

import jax
import jax.numpy as jnp
from jax import lax
from jax.experimental import pallas as pl
from jax.experimental.pallas import tpu as pltpu
from jax.sharding import PartitionSpec as P

HEAD_DIM = 128
BLOCK_ROWS = 4
BLOCK_COLS = 32
PER_BLOCK = BLOCK_ROWS * BLOCK_COLS
SCORE_SCALE = 1.0 / math.sqrt(HEAD_DIM)
EXP2_SCALE = SCORE_SCALE * math.log2(math.e)
CHUNK_HEADS = (9, 3)
GROUP = 8
VMEM_LIMIT = 24 * 1024 * 1024


def extended(cells, sides, width):
    for axis, dim in sides:
        count = lax.axis_size(axis)
        ends = count - 1
        head = lax.slice_in_dim(cells, 0, width, axis=dim)
        tail = lax.slice_in_dim(cells, cells.shape[dim] - width, cells.shape[dim], axis=dim)
        cells = jnp.concatenate(
            [
                lax.ppermute(tail, axis, [(i, (i + 1) % count) for i in range(ends)]),
                cells,
                lax.ppermute(head, axis, [((i + 1) % count, i) for i in range(ends)]),
            ],
            axis=dim,
        )
    return cells


def position(v_fresh, conv_w):
    rows_here, cols_here, feature_width = v_fresh.shape
    rims = extended(v_fresh, (("rows", 0), ("cols", 1)), 1)
    position_term = jnp.zeros((rows_here, cols_here, feature_width), jnp.float32)
    for row_tap in range(3):
        for col_tap in range(3):
            position_term = position_term + conv_w[row_tap, col_tap] * rims[
                row_tap : row_tap + rows_here, col_tap : col_tap + cols_here
            ].astype(jnp.float32)
    return position_term


def split_heads(flat_rows):
    return flat_rows.reshape(flat_rows.shape[:-1] + (flat_rows.shape[-1] // HEAD_DIM, HEAD_DIM))


def attend(softmax_state, queries, key_blocks, value_blocks, allowed):
    old_peak, old_total, old_summed = softmax_state
    scores = (
        jnp.einsum(
            "bqhd,nkhd->bhqnk", queries, key_blocks, preferred_element_type=jnp.float32
        )
        * SCORE_SCALE
    )
    scores = jnp.where(allowed[:, None, None, :, None], scores, -1e30)
    new_peak = jnp.maximum(old_peak, jnp.max(scores, axis=(3, 4)))
    weights = jnp.exp(scores - new_peak[:, :, :, None, None]).astype(jnp.bfloat16)
    factor = jnp.exp(old_peak - new_peak)
    new_total = old_total * factor + jnp.sum(weights.astype(jnp.float32), axis=(3, 4))
    product = jnp.einsum(
        "bhqnk,nkhd->bqhd", weights, value_blocks, preferred_element_type=jnp.float32
    )
    new_summed = old_summed * jnp.transpose(factor, (0, 2, 1))[:, :, :, None] + product
    return (new_peak, new_total, new_summed)


def general_body(
    q_fresh, k_fresh, v_fresh, k_stale, v_stale, text_k, text_v, conv_w, reads, pattern, text_blocks
):
    rows_here, cols_here, feature_width = q_fresh.shape
    blocks_here = rows_here // BLOCK_ROWS
    head_count = feature_width // HEAD_DIM

    def as_blocks(grid_values):
        return split_heads(grid_values.reshape(blocks_here, PER_BLOCK, feature_width))

    queries = as_blocks(q_fresh)
    text_keys, text_values = (
        lax.all_gather(text_k, ("rows", "cols"), axis=0, tiled=True),
        lax.all_gather(text_v, ("rows", "cols"), axis=0, tiled=True),
    )
    text_count = text_keys.shape[0] // PER_BLOCK
    text_keys = split_heads(text_keys.reshape(text_count, PER_BLOCK, feature_width))
    text_values = split_heads(text_values.reshape(text_count, PER_BLOCK, feature_width))
    wanted = pattern[:, 0, :]
    fetch_rows = reads[0, 0, :]
    fetch_count = fetch_rows.shape[0]
    slot_count = blocks_here + fetch_count
    slot_mask = jnp.any(
        wanted[:, :, None] == jnp.arange(slot_count, dtype=jnp.int32)[None, None, :], axis=1
    )
    text_mask = jnp.any(
        text_blocks[:, 0, :, None] == jnp.arange(text_count, dtype=jnp.int32)[None, None, :], axis=1
    )
    softmax_state = (
        jnp.full((blocks_here, head_count, PER_BLOCK), -1e30, jnp.float32),
        jnp.zeros((blocks_here, head_count, PER_BLOCK), jnp.float32),
        jnp.zeros((blocks_here, PER_BLOCK, head_count, HEAD_DIM), jnp.float32),
    )
    softmax_state = attend(
        softmax_state,
        queries,
        jnp.concatenate([as_blocks(k_fresh), text_keys], axis=0),
        jnp.concatenate([as_blocks(v_fresh), text_values], axis=0),
        jnp.concatenate([slot_mask[:, :blocks_here], text_mask], axis=1),
    )
    chosen = jnp.where(
        wanted >= blocks_here, fetch_rows[jnp.clip(wanted - blocks_here, 0, fetch_count - 1)], -1
    )
    piece_keys = lax.all_gather(as_blocks(k_stale), "rows", axis=0, tiled=True)
    piece_values = lax.all_gather(as_blocks(v_stale), "rows", axis=0, tiled=True)
    block_rows = jnp.arange(piece_keys.shape[0], dtype=jnp.int32)
    piece_mask = jnp.any(chosen[:, :, None] == block_rows[None, None, :], axis=1)
    softmax_state = attend(softmax_state, queries, piece_keys, piece_values, piece_mask)
    _, final_total, final_summed = softmax_state
    mixed_rows = final_summed / jnp.transpose(final_total, (0, 2, 1))[:, :, :, None]
    attention = mixed_rows.reshape(rows_here, cols_here, feature_width)
    return attention + position(v_fresh, conv_w)


def head_scores(queries, keys):
    return lax.dot_general(
        queries, keys, (((1,), (1,)), ((), ())), preferred_element_type=jnp.float32
    )


def run_copies(copies, sems):
    copies = [pltpu.make_async_copy(*pair, sems.at[i]) for i, pair in enumerate(copies)]
    for copy in copies:
        copy.start()
    for copy in copies:
        copy.wait()


def pack_kernel(k_hbm, v_hbm, cells, text_k, text_v, stale, ends, text, sems):
    tokens, shard = k_hbm.shape[0], text_k.shape[0]
    copies = []
    for which, source in enumerate((text_k, text_v)):
        copies.append((source, text.at[pl.ds(which * shard, shard)]))
    for which, source in enumerate((k_hbm, v_hbm)):
        copies.append((source, stale.at[pl.ds(which * tokens, tokens)]))
    for which, at in enumerate((0, cells.shape[0] - 1)):
        copies.append((cells.at[at], ends.at[pl.ds(which * cells.shape[1], cells.shape[1])]))
    run_copies(copies, sems)


def offer_kernel(reads_ref, text, ends_mate, out):
    both, width = text.shape
    count = ends_mate.shape[0] // 2
    row = lax.axis_index("rows")
    partner = (row + 2) % 4

    def flag(owner):
        found = 0
        for turn in range(2):
            entry = reads_ref[0, 0, turn]
            found = jnp.where(entry // 2 == owner, entry % 2, found)
        return jnp.full((8, width // 2), found.astype(jnp.float32), jnp.float32)

    flags = [flag(owner) for owner in (partner, partner + 1 - 2 * (partner % 2))]
    out[pl.ds(0, both), :] = text[...]
    out[pl.ds(both, count), :] = jnp.where(
        row % 2 == 0, ends_mate[pl.ds(count, count), :], ends_mate[pl.ds(0, count), :]
    )
    out[pl.ds(both + count, 8), :] = jnp.concatenate(flags, axis=1).astype(out.dtype)


def send_kernel(across, stale, passed, *outs):
    tokens, width = stale.shape[0] // 2, stale.shape[1]

    def block_of(slot):
        lanes = pl.ds(slot * (width // 2), HEAD_DIM)
        flag = jnp.max(across[pl.ds(across.shape[0] - 8, 8), lanes].astype(jnp.float32))
        return jnp.where(flag > 0.5, PER_BLOCK, 0)

    starts = block_of(0), block_of(1)
    first = 0
    for out in outs:
        part = pl.ds(first, out.shape[1])
        first += out.shape[1]
        for which in range(2):
            for slot, source in enumerate((stale, passed)):
                rows = pl.ds(pl.multiple_of(which * tokens + starts[slot], PER_BLOCK), PER_BLOCK)
                at = (2 * which + slot) * PER_BLOCK
                out[pl.ds(at, PER_BLOCK), :] = source[rows, part]


def split_kernel(source, first, second):
    half = first.shape[0]
    first[...] = source[pl.ds(0, half), :]
    second[...] = source[pl.ds(half, half), :]


def above_below(ends_mate, across, part):
    count = ends_mate.shape[0] // 2
    row = lax.axis_index("rows")
    beside_first, beside_last = (ends_mate[pl.ds(at, count), part] for at in (0, count))
    passed = across[pl.ds(across.shape[0] - 8 - count, count), part]
    passed = jnp.where((row > 0) & (row < 3), passed, jnp.zeros_like(passed))
    first_core = row % 2 == 0
    return (
        jnp.where(first_core, passed, beside_last),
        jnp.where(first_core, beside_first, passed),
    )


def join_kernel(text, across, cells, ends_mate, both, plus, minus):
    shard = text.shape[0] // 2
    rows_here, cols_here, width = cells.shape
    above, below = above_below(ends_mate, across, slice(None))
    rows = [above] + [cells[i] for i in range(rows_here)] + [below]
    rows = [row.astype(jnp.float32) for row in rows]
    spare = jnp.zeros((16 - len(rows), width), jnp.float32)
    both[pl.ds(0, 2 * shard), :] = text[...]
    both[pl.ds(2 * shard, 2 * shard), :] = across[pl.ds(0, 2 * shard), :]
    for target in (plus, minus):
        target[pl.ds(0, 2 * shard), :] = across[pl.ds(0, 2 * shard), :]
    for target, at in ((plus, cols_here - 1), (minus, 0)):
        edge = jnp.concatenate([row[at : at + 1] for row in rows] + [spare], axis=0)
        target[pl.ds(2 * shard, 16), :] = edge.astype(target.dtype)


def term_kernel(cells, ends_mate, across, left, right, weights, out):
    rows_here, cols_here, width = cells.shape
    col = lax.axis_index("cols")
    edges = pl.ds(left.shape[0] - 16, 16)
    place = lax.broadcasted_iota(jnp.int32, (cols_here, HEAD_DIM), 0)
    for lane in range(width // HEAD_DIM):
        part = pl.ds(lane * HEAD_DIM, HEAD_DIM)
        above, below = above_below(ends_mate, across, part)
        lefts = left[edges, part].astype(jnp.float32)
        rights = right[edges, part].astype(jnp.float32)
        lefts = jnp.where(col > 0, lefts, 0.0)
        rights = jnp.where(col < 3, rights, 0.0)
        taps = []
        for row in range(rows_here + 2):
            if row == 0:
                centre = above
            elif row == rows_here + 1:
                centre = below
            else:
                centre = cells[row - 1, :, part]
            centre = centre.astype(jnp.float32)
            before = jnp.where(place == 0, lefts[row : row + 1], pltpu.roll(centre, 1, 0))
            after = jnp.where(
                place == cols_here - 1, rights[row : row + 1], pltpu.roll(centre, cols_here - 1, 0)
            )
            taps.append((before, centre, after))
        for row in range(rows_here):
            total = None
            for row_tap in range(3):
                for col_tap in range(3):
                    piece = weights[row_tap, col_tap : col_tap + 1, part] * taps[row + row_tap][col_tap]
                    total = piece if total is None else total + piece
            out[pl.ds(row * cols_here, cols_here), part] = total


def attend_kernel(first_head, reads_ref, pattern_ref, text_ref, q, k, v, *refs):
    passed, arrived, term = refs[:3]
    near, near_mate, side, side_mate = (refs[3 + 4 * i : 7 + 4 * i] for i in range(4))
    out = refs[-1]
    row, col = lax.axis_index("rows"), lax.axis_index("cols")
    across, core = row // 2, row % 2
    shard = near[0].shape[0] // 2
    half = 2 * PER_BLOCK
    head_count = arrived.shape[1] // HEAD_DIM

    def lanes(head):
        return pl.ds((first_head + head) * HEAD_DIM, HEAD_DIM)

    def text_part(chosen, head, which):
        from_own = chosen % 2 == core
        from_near = chosen // 2 == across
        part = lanes(head)

        def one(piece):
            rows = pl.ds(which * shard, shard)
            return jnp.where(
                from_near,
                jnp.where(from_own, near[piece][rows, part], near_mate[piece][rows, part]),
                jnp.where(from_own, side[piece][rows, part], side_mate[piece][rows, part]),
            )

        return [one(piece) for piece in range(4)]

    def far_part(block, head, which):
        slot = pattern_ref[block, 0, 0] + pattern_ref[block, 0, 1] - block - 2
        wanted = reads_ref[0, 0, slot]
        owner = wanted // 2
        mate_at = (wanted % 2) * PER_BLOCK + which * half
        far_at = jnp.where(owner % 2 == core, 0, PER_BLOCK) + which * half
        mate = passed[pl.ds(pl.multiple_of(mate_at, PER_BLOCK), PER_BLOCK), lanes(head)]
        here = pl.ds(head * HEAD_DIM, HEAD_DIM)
        far = arrived[pl.ds(pl.multiple_of(far_at, PER_BLOCK), PER_BLOCK), here]
        return jnp.where(owner // 2 == across, mate, far)

    def gathered(block, head, which):
        own = (k, v)[which][pl.ds(block * PER_BLOCK, PER_BLOCK), lanes(head)]
        parts = [own]
        for turn in range(2):
            parts += text_part(text_ref[block, 0, turn], head, which)
        return jnp.concatenate(parts + [far_part(block, head, which)], axis=0)

    jobs = [(block, head) for head in range(head_count) for block in range(2)]
    size = -(-len(jobs) // -(-len(jobs) // GROUP))
    for at in range(0, len(jobs), size):
        group = jobs[at : at + size]
        scores = [
            head_scores(
                q[pl.ds(block * PER_BLOCK, PER_BLOCK), lanes(head)], gathered(block, head, 0)
            )
            for block, head in group
        ]
        peaks = [jnp.max(s, axis=1, keepdims=True) * EXP2_SCALE for s in scores]
        weights = [
            jnp.exp2(s * EXP2_SCALE - peak).astype(jnp.bfloat16) for s, peak in zip(scores, peaks)
        ]
        totals = [jnp.sum(w.astype(jnp.float32), axis=1, keepdims=True) for w in weights]
        products = [
            jnp.dot(w, gathered(block, head, 1), preferred_element_type=jnp.float32)
            for w, (block, head) in zip(weights, group)
        ]
        for product, total, (block, head) in zip(products, totals, group):
            rows = pl.ds(block * PER_BLOCK, PER_BLOCK)
            out[rows, pl.ds(head * HEAD_DIM, HEAD_DIM)] = product / total + term[rows, lanes(head)]


def body(
    q_fresh, k_fresh, v_fresh, k_stale, v_stale, text_k, text_v, conv_w, reads, pattern, text_blocks
):
    rows_here, cols_here, width = q_fresh.shape
    tokens = rows_here * cols_here
    shard = text_k.shape[0]
    swap = [(r, (r + 2) % 4) for r in range(4)]
    mates = [(r, r ^ 1) for r in range(4)]
    in_vmem = pl.BlockSpec(memory_space=pltpu.VMEM)
    in_hbm = pl.BlockSpec(memory_space=pltpu.HBM)
    params = pltpu.CompilerParams(vmem_limit_bytes=VMEM_LIMIT)
    cost = pl.CostEstimate(flops=1 << 20, transcendentals=0, bytes_accessed=1 << 16)

    def after(value, *others):
        return lax.optimization_barrier((value, *others))[0]

    def flat(grid_values):
        return grid_values.reshape(tokens, width)

    def to_mate(values):
        return lax.ppermute(values, "rows", mates)

    def rows_of(*counts):
        shapes = tuple(jax.ShapeDtypeStruct((n, width), jnp.bfloat16) for n in counts)
        return shapes if len(shapes) > 1 else shapes[0]

    def local(kernel, name, shapes, *args, specs=None, scratch=()):
        many = isinstance(shapes, tuple)
        return pl.pallas_call(
            kernel,
            out_shape=shapes,
            in_specs=specs or [in_vmem] * len(args),
            out_specs=(in_vmem,) * len(shapes) if many else in_vmem,
            scratch_shapes=scratch,
            compiler_params=params,
            cost_estimate=cost,
            name=name,
        )(*args)

    chunks = tuple(
        jax.ShapeDtypeStruct((2 * tokens, n * HEAD_DIM), jnp.bfloat16) for n in CHUNK_HEADS
    )
    in_place = [
        pltpu.with_memory_space_constraint(value, pltpu.HBM)
        for value in (flat(k_stale), flat(v_stale), v_fresh, text_k, text_v)
    ]
    stale, ends, text = local(
        pack_kernel,
        "pack",
        rows_of(2 * tokens, 2 * cols_here, 2 * shard),
        *in_place,
        specs=[in_hbm] * 5,
        scratch=[pltpu.SemaphoreType.DMA((6,))],
    )
    forward = [(i, (i + 1) % 4) for i in range(4)]
    backward = [(i, (i + 3) % 4) for i in range(4)]
    opposite = [(i, (i + 2) % 4) for i in range(4)]

    near_parts = [lax.ppermute(text, "cols", p) for p in (forward, backward)]
    ends_mate = to_mate(ends)
    offer = local(
        offer_kernel,
        "offer",
        rows_of(2 * shard + cols_here + 8),
        reads,
        text,
        ends_mate,
        specs=[pl.BlockSpec(memory_space=pltpu.SMEM)] + [in_vmem] * 2,
    )
    across = lax.ppermute(offer, "rows", swap)
    passed = to_mate(after(stale, ends_mate))
    packed = local(
        send_kernel, "send", chunks, after(across, *near_parts), stale, passed
    )
    far = [lax.ppermute(chunk, "rows", swap) for chunk in packed]

    both, plus, minus = local(
        join_kernel,
        "join",
        rows_of(4 * shard, 2 * shard + 16, 2 * shard + 16),
        text,
        after(across, packed[0], *near_parts),
        v_fresh,
        ends_mate,
    )
    left = lax.ppermute(plus, "cols", forward)
    right = lax.ppermute(minus, "cols", backward)
    across_cols = lax.ppermute(both, "cols", opposite)
    own_side, far_side = (
        local(split_kernel, "split", rows_of(2 * shard, 2 * shard), value)
        for value in (both, across_cols)
    )
    near_parts = [text, *near_parts, far_side[0]]
    side_parts = [own_side[1], left, right, far_side[1]]
    near_mate = [to_mate(part) for part in near_parts]
    side_mate = [to_mate(part) for part in side_parts]
    term = local(
        term_kernel,
        "term",
        jax.ShapeDtypeStruct((tokens, width), jnp.float32),
        v_fresh, ends_mate, across, left, right, conv_w,
    )

    out = None
    first_head = 0
    for chunk, head_count in enumerate(CHUNK_HEADS):
        if out is not None:
            far[chunk] = after(far[chunk], out)
        block = pl.BlockSpec(
            (pl.Element(tokens), pl.Element(head_count * HEAD_DIM)),
            lambda i, *_, at=first_head * HEAD_DIM: (0, at),
        )
        out = pl.pallas_call(
            functools.partial(attend_kernel, first_head),
            out_shape=jax.ShapeDtypeStruct((tokens, width), jnp.float32),
            grid_spec=pltpu.PrefetchScalarGridSpec(
                num_scalar_prefetch=3,
                grid=(1,),
                in_specs=[in_vmem] * 22 + [in_hbm] * (out is not None),
                out_specs=block,
            ),
            input_output_aliases={25: 0} if out is not None else {},
            compiler_params=params,
            cost_estimate=cost,
            name=f"attend{chunk}",
        )(
            reads, pattern, text_blocks, flat(q_fresh), flat(k_fresh), flat(v_fresh),
            passed, far[chunk], term, *near_parts, *near_mate, *side_parts, *side_mate,
            *([out] if out is not None else []),
        )
        first_head += head_count
    return out.reshape(rows_here, cols_here, width)


def fits(mesh, reads, pattern, text_k):
    sizes = dict(mesh.shape)
    return (
        sizes["rows"] == 4
        and sizes["cols"] == 4
        and reads.shape[-1] == 2
        and pattern.shape[-1] == 2
        and pattern.shape[0] == 2 * sizes["groups"] * 4
        and text_k.shape[0] == sizes["groups"] * 4 * PER_BLOCK
    )


def solution(mesh):
    grid = P(("groups", "rows"), "cols", None)
    text = P(("groups", "rows", "cols"), None)
    in_specs = (grid, grid, grid, grid, grid, text, text, P(), grid, grid, grid)

    def program(*args):
        chosen = body if fits(mesh, args[8], args[9], args[5]) else general_body
        return jax.shard_map(
            chosen, mesh=mesh, in_specs=in_specs, out_specs=grid, check_vma=False
        )(*args)

    return program
```

```python
import functools
import math

import jax
import jax.numpy as jnp
from jax import lax
from jax.experimental import pallas as pl
from jax.experimental.pallas import tpu as pltpu
from jax.sharding import PartitionSpec as P

HEAD_DIM = 128
BLOCK_ROWS = 4
BLOCK_COLS = 32
PER_BLOCK = BLOCK_ROWS * BLOCK_COLS
SCORE_SCALE = 1.0 / math.sqrt(HEAD_DIM)
EXP2_SCALE = SCORE_SCALE * math.log2(math.e)
CHUNK_HEADS = (8, 4)
GROUP = 8
VMEM_LIMIT = 24 * 1024 * 1024


def extended(cells, sides, width):
    for axis, dim in sides:
        count = lax.axis_size(axis)
        ends = count - 1
        head = lax.slice_in_dim(cells, 0, width, axis=dim)
        tail = lax.slice_in_dim(cells, cells.shape[dim] - width, cells.shape[dim], axis=dim)
        cells = jnp.concatenate(
            [
                lax.ppermute(tail, axis, [(i, (i + 1) % count) for i in range(ends)]),
                cells,
                lax.ppermute(head, axis, [((i + 1) % count, i) for i in range(ends)]),
            ],
            axis=dim,
        )
    return cells


def position(v_fresh, conv_w):
    rows_here, cols_here, feature_width = v_fresh.shape
    rims = extended(v_fresh, (("rows", 0), ("cols", 1)), 1)
    position_term = jnp.zeros((rows_here, cols_here, feature_width), jnp.float32)
    for row_tap in range(3):
        for col_tap in range(3):
            position_term = position_term + conv_w[row_tap, col_tap] * rims[
                row_tap : row_tap + rows_here, col_tap : col_tap + cols_here
            ].astype(jnp.float32)
    return position_term


def split_heads(flat_rows):
    return flat_rows.reshape(flat_rows.shape[:-1] + (flat_rows.shape[-1] // HEAD_DIM, HEAD_DIM))


def attend(softmax_state, queries, key_blocks, value_blocks, allowed):
    old_peak, old_total, old_summed = softmax_state
    scores = (
        jnp.einsum(
            "bqhd,nkhd->bhqnk", queries, key_blocks, preferred_element_type=jnp.float32
        )
        * SCORE_SCALE
    )
    scores = jnp.where(allowed[:, None, None, :, None], scores, -1e30)
    new_peak = jnp.maximum(old_peak, jnp.max(scores, axis=(3, 4)))
    weights = jnp.exp(scores - new_peak[:, :, :, None, None]).astype(jnp.bfloat16)
    factor = jnp.exp(old_peak - new_peak)
    new_total = old_total * factor + jnp.sum(weights.astype(jnp.float32), axis=(3, 4))
    product = jnp.einsum(
        "bhqnk,nkhd->bqhd", weights, value_blocks, preferred_element_type=jnp.float32
    )
    new_summed = old_summed * jnp.transpose(factor, (0, 2, 1))[:, :, :, None] + product
    return (new_peak, new_total, new_summed)


def general_body(
    q_fresh, k_fresh, v_fresh, k_stale, v_stale, text_k, text_v, conv_w, reads, pattern, text_blocks
):
    rows_here, cols_here, feature_width = q_fresh.shape
    blocks_here = rows_here // BLOCK_ROWS
    head_count = feature_width // HEAD_DIM

    def as_blocks(grid_values):
        return split_heads(grid_values.reshape(blocks_here, PER_BLOCK, feature_width))

    queries = as_blocks(q_fresh)
    text_keys, text_values = (
        lax.all_gather(text_k, ("rows", "cols"), axis=0, tiled=True),
        lax.all_gather(text_v, ("rows", "cols"), axis=0, tiled=True),
    )
    text_count = text_keys.shape[0] // PER_BLOCK
    text_keys = split_heads(text_keys.reshape(text_count, PER_BLOCK, feature_width))
    text_values = split_heads(text_values.reshape(text_count, PER_BLOCK, feature_width))
    wanted = pattern[:, 0, :]
    fetch_rows = reads[0, 0, :]
    fetch_count = fetch_rows.shape[0]
    slot_count = blocks_here + fetch_count
    slot_mask = jnp.any(
        wanted[:, :, None] == jnp.arange(slot_count, dtype=jnp.int32)[None, None, :], axis=1
    )
    text_mask = jnp.any(
        text_blocks[:, 0, :, None] == jnp.arange(text_count, dtype=jnp.int32)[None, None, :], axis=1
    )
    softmax_state = (
        jnp.full((blocks_here, head_count, PER_BLOCK), -1e30, jnp.float32),
        jnp.zeros((blocks_here, head_count, PER_BLOCK), jnp.float32),
        jnp.zeros((blocks_here, PER_BLOCK, head_count, HEAD_DIM), jnp.float32),
    )
    softmax_state = attend(
        softmax_state,
        queries,
        jnp.concatenate([as_blocks(k_fresh), text_keys], axis=0),
        jnp.concatenate([as_blocks(v_fresh), text_values], axis=0),
        jnp.concatenate([slot_mask[:, :blocks_here], text_mask], axis=1),
    )
    chosen = jnp.where(
        wanted >= blocks_here, fetch_rows[jnp.clip(wanted - blocks_here, 0, fetch_count - 1)], -1
    )
    piece_keys = lax.all_gather(as_blocks(k_stale), "rows", axis=0, tiled=True)
    piece_values = lax.all_gather(as_blocks(v_stale), "rows", axis=0, tiled=True)
    block_rows = jnp.arange(piece_keys.shape[0], dtype=jnp.int32)
    piece_mask = jnp.any(chosen[:, :, None] == block_rows[None, None, :], axis=1)
    softmax_state = attend(softmax_state, queries, piece_keys, piece_values, piece_mask)
    _, final_total, final_summed = softmax_state
    mixed_rows = final_summed / jnp.transpose(final_total, (0, 2, 1))[:, :, :, None]
    attention = mixed_rows.reshape(rows_here, cols_here, feature_width)
    return attention + position(v_fresh, conv_w)


def head_scores(queries, keys):
    return lax.dot_general(
        queries, keys, (((1,), (1,)), ((), ())), preferred_element_type=jnp.float32
    )


def run_copies(copies, sems):
    copies = [pltpu.make_async_copy(*pair, sems.at[i]) for i, pair in enumerate(copies)]
    for copy in copies:
        copy.start()
    for copy in copies:
        copy.wait()


def pack_kernel(k_hbm, v_hbm, cells, text_k, text_v, stale, ends, text, sems):
    tokens, shard = k_hbm.shape[0], text_k.shape[0]
    copies = []
    for which, source in enumerate((text_k, text_v)):
        copies.append((source, text.at[pl.ds(which * shard, shard)]))
    for which, source in enumerate((k_hbm, v_hbm)):
        copies.append((source, stale.at[pl.ds(which * tokens, tokens)]))
    for which, at in enumerate((0, cells.shape[0] - 1)):
        copies.append((cells.at[at], ends.at[pl.ds(which * cells.shape[1], cells.shape[1])]))
    run_copies(copies, sems)


def offer_kernel(reads_ref, text, ends_mate, out):
    both, width = text.shape
    count = ends_mate.shape[0] // 2
    row = lax.axis_index("rows")
    partner = (row + 2) % 4

    def flag(owner):
        found = 0
        for turn in range(2):
            entry = reads_ref[0, 0, turn]
            found = jnp.where(entry // 2 == owner, entry % 2, found)
        return jnp.full((8, width // 2), found.astype(jnp.float32), jnp.float32)

    flags = [flag(owner) for owner in (partner, partner + 1 - 2 * (partner % 2))]
    out[pl.ds(0, both), :] = text[...]
    out[pl.ds(both, count), :] = jnp.where(
        row % 2 == 0, ends_mate[pl.ds(count, count), :], ends_mate[pl.ds(0, count), :]
    )
    out[pl.ds(both + count, 8), :] = jnp.concatenate(flags, axis=1).astype(out.dtype)


def send_kernel(across, stale, passed, *outs):
    tokens, width = stale.shape[0] // 2, stale.shape[1]

    def block_of(slot):
        lanes = pl.ds(slot * (width // 2), HEAD_DIM)
        flag = jnp.max(across[pl.ds(across.shape[0] - 8, 8), lanes].astype(jnp.float32))
        return jnp.where(flag > 0.5, PER_BLOCK, 0)

    starts = block_of(0), block_of(1)
    first = 0
    for out in outs:
        part = pl.ds(first, out.shape[1])
        first += out.shape[1]
        for which in range(2):
            for slot, source in enumerate((stale, passed)):
                rows = pl.ds(pl.multiple_of(which * tokens + starts[slot], PER_BLOCK), PER_BLOCK)
                at = (2 * which + slot) * PER_BLOCK
                out[pl.ds(at, PER_BLOCK), :] = source[rows, part]


def bundle_kernel(*refs):
    out = refs[-1]
    at = 0
    for ref in refs[:-1]:
        out[pl.ds(at, ref.shape[0]), :] = ref[...]
        at += ref.shape[0]


def split_kernel(source, first, second):
    half = first.shape[0]
    first[...] = source[pl.ds(0, half), :]
    second[...] = source[pl.ds(half, half), :]


def above_below(ends_mate, across, part):
    count = ends_mate.shape[0] // 2
    row = lax.axis_index("rows")
    beside_first, beside_last = (ends_mate[pl.ds(at, count), part] for at in (0, count))
    passed = across[pl.ds(across.shape[0] - 8 - count, count), part]
    passed = jnp.where((row > 0) & (row < 3), passed, jnp.zeros_like(passed))
    first_core = row % 2 == 0
    return (
        jnp.where(first_core, passed, beside_last),
        jnp.where(first_core, beside_first, passed),
    )


def join_kernel(text, across, cells, ends_mate, both, plus, minus):
    shard = text.shape[0] // 2
    rows_here, cols_here, width = cells.shape
    above, below = above_below(ends_mate, across, slice(None))
    rows = [above] + [cells[i] for i in range(rows_here)] + [below]
    rows = [row.astype(jnp.float32) for row in rows]
    spare = jnp.zeros((16 - len(rows), width), jnp.float32)
    both[pl.ds(0, 2 * shard), :] = text[...]
    both[pl.ds(2 * shard, 2 * shard), :] = across[pl.ds(0, 2 * shard), :]
    for target in (plus, minus):
        target[pl.ds(0, 2 * shard), :] = across[pl.ds(0, 2 * shard), :]
    for target, at in ((plus, cols_here - 1), (minus, 0)):
        edge = jnp.concatenate([row[at : at + 1] for row in rows] + [spare], axis=0)
        target[pl.ds(2 * shard, 16), :] = edge.astype(target.dtype)


def term_kernel(cells, ends_mate, across, left, right, weights, out):
    rows_here, cols_here, width = cells.shape
    col = lax.axis_index("cols")
    edges = pl.ds(left.shape[0] - 16, 16)
    place = lax.broadcasted_iota(jnp.int32, (cols_here, HEAD_DIM), 0)
    for lane in range(width // HEAD_DIM):
        part = pl.ds(lane * HEAD_DIM, HEAD_DIM)
        above, below = above_below(ends_mate, across, part)
        lefts = left[edges, part].astype(jnp.float32)
        rights = right[edges, part].astype(jnp.float32)
        lefts = jnp.where(col > 0, lefts, 0.0)
        rights = jnp.where(col < 3, rights, 0.0)
        taps = []
        for row in range(rows_here + 2):
            if row == 0:
                centre = above
            elif row == rows_here + 1:
                centre = below
            else:
                centre = cells[row - 1, :, part]
            centre = centre.astype(jnp.float32)
            before = jnp.where(place == 0, lefts[row : row + 1], pltpu.roll(centre, 1, 0))
            after = jnp.where(
                place == cols_here - 1, rights[row : row + 1], pltpu.roll(centre, cols_here - 1, 0)
            )
            taps.append((before, centre, after))
        for row in range(rows_here):
            total = None
            for row_tap in range(3):
                for col_tap in range(3):
                    piece = weights[row_tap, col_tap : col_tap + 1, part] * taps[row + row_tap][col_tap]
                    total = piece if total is None else total + piece
            out[pl.ds(row * cols_here, cols_here), part] = total


def attend_kernel(first_head, reads_ref, pattern_ref, text_ref, q, k, v, *refs):
    passed, arrived, term = refs[:3]
    early, early_mate, late, late_mate = refs[3], refs[4], refs[5:9], refs[9:13]
    out = refs[-1]
    row, col = lax.axis_index("rows"), lax.axis_index("cols")
    across, core = row // 2, row % 2
    shard = early.shape[0] // 8
    half = 2 * PER_BLOCK
    head_count = arrived.shape[1] // HEAD_DIM

    def lanes(head):
        return pl.ds((first_head + head) * HEAD_DIM, HEAD_DIM)

    def text_part(chosen, head, which):
        from_own = chosen % 2 == core
        from_near = chosen // 2 == across
        part = lanes(head)

        def one(piece):
            def pick(own, other, at):
                rows = pl.ds((2 * at + which) * shard, shard)
                return jnp.where(from_own, own[rows, part], other[rows, part])

            near_at, side_at = ((2, 3), (0, None), (1, None), (None, None))[piece]
            return jnp.where(
                from_near,
                pick(late[0], late_mate[0], 0)
                if near_at is None
                else pick(early, early_mate, near_at),
                pick(late[piece], late_mate[piece], 0)
                if side_at is None
                else pick(early, early_mate, side_at),
            )

        return [one(piece) for piece in range(4)]

    def far_part(block, head, which):
        slot = pattern_ref[block, 0, 0] + pattern_ref[block, 0, 1] - block - 2
        wanted = reads_ref[0, 0, slot]
        owner = wanted // 2
        mate_at = (wanted % 2) * PER_BLOCK + which * half
        far_at = jnp.where(owner % 2 == core, 0, PER_BLOCK) + which * half
        mate = passed[pl.ds(pl.multiple_of(mate_at, PER_BLOCK), PER_BLOCK), lanes(head)]
        here = pl.ds(head * HEAD_DIM, HEAD_DIM)
        far = arrived[pl.ds(pl.multiple_of(far_at, PER_BLOCK), PER_BLOCK), here]
        return jnp.where(owner // 2 == across, mate, far)

    def gathered(block, head, which):
        own = (k, v)[which][pl.ds(block * PER_BLOCK, PER_BLOCK), lanes(head)]
        parts = [own]
        for turn in range(2):
            parts += text_part(text_ref[block, 0, turn], head, which)
        return jnp.concatenate(parts + [far_part(block, head, which)], axis=0)

    jobs = [(block, head) for head in range(head_count) for block in range(2)]
    size = -(-len(jobs) // -(-len(jobs) // GROUP))
    for at in range(0, len(jobs), size):
        group = jobs[at : at + size]
        scores = [
            head_scores(
                q[pl.ds(block * PER_BLOCK, PER_BLOCK), lanes(head)], gathered(block, head, 0)
            )
            for block, head in group
        ]
        peaks = [jnp.max(s, axis=1, keepdims=True) * EXP2_SCALE for s in scores]
        weights = [
            jnp.exp2(s * EXP2_SCALE - peak).astype(jnp.bfloat16) for s, peak in zip(scores, peaks)
        ]
        totals = [jnp.sum(w.astype(jnp.float32), axis=1, keepdims=True) for w in weights]
        products = [
            jnp.dot(w, gathered(block, head, 1), preferred_element_type=jnp.float32)
            for w, (block, head) in zip(weights, group)
        ]
        for product, total, (block, head) in zip(products, totals, group):
            rows = pl.ds(block * PER_BLOCK, PER_BLOCK)
            out[rows, pl.ds(head * HEAD_DIM, HEAD_DIM)] = product / total + term[rows, lanes(head)]


def body(
    q_fresh, k_fresh, v_fresh, k_stale, v_stale, text_k, text_v, conv_w, reads, pattern, text_blocks
):
    rows_here, cols_here, width = q_fresh.shape
    tokens = rows_here * cols_here
    shard = text_k.shape[0]
    swap = [(r, (r + 2) % 4) for r in range(4)]
    mates = [(r, r ^ 1) for r in range(4)]
    in_vmem = pl.BlockSpec(memory_space=pltpu.VMEM)
    in_hbm = pl.BlockSpec(memory_space=pltpu.HBM)
    params = pltpu.CompilerParams(vmem_limit_bytes=VMEM_LIMIT)
    cost = pl.CostEstimate(flops=1 << 20, transcendentals=0, bytes_accessed=1 << 16)

    def after(value, *others):
        return lax.optimization_barrier((value, *others))[0]

    def flat(grid_values):
        return grid_values.reshape(tokens, width)

    def to_mate(values):
        return lax.ppermute(values, "rows", mates)

    def rows_of(*counts):
        shapes = tuple(jax.ShapeDtypeStruct((n, width), jnp.bfloat16) for n in counts)
        return shapes if len(shapes) > 1 else shapes[0]

    def local(kernel, name, shapes, *args, specs=None, scratch=()):
        many = isinstance(shapes, tuple)
        return pl.pallas_call(
            kernel,
            out_shape=shapes,
            in_specs=specs or [in_vmem] * len(args),
            out_specs=(in_vmem,) * len(shapes) if many else in_vmem,
            scratch_shapes=scratch,
            compiler_params=params,
            cost_estimate=cost,
            name=name,
        )(*args)

    chunks = tuple(
        jax.ShapeDtypeStruct((2 * tokens, n * HEAD_DIM), jnp.bfloat16) for n in CHUNK_HEADS
    )
    in_place = [
        pltpu.with_memory_space_constraint(value, pltpu.HBM)
        for value in (flat(k_stale), flat(v_stale), v_fresh, text_k, text_v)
    ]
    stale, ends, text = local(
        pack_kernel,
        "pack",
        rows_of(2 * tokens, 2 * cols_here, 2 * shard),
        *in_place,
        specs=[in_hbm] * 5,
        scratch=[pltpu.SemaphoreType.DMA((6,))],
    )
    forward = [(i, (i + 1) % 4) for i in range(4)]
    backward = [(i, (i + 3) % 4) for i in range(4)]
    opposite = [(i, (i + 2) % 4) for i in range(4)]

    near_parts = [lax.ppermute(text, "cols", p) for p in (forward, backward)]
    ends_mate = to_mate(ends)
    offer = local(
        offer_kernel,
        "offer",
        rows_of(2 * shard + cols_here + 8),
        reads,
        text,
        ends_mate,
        specs=[pl.BlockSpec(memory_space=pltpu.SMEM)] + [in_vmem] * 2,
    )
    across = lax.ppermute(offer, "rows", swap)
    passed = to_mate(after(stale, ends_mate))
    packed = local(
        send_kernel, "send", chunks, across, stale, passed
    )
    far = [lax.ppermute(chunk, "rows", swap) for chunk in packed]

    both, plus, minus = local(
        join_kernel,
        "join",
        rows_of(4 * shard, 2 * shard + 16, 2 * shard + 16),
        text,
        after(across, packed[0]),
        v_fresh,
        ends_mate,
    )
    left = lax.ppermute(plus, "cols", forward)
    right = lax.ppermute(minus, "cols", backward)
    across_cols = lax.ppermute(both, "cols", opposite)
    early = local(bundle_kernel, "bundle", rows_of(8 * shard), *near_parts, both)
    early_mate = to_mate(early)
    across_cols = after(across_cols, early_mate)
    far_side = local(split_kernel, "split", rows_of(2 * shard, 2 * shard), across_cols)
    late = [far_side[0], left, right, far_side[1]]
    late_mate = [to_mate(part) for part in late]
    term = local(
        term_kernel,
        "term",
        jax.ShapeDtypeStruct((tokens, width), jnp.float32),
        v_fresh, ends_mate, across, left, right, conv_w,
    )

    out = None
    first_head = 0
    for chunk, head_count in enumerate(CHUNK_HEADS):
        if out is not None:
            far[chunk] = after(far[chunk], out)
        block = pl.BlockSpec(
            (pl.Element(tokens), pl.Element(head_count * HEAD_DIM)),
            lambda i, *_, at=first_head * HEAD_DIM: (0, at),
        )
        out = pl.pallas_call(
            functools.partial(attend_kernel, first_head),
            out_shape=jax.ShapeDtypeStruct((tokens, width), jnp.float32),
            grid_spec=pltpu.PrefetchScalarGridSpec(
                num_scalar_prefetch=3,
                grid=(1,),
                in_specs=[in_vmem] * 16 + [in_hbm] * (out is not None),
                out_specs=block,
            ),
            input_output_aliases={19: 0} if out is not None else {},
            compiler_params=params,
            cost_estimate=cost,
            name=f"attend{chunk}",
        )(
            reads, pattern, text_blocks, flat(q_fresh), flat(k_fresh), flat(v_fresh),
            passed, far[chunk], term, early, early_mate, *late, *late_mate,
            *([out] if out is not None else []),
        )
        first_head += head_count
    return out.reshape(rows_here, cols_here, width)


def fits(mesh, reads, pattern, text_k):
    sizes = dict(mesh.shape)
    return (
        sizes["rows"] == 4
        and sizes["cols"] == 4
        and reads.shape[-1] == 2
        and pattern.shape[-1] == 2
        and pattern.shape[0] == 2 * sizes["groups"] * 4
        and text_k.shape[0] == sizes["groups"] * 4 * PER_BLOCK
    )


def solution(mesh):
    grid = P(("groups", "rows"), "cols", None)
    text = P(("groups", "rows", "cols"), None)
    in_specs = (grid, grid, grid, grid, grid, text, text, P(), grid, grid, grid)

    def program(*args):
        chosen = body if fits(mesh, args[8], args[9], args[5]) else general_body
        return jax.shard_map(
            chosen, mesh=mesh, in_specs=in_specs, out_specs=grid, check_vma=False
        )(*args)

    return program
```

```python
import functools
import math

import jax
import jax.numpy as jnp
from jax import lax
from jax.experimental import pallas as pl
from jax.experimental.pallas import tpu as pltpu
from jax.sharding import PartitionSpec as P

HEAD_DIM = 128
BLOCK_ROWS = 4
BLOCK_COLS = 32
PER_BLOCK = BLOCK_ROWS * BLOCK_COLS
SCORE_SCALE = 1.0 / math.sqrt(HEAD_DIM)
EXP2_SCALE = SCORE_SCALE * math.log2(math.e)
CHUNK_HEADS = (9, 3)
GROUP = 8
VMEM_LIMIT = 24 * 1024 * 1024


def extended(cells, sides, width):
    for axis, dim in sides:
        count = lax.axis_size(axis)
        ends = count - 1
        head = lax.slice_in_dim(cells, 0, width, axis=dim)
        tail = lax.slice_in_dim(cells, cells.shape[dim] - width, cells.shape[dim], axis=dim)
        cells = jnp.concatenate(
            [
                lax.ppermute(tail, axis, [(i, (i + 1) % count) for i in range(ends)]),
                cells,
                lax.ppermute(head, axis, [((i + 1) % count, i) for i in range(ends)]),
            ],
            axis=dim,
        )
    return cells


def position(v_fresh, conv_w):
    rows_here, cols_here, feature_width = v_fresh.shape
    rims = extended(v_fresh, (("rows", 0), ("cols", 1)), 1)
    position_term = jnp.zeros((rows_here, cols_here, feature_width), jnp.float32)
    for row_tap in range(3):
        for col_tap in range(3):
            position_term = position_term + conv_w[row_tap, col_tap] * rims[
                row_tap : row_tap + rows_here, col_tap : col_tap + cols_here
            ].astype(jnp.float32)
    return position_term


def split_heads(flat_rows):
    return flat_rows.reshape(flat_rows.shape[:-1] + (flat_rows.shape[-1] // HEAD_DIM, HEAD_DIM))


def attend(softmax_state, queries, key_blocks, value_blocks, allowed):
    old_peak, old_total, old_summed = softmax_state
    scores = (
        jnp.einsum(
            "bqhd,nkhd->bhqnk", queries, key_blocks, preferred_element_type=jnp.float32
        )
        * SCORE_SCALE
    )
    scores = jnp.where(allowed[:, None, None, :, None], scores, -1e30)
    new_peak = jnp.maximum(old_peak, jnp.max(scores, axis=(3, 4)))
    weights = jnp.exp(scores - new_peak[:, :, :, None, None]).astype(jnp.bfloat16)
    factor = jnp.exp(old_peak - new_peak)
    new_total = old_total * factor + jnp.sum(weights.astype(jnp.float32), axis=(3, 4))
    product = jnp.einsum(
        "bhqnk,nkhd->bqhd", weights, value_blocks, preferred_element_type=jnp.float32
    )
    new_summed = old_summed * jnp.transpose(factor, (0, 2, 1))[:, :, :, None] + product
    return (new_peak, new_total, new_summed)


def general_body(
    q_fresh, k_fresh, v_fresh, k_stale, v_stale, text_k, text_v, conv_w, reads, pattern, text_blocks
):
    rows_here, cols_here, feature_width = q_fresh.shape
    blocks_here = rows_here // BLOCK_ROWS
    head_count = feature_width // HEAD_DIM

    def as_blocks(grid_values):
        return split_heads(grid_values.reshape(blocks_here, PER_BLOCK, feature_width))

    queries = as_blocks(q_fresh)
    text_keys, text_values = (
        lax.all_gather(text_k, ("rows", "cols"), axis=0, tiled=True),
        lax.all_gather(text_v, ("rows", "cols"), axis=0, tiled=True),
    )
    text_count = text_keys.shape[0] // PER_BLOCK
    text_keys = split_heads(text_keys.reshape(text_count, PER_BLOCK, feature_width))
    text_values = split_heads(text_values.reshape(text_count, PER_BLOCK, feature_width))
    wanted = pattern[:, 0, :]
    fetch_rows = reads[0, 0, :]
    fetch_count = fetch_rows.shape[0]
    slot_count = blocks_here + fetch_count
    slot_mask = jnp.any(
        wanted[:, :, None] == jnp.arange(slot_count, dtype=jnp.int32)[None, None, :], axis=1
    )
    text_mask = jnp.any(
        text_blocks[:, 0, :, None] == jnp.arange(text_count, dtype=jnp.int32)[None, None, :], axis=1
    )
    softmax_state = (
        jnp.full((blocks_here, head_count, PER_BLOCK), -1e30, jnp.float32),
        jnp.zeros((blocks_here, head_count, PER_BLOCK), jnp.float32),
        jnp.zeros((blocks_here, PER_BLOCK, head_count, HEAD_DIM), jnp.float32),
    )
    softmax_state = attend(
        softmax_state,
        queries,
        jnp.concatenate([as_blocks(k_fresh), text_keys], axis=0),
        jnp.concatenate([as_blocks(v_fresh), text_values], axis=0),
        jnp.concatenate([slot_mask[:, :blocks_here], text_mask], axis=1),
    )
    chosen = jnp.where(
        wanted >= blocks_here, fetch_rows[jnp.clip(wanted - blocks_here, 0, fetch_count - 1)], -1
    )
    piece_keys = lax.all_gather(as_blocks(k_stale), "rows", axis=0, tiled=True)
    piece_values = lax.all_gather(as_blocks(v_stale), "rows", axis=0, tiled=True)
    block_rows = jnp.arange(piece_keys.shape[0], dtype=jnp.int32)
    piece_mask = jnp.any(chosen[:, :, None] == block_rows[None, None, :], axis=1)
    softmax_state = attend(softmax_state, queries, piece_keys, piece_values, piece_mask)
    _, final_total, final_summed = softmax_state
    mixed_rows = final_summed / jnp.transpose(final_total, (0, 2, 1))[:, :, :, None]
    attention = mixed_rows.reshape(rows_here, cols_here, feature_width)
    return attention + position(v_fresh, conv_w)


def head_scores(queries, keys):
    return lax.dot_general(
        queries, keys, (((1,), (1,)), ((), ())), preferred_element_type=jnp.float32
    )


def run_copies(copies, sems):
    copies = [pltpu.make_async_copy(*pair, sems.at[i]) for i, pair in enumerate(copies)]
    for copy in copies:
        copy.start()
    for copy in copies:
        copy.wait()


def pack_kernel(k_hbm, v_hbm, cells, text_k, text_v, stale, beside, diagonal, text, sems):
    tokens, shard = k_hbm.shape[0], text_k.shape[0]
    row = lax.axis_index("rows")
    end = cells.shape[0] - 1
    copies = []
    for which, source in enumerate((text_k, text_v)):
        copies.append((source, text.at[pl.ds(which * shard, shard)]))
    for which, source in enumerate((k_hbm, v_hbm)):
        copies.append((source, stale.at[pl.ds(which * tokens, tokens)]))
    copies.append((cells.at[jnp.where(row % 2 == 0, end, 0)], beside))
    copies.append((cells.at[jnp.where(row < 2, end, 0)], diagonal))
    run_copies(copies, sems)


def offer_kernel(reads_ref, text, out):
    both, width = text.shape
    partner = (lax.axis_index("rows") + 2) % 4

    def flag(owner):
        found = 0
        for turn in range(2):
            entry = reads_ref[0, 0, turn]
            found = jnp.where(entry // 2 == owner, entry % 2, found)
        return jnp.full((8, width // 2), found.astype(jnp.float32), jnp.float32)

    flags = [flag(owner) for owner in (partner, partner + 1 - 2 * (partner % 2))]
    out[pl.ds(0, both), :] = text[...]
    out[pl.ds(both, 8), :] = jnp.concatenate(flags, axis=1).astype(out.dtype)


def send_kernel(across, stale, passed, *outs):
    tokens, width = stale.shape[0] // 2, stale.shape[1]

    def block_of(slot):
        lanes = pl.ds(slot * (width // 2), HEAD_DIM)
        flag = jnp.max(across[pl.ds(across.shape[0] - 8, 8), lanes].astype(jnp.float32))
        return jnp.where(flag > 0.5, PER_BLOCK, 0)

    starts = block_of(0), block_of(1)
    first = 0
    for out in outs:
        part = pl.ds(first, out.shape[1])
        first += out.shape[1]
        for which in range(2):
            for slot, source in enumerate((stale, passed)):
                rows = pl.ds(pl.multiple_of(which * tokens + starts[slot], PER_BLOCK), PER_BLOCK)
                at = (2 * which + slot) * PER_BLOCK
                out[pl.ds(at, PER_BLOCK), :] = source[rows, part]


def bundle_kernel(*refs):
    out = refs[-1]
    at = 0
    for ref in refs[:-1]:
        count = ref.shape[0] - ref.shape[0] % 64
        out[pl.ds(at, count), :] = ref[pl.ds(0, count), :]
        at += count


def choose_kernel(upper, lower, first, second):
    upwards = lax.axis_index("cols") >= 2
    half = first.shape[0]
    for at, out in ((0, first), (half, second)):
        rows = pl.ds(at, half)
        out[...] = jnp.where(upwards, upper[rows, :], lower[rows, :])


def above_below(beside, diagonal):
    first_core = lax.axis_index("rows") % 2 == 0
    return (
        jnp.where(first_core, diagonal, beside),
        jnp.where(first_core, beside, diagonal),
    )


def join_kernel(text, across, cells, beside, diagonal, both, plus, minus):
    shard = text.shape[0] // 2
    rows_here, cols_here, width = cells.shape
    above, below = above_below(beside[...], diagonal[...])
    rows = [above] + [cells[i] for i in range(rows_here)] + [below]
    rows = [row.astype(jnp.float32) for row in rows]
    spare = jnp.zeros((16 - len(rows), width), jnp.float32)
    both[pl.ds(0, 2 * shard), :] = text[...]
    both[pl.ds(2 * shard, 2 * shard), :] = across[pl.ds(0, 2 * shard), :]
    for target in (plus, minus):
        target[pl.ds(0, 2 * shard), :] = across[pl.ds(0, 2 * shard), :]
    for target, at in ((plus, cols_here - 1), (minus, 0)):
        edge = jnp.concatenate([row[at : at + 1] for row in rows] + [spare], axis=0)
        target[pl.ds(2 * shard, 16), :] = edge.astype(target.dtype)


def term_kernel(cells, beside, diagonal, left, right, weights, out):
    rows_here, cols_here, width = cells.shape
    col = lax.axis_index("cols")
    edges = pl.ds(left.shape[0] - 16, 16)
    place = lax.broadcasted_iota(jnp.int32, (cols_here, HEAD_DIM), 0)
    for lane in range(width // HEAD_DIM):
        part = pl.ds(lane * HEAD_DIM, HEAD_DIM)
        above, below = above_below(beside[:, part], diagonal[:, part])
        lefts = left[edges, part].astype(jnp.float32)
        rights = right[edges, part].astype(jnp.float32)
        lefts = jnp.where(col > 0, lefts, 0.0)
        rights = jnp.where(col < 3, rights, 0.0)
        taps = []
        for row in range(rows_here + 2):
            if row == 0:
                centre = above
            elif row == rows_here + 1:
                centre = below
            else:
                centre = cells[row - 1, :, part]
            centre = centre.astype(jnp.float32)
            before = jnp.where(place == 0, lefts[row : row + 1], pltpu.roll(centre, 1, 0))
            after = jnp.where(
                place == cols_here - 1, rights[row : row + 1], pltpu.roll(centre, cols_here - 1, 0)
            )
            taps.append((before, centre, after))
        for row in range(rows_here):
            total = None
            for row_tap in range(3):
                for col_tap in range(3):
                    piece = weights[row_tap, col_tap : col_tap + 1, part] * taps[row + row_tap][col_tap]
                    total = piece if total is None else total + piece
            out[pl.ds(row * cols_here, cols_here), part] = total


def attend_kernel(first_head, reads_ref, pattern_ref, text_ref, q, k, v, *refs):
    passed, arrived, term = refs[:3]
    both, both_mate, early, early_mate = refs[3:7]
    late, late_mate = refs[7:11], refs[11:15]
    out = refs[-1]
    row, col = lax.axis_index("rows"), lax.axis_index("cols")
    across, core = row // 2, row % 2
    shard = both.shape[0] // 4
    half = 2 * PER_BLOCK
    head_count = arrived.shape[1] // HEAD_DIM

    def lanes(head):
        return pl.ds((first_head + head) * HEAD_DIM, HEAD_DIM)

    def text_part(chosen, head, which):
        from_own = chosen % 2 == core
        from_near = chosen // 2 == across
        part = lanes(head)

        def one(piece):
            def pick(own, other, at):
                rows = pl.ds((2 * at + which) * shard, shard)
                return jnp.where(from_own, own[rows, part], other[rows, part])

            if piece == 0:
                near, side = pick(both, both_mate, 0), pick(both, both_mate, 1)
            else:
                side = pick(late[piece], late_mate[piece], 0)
                if piece < 3:
                    near = pick(early, early_mate, piece - 1)
                else:
                    near = pick(late[0], late_mate[0], 0)
            return jnp.where(from_near, near, side)

        return [one(piece) for piece in range(4)]

    def far_part(block, head, which):
        slot = pattern_ref[block, 0, 0] + pattern_ref[block, 0, 1] - block - 2
        wanted = reads_ref[0, 0, slot]
        owner = wanted // 2
        mate_at = (wanted % 2) * PER_BLOCK + which * half
        far_at = jnp.where(owner % 2 == core, 0, PER_BLOCK) + which * half
        mate = passed[pl.ds(pl.multiple_of(mate_at, PER_BLOCK), PER_BLOCK), lanes(head)]
        here = pl.ds(head * HEAD_DIM, HEAD_DIM)
        far = arrived[pl.ds(pl.multiple_of(far_at, PER_BLOCK), PER_BLOCK), here]
        return jnp.where(owner // 2 == across, mate, far)

    def gathered(block, head, which):
        own = (k, v)[which][pl.ds(block * PER_BLOCK, PER_BLOCK), lanes(head)]
        parts = [own]
        for turn in range(2):
            parts += text_part(text_ref[block, 0, turn], head, which)
        return jnp.concatenate(parts + [far_part(block, head, which)], axis=0)

    jobs = [(block, head) for head in range(head_count) for block in range(2)]
    size = -(-len(jobs) // -(-len(jobs) // GROUP))
    for at in range(0, len(jobs), size):
        group = jobs[at : at + size]
        scores = [
            head_scores(
                q[pl.ds(block * PER_BLOCK, PER_BLOCK), lanes(head)], gathered(block, head, 0)
            )
            for block, head in group
        ]
        peaks = [jnp.max(s, axis=1, keepdims=True) * EXP2_SCALE for s in scores]
        weights = [
            jnp.exp2(s * EXP2_SCALE - peak).astype(jnp.bfloat16) for s, peak in zip(scores, peaks)
        ]
        totals = [jnp.sum(w.astype(jnp.float32), axis=1, keepdims=True) for w in weights]
        products = [
            jnp.dot(w, gathered(block, head, 1), preferred_element_type=jnp.float32)
            for w, (block, head) in zip(weights, group)
        ]
        for product, total, (block, head) in zip(products, totals, group):
            rows = pl.ds(block * PER_BLOCK, PER_BLOCK)
            out[rows, pl.ds(head * HEAD_DIM, HEAD_DIM)] = product / total + term[rows, lanes(head)]


def body(
    q_fresh, k_fresh, v_fresh, k_stale, v_stale, text_k, text_v, conv_w, reads, pattern, text_blocks
):
    rows_here, cols_here, width = q_fresh.shape
    tokens = rows_here * cols_here
    shard = text_k.shape[0]
    swap = [(r, (r + 2) % 4) for r in range(4)]
    mates = [(r, r ^ 1) for r in range(4)]
    in_vmem = pl.BlockSpec(memory_space=pltpu.VMEM)
    in_hbm = pl.BlockSpec(memory_space=pltpu.HBM)
    params = pltpu.CompilerParams(vmem_limit_bytes=VMEM_LIMIT)
    cost = pl.CostEstimate(flops=1 << 20, transcendentals=0, bytes_accessed=1 << 16)

    def after(value, *others):
        return lax.optimization_barrier((value, *others))[0]

    def flat(grid_values):
        return grid_values.reshape(tokens, width)

    def to_mate(values):
        return lax.ppermute(values, "rows", mates)

    def rows_of(*counts):
        shapes = tuple(jax.ShapeDtypeStruct((n, width), jnp.bfloat16) for n in counts)
        return shapes if len(shapes) > 1 else shapes[0]

    def local(kernel, name, shapes, *args, specs=None, scratch=()):
        many = isinstance(shapes, tuple)
        return pl.pallas_call(
            kernel,
            out_shape=shapes,
            in_specs=specs or [in_vmem] * len(args),
            out_specs=(in_vmem,) * len(shapes) if many else in_vmem,
            scratch_shapes=scratch,
            compiler_params=params,
            cost_estimate=cost,
            name=name,
        )(*args)

    chunks = tuple(
        jax.ShapeDtypeStruct((2 * tokens, n * HEAD_DIM), jnp.bfloat16) for n in CHUNK_HEADS
    )
    in_place = [
        pltpu.with_memory_space_constraint(value, pltpu.HBM)
        for value in (flat(k_stale), flat(v_stale), v_fresh, text_k, text_v)
    ]
    stale, beside, diagonal, text = local(
        pack_kernel,
        "pack",
        rows_of(2 * tokens, cols_here, cols_here, 2 * shard),
        *in_place,
        specs=[in_hbm] * 5,
        scratch=[pltpu.SemaphoreType.DMA((6,))],
    )
    forward = [(i, (i + 1) % 4) for i in range(4)]
    backward = [(i, (i + 3) % 4) for i in range(4)]

    near_parts = [lax.ppermute(text, "cols", p) for p in (forward, backward)]
    beside = to_mate(beside)
    diagonal = lax.ppermute(diagonal, "rows", [(1, 2), (2, 1)])
    offer = local(
        offer_kernel,
        "offer",
        rows_of(2 * shard + 8),
        reads,
        text,
        specs=[pl.BlockSpec(memory_space=pltpu.SMEM), in_vmem],
    )
    across = lax.ppermute(offer, "rows", swap)
    passed = to_mate(after(stale, beside))
    packed = local(
        send_kernel, "send", chunks, after(across, diagonal), stale, passed
    )
    far = [lax.ppermute(chunk, "rows", swap) for chunk in packed]

    both, plus, minus = local(
        join_kernel,
        "join",
        rows_of(4 * shard, 2 * shard + 16, 2 * shard + 16),
        text,
        after(across, packed[0]),
        v_fresh,
        beside,
        diagonal,
    )
    left = lax.ppermute(plus, "cols", forward)
    right = lax.ppermute(minus, "cols", backward)
    early = local(bundle_kernel, "bundle", rows_of(4 * shard), *near_parts)
    early_mate, both_mate = to_mate(early), to_mate(both)
    near_parts[0] = after(near_parts[0], early_mate, both_mate)
    upper, lower = (
        local(bundle_kernel, "pair", rows_of(4 * shard), *pair)
        for pair in ((near_parts[0], left), (near_parts[1], right))
    )
    upper = lax.ppermute(upper, "cols", [(1, 2), (2, 3)])
    lower = lax.ppermute(lower, "cols", [(1, 0), (2, 1)])
    far_side = local(choose_kernel, "choose", rows_of(2 * shard, 2 * shard), upper, lower)
    late = [far_side[0], left, right, far_side[1]]
    late_mate = [to_mate(part) for part in late]
    term = local(
        term_kernel,
        "term",
        jax.ShapeDtypeStruct((tokens, width), jnp.float32),
        v_fresh, beside, diagonal, left, right, conv_w,
    )

    out = None
    first_head = 0
    for chunk, head_count in enumerate(CHUNK_HEADS):
        if out is not None:
            far[chunk] = after(far[chunk], out)
        block = pl.BlockSpec(
            (pl.Element(tokens), pl.Element(head_count * HEAD_DIM)),
            lambda i, *_, at=first_head * HEAD_DIM: (0, at),
        )
        out = pl.pallas_call(
            functools.partial(attend_kernel, first_head),
            out_shape=jax.ShapeDtypeStruct((tokens, width), jnp.float32),
            grid_spec=pltpu.PrefetchScalarGridSpec(
                num_scalar_prefetch=3,
                grid=(1,),
                in_specs=[in_vmem] * 18 + [in_hbm] * (out is not None),
                out_specs=block,
            ),
            input_output_aliases={21: 0} if out is not None else {},
            compiler_params=params,
            cost_estimate=cost,
            name=f"attend{chunk}",
        )(
            reads, pattern, text_blocks, flat(q_fresh), flat(k_fresh), flat(v_fresh),
            passed, far[chunk], term, both, both_mate, early, early_mate, *late, *late_mate,
            *([out] if out is not None else []),
        )
        first_head += head_count
    return out.reshape(rows_here, cols_here, width)


def fits(mesh, reads, pattern, text_k):
    sizes = dict(mesh.shape)
    return (
        sizes["rows"] == 4
        and sizes["cols"] == 4
        and reads.shape[-1] == 2
        and pattern.shape[-1] == 2
        and pattern.shape[0] == 2 * sizes["groups"] * 4
        and text_k.shape[0] == sizes["groups"] * 4 * PER_BLOCK
    )


def solution(mesh):
    grid = P(("groups", "rows"), "cols", None)
    text = P(("groups", "rows", "cols"), None)
    in_specs = (grid, grid, grid, grid, grid, text, text, P(), grid, grid, grid)

    def program(*args):
        chosen = body if fits(mesh, args[8], args[9], args[5]) else general_body
        return jax.shard_map(
            chosen, mesh=mesh, in_specs=in_specs, out_specs=grid, check_vma=False
        )(*args)

    return program
```

```python
import functools
import math

import jax
import jax.numpy as jnp
from jax import lax
from jax.experimental import pallas as pl
from jax.experimental.pallas import tpu as pltpu
from jax.sharding import PartitionSpec as P

HEAD_DIM = 128
BLOCK_ROWS = 4
BLOCK_COLS = 32
PER_BLOCK = BLOCK_ROWS * BLOCK_COLS
SCORE_SCALE = 1.0 / math.sqrt(HEAD_DIM)
EXP2_SCALE = SCORE_SCALE * math.log2(math.e)
CHUNK_HEADS = (9, 3)
GROUP = 8
VMEM_LIMIT = 24 * 1024 * 1024


def extended(cells, sides, width):
    for axis, dim in sides:
        count = lax.axis_size(axis)
        ends = count - 1
        head = lax.slice_in_dim(cells, 0, width, axis=dim)
        tail = lax.slice_in_dim(cells, cells.shape[dim] - width, cells.shape[dim], axis=dim)
        cells = jnp.concatenate(
            [
                lax.ppermute(tail, axis, [(i, (i + 1) % count) for i in range(ends)]),
                cells,
                lax.ppermute(head, axis, [((i + 1) % count, i) for i in range(ends)]),
            ],
            axis=dim,
        )
    return cells


def position(v_fresh, conv_w):
    rows_here, cols_here, feature_width = v_fresh.shape
    rims = extended(v_fresh, (("rows", 0), ("cols", 1)), 1)
    position_term = jnp.zeros((rows_here, cols_here, feature_width), jnp.float32)
    for row_tap in range(3):
        for col_tap in range(3):
            position_term = position_term + conv_w[row_tap, col_tap] * rims[
                row_tap : row_tap + rows_here, col_tap : col_tap + cols_here
            ].astype(jnp.float32)
    return position_term


def split_heads(flat_rows):
    return flat_rows.reshape(flat_rows.shape[:-1] + (flat_rows.shape[-1] // HEAD_DIM, HEAD_DIM))


def attend(softmax_state, queries, key_blocks, value_blocks, allowed):
    old_peak, old_total, old_summed = softmax_state
    scores = (
        jnp.einsum(
            "bqhd,nkhd->bhqnk", queries, key_blocks, preferred_element_type=jnp.float32
        )
        * SCORE_SCALE
    )
    scores = jnp.where(allowed[:, None, None, :, None], scores, -1e30)
    new_peak = jnp.maximum(old_peak, jnp.max(scores, axis=(3, 4)))
    weights = jnp.exp(scores - new_peak[:, :, :, None, None]).astype(jnp.bfloat16)
    factor = jnp.exp(old_peak - new_peak)
    new_total = old_total * factor + jnp.sum(weights.astype(jnp.float32), axis=(3, 4))
    product = jnp.einsum(
        "bhqnk,nkhd->bqhd", weights, value_blocks, preferred_element_type=jnp.float32
    )
    new_summed = old_summed * jnp.transpose(factor, (0, 2, 1))[:, :, :, None] + product
    return (new_peak, new_total, new_summed)


def general_body(
    q_fresh, k_fresh, v_fresh, k_stale, v_stale, text_k, text_v, conv_w, reads, pattern, text_blocks
):
    rows_here, cols_here, feature_width = q_fresh.shape
    blocks_here = rows_here // BLOCK_ROWS
    head_count = feature_width // HEAD_DIM

    def as_blocks(grid_values):
        return split_heads(grid_values.reshape(blocks_here, PER_BLOCK, feature_width))

    queries = as_blocks(q_fresh)
    text_keys, text_values = (
        lax.all_gather(text_k, ("rows", "cols"), axis=0, tiled=True),
        lax.all_gather(text_v, ("rows", "cols"), axis=0, tiled=True),
    )
    text_count = text_keys.shape[0] // PER_BLOCK
    text_keys = split_heads(text_keys.reshape(text_count, PER_BLOCK, feature_width))
    text_values = split_heads(text_values.reshape(text_count, PER_BLOCK, feature_width))
    wanted = pattern[:, 0, :]
    fetch_rows = reads[0, 0, :]
    fetch_count = fetch_rows.shape[0]
    slot_count = blocks_here + fetch_count
    slot_mask = jnp.any(
        wanted[:, :, None] == jnp.arange(slot_count, dtype=jnp.int32)[None, None, :], axis=1
    )
    text_mask = jnp.any(
        text_blocks[:, 0, :, None] == jnp.arange(text_count, dtype=jnp.int32)[None, None, :], axis=1
    )
    softmax_state = (
        jnp.full((blocks_here, head_count, PER_BLOCK), -1e30, jnp.float32),
        jnp.zeros((blocks_here, head_count, PER_BLOCK), jnp.float32),
        jnp.zeros((blocks_here, PER_BLOCK, head_count, HEAD_DIM), jnp.float32),
    )
    softmax_state = attend(
        softmax_state,
        queries,
        jnp.concatenate([as_blocks(k_fresh), text_keys], axis=0),
        jnp.concatenate([as_blocks(v_fresh), text_values], axis=0),
        jnp.concatenate([slot_mask[:, :blocks_here], text_mask], axis=1),
    )
    chosen = jnp.where(
        wanted >= blocks_here, fetch_rows[jnp.clip(wanted - blocks_here, 0, fetch_count - 1)], -1
    )
    piece_keys = lax.all_gather(as_blocks(k_stale), "rows", axis=0, tiled=True)
    piece_values = lax.all_gather(as_blocks(v_stale), "rows", axis=0, tiled=True)
    block_rows = jnp.arange(piece_keys.shape[0], dtype=jnp.int32)
    piece_mask = jnp.any(chosen[:, :, None] == block_rows[None, None, :], axis=1)
    softmax_state = attend(softmax_state, queries, piece_keys, piece_values, piece_mask)
    _, final_total, final_summed = softmax_state
    mixed_rows = final_summed / jnp.transpose(final_total, (0, 2, 1))[:, :, :, None]
    attention = mixed_rows.reshape(rows_here, cols_here, feature_width)
    return attention + position(v_fresh, conv_w)


def head_scores(queries, keys):
    return lax.dot_general(
        queries, keys, (((1,), (1,)), ((), ())), preferred_element_type=jnp.float32
    )


def run_copies(copies, sems):
    copies = [pltpu.make_async_copy(*pair, sems.at[i]) for i, pair in enumerate(copies)]
    for copy in copies:
        copy.start()
    for copy in copies:
        copy.wait()


def pack_kernel(reads_ref, cells, text_k, text_v, offer, beside, diagonal, text, sems):
    shard, width = text_k.shape
    row = lax.axis_index("rows")
    end = cells.shape[0] - 1
    partner = (row + 2) % 4

    def flag(owner):
        found = 0
        for turn in range(2):
            entry = reads_ref[0, 0, turn]
            found = jnp.where(entry // 2 == owner, entry % 2, found)
        return jnp.full((8, width // 2), found.astype(jnp.float32), jnp.float32)

    copies = []
    for which, source in enumerate((text_k, text_v)):
        for target in (text, offer):
            copies.append((source, target.at[pl.ds(which * shard, shard)]))
    copies.append((cells.at[jnp.where(row % 2 == 0, end, 0)], beside))
    copies.append((cells.at[jnp.where(row < 2, end, 0)], diagonal))
    flags = [flag(owner) for owner in (partner, partner + 1 - 2 * (partner % 2))]
    offer[pl.ds(2 * shard, 8), :] = jnp.concatenate(flags, axis=1).astype(offer.dtype)
    run_copies(copies, sems)


def fetch_kernel(k_hbm, v_hbm, text, stale, sems):
    del text
    tokens = k_hbm.shape[0]
    run_copies(
        [
            (source, stale.at[pl.ds(which * tokens, tokens)])
            for which, source in enumerate((k_hbm, v_hbm))
        ],
        sems,
    )


def send_kernel(across, stale, passed, *outs):
    tokens, width = stale.shape[0] // 2, stale.shape[1]

    def block_of(slot):
        lanes = pl.ds(slot * (width // 2), HEAD_DIM)
        flag = jnp.max(across[pl.ds(across.shape[0] - 8, 8), lanes].astype(jnp.float32))
        return jnp.where(flag > 0.5, PER_BLOCK, 0)

    starts = block_of(0), block_of(1)
    first = 0
    for out in outs:
        part = pl.ds(first, out.shape[1])
        first += out.shape[1]
        for which in range(2):
            for slot, source in enumerate((stale, passed)):
                rows = pl.ds(pl.multiple_of(which * tokens + starts[slot], PER_BLOCK), PER_BLOCK)
                at = (2 * which + slot) * PER_BLOCK
                out[pl.ds(at, PER_BLOCK), :] = source[rows, part]


def bundle_kernel(*refs):
    out = refs[-1]
    at = 0
    for ref in refs[:-1]:
        count = ref.shape[0] - ref.shape[0] % 64
        out[pl.ds(at, count), :] = ref[pl.ds(0, count), :]
        at += count


def choose_kernel(upper, lower, first, second):
    upwards = lax.axis_index("cols") >= 2
    half = first.shape[0]
    for at, out in ((0, first), (half, second)):
        rows = pl.ds(at, half)
        out[...] = jnp.where(upwards, upper[rows, :], lower[rows, :])


def above_below(beside, diagonal):
    first_core = lax.axis_index("rows") % 2 == 0
    return (
        jnp.where(first_core, diagonal, beside),
        jnp.where(first_core, beside, diagonal),
    )


def join_kernel(text, across, cells, beside, diagonal, both, plus, minus):
    shard = text.shape[0] // 2
    rows_here, cols_here, width = cells.shape
    above, below = above_below(beside[...], diagonal[...])
    rows = [above] + [cells[i] for i in range(rows_here)] + [below]
    rows = [row.astype(jnp.float32) for row in rows]
    spare = jnp.zeros((16 - len(rows), width), jnp.float32)
    both[pl.ds(0, 2 * shard), :] = text[...]
    both[pl.ds(2 * shard, 2 * shard), :] = across[pl.ds(0, 2 * shard), :]
    for target in (plus, minus):
        target[pl.ds(0, 2 * shard), :] = across[pl.ds(0, 2 * shard), :]
    for target, at in ((plus, cols_here - 1), (minus, 0)):
        edge = jnp.concatenate([row[at : at + 1] for row in rows] + [spare], axis=0)
        target[pl.ds(2 * shard, 16), :] = edge.astype(target.dtype)


def term_kernel(cells, beside, diagonal, left, right, weights, out):
    rows_here, cols_here, width = cells.shape
    col = lax.axis_index("cols")
    edges = pl.ds(left.shape[0] - 16, 16)
    place = lax.broadcasted_iota(jnp.int32, (cols_here, HEAD_DIM), 0)
    for lane in range(width // HEAD_DIM):
        part = pl.ds(lane * HEAD_DIM, HEAD_DIM)
        above, below = above_below(beside[:, part], diagonal[:, part])
        lefts = left[edges, part].astype(jnp.float32)
        rights = right[edges, part].astype(jnp.float32)
        lefts = jnp.where(col > 0, lefts, 0.0)
        rights = jnp.where(col < 3, rights, 0.0)
        taps = []
        for row in range(rows_here + 2):
            if row == 0:
                centre = above
            elif row == rows_here + 1:
                centre = below
            else:
                centre = cells[row - 1, :, part]
            centre = centre.astype(jnp.float32)
            before = jnp.where(place == 0, lefts[row : row + 1], pltpu.roll(centre, 1, 0))
            after = jnp.where(
                place == cols_here - 1, rights[row : row + 1], pltpu.roll(centre, cols_here - 1, 0)
            )
            taps.append((before, centre, after))
        for row in range(rows_here):
            total = None
            for row_tap in range(3):
                for col_tap in range(3):
                    piece = weights[row_tap, col_tap : col_tap + 1, part] * taps[row + row_tap][col_tap]
                    total = piece if total is None else total + piece
            out[pl.ds(row * cols_here, cols_here), part] = total


def grouped(jobs):
    size = -(-len(jobs) // -(-len(jobs) // GROUP))
    return [jobs[at : at + size] for at in range(0, len(jobs), size)]


def lanes_of(head):
    return pl.ds(head * HEAD_DIM, HEAD_DIM)


def rows_at(block):
    return pl.ds(block * PER_BLOCK, PER_BLOCK)


def text_choice(chosen):
    row = lax.axis_index("rows")
    return chosen % 2 == row % 2, chosen // 2 == row // 2


def pick(from_own, own, other, shard, at, part):
    rows = pl.ds(at * shard, shard)
    return jnp.where(from_own, own[rows, part], other[rows, part])


def early_kernel(
    text_ref, q, k, v, both, both_mate, early, early_mate, left, left_mate, right, right_mate,
    sums, stats,
):
    shard = both.shape[0] // 4
    heads = q.shape[1] // HEAD_DIM
    lane = lax.broadcasted_iota(jnp.int32, (PER_BLOCK, HEAD_DIM), 1)

    def gathered(block, head, which):
        part = lanes_of(head)
        parts = [(k, v)[which][rows_at(block), part]]
        for turn in range(2):
            from_own, from_near = text_choice(text_ref[block, 0, turn])
            for near, side in (
                ((both, both_mate, which), (both, both_mate, 2 + which)),
                ((early, early_mate, which), (left, left_mate, which)),
                ((early, early_mate, 2 + which), (right, right_mate, which)),
            ):
                parts.append(
                    jnp.where(
                        from_near,
                        pick(from_own, near[0], near[1], shard, near[2], part),
                        pick(from_own, side[0], side[1], shard, side[2], part),
                    )
                )
        return jnp.concatenate(parts, axis=0)

    kept = [jnp.zeros((PER_BLOCK, HEAD_DIM), jnp.float32) for _ in range(2)]
    for group in grouped([(block, head) for head in range(heads) for block in range(2)]):
        scores = [
            head_scores(q[rows_at(block), lanes_of(head)], gathered(block, head, 0))
            for block, head in group
        ]
        peaks = [jnp.max(s, axis=1, keepdims=True) * EXP2_SCALE for s in scores]
        weights = [
            jnp.exp2(s * EXP2_SCALE - peak).astype(jnp.bfloat16) for s, peak in zip(scores, peaks)
        ]
        totals = [jnp.sum(w.astype(jnp.float32), axis=1, keepdims=True) for w in weights]
        for w, peak, total, (block, head) in zip(weights, peaks, totals, group):
            sums[rows_at(block), lanes_of(head)] = jnp.dot(
                w, gathered(block, head, 1), preferred_element_type=jnp.float32
            )
            kept[block] = jnp.where(lane == head, peak, kept[block])
            kept[block] = jnp.where(lane == heads + head, total, kept[block])
    for block in range(2):
        stats[rows_at(block), :] = kept[block]


def late_kernel(first_head, reads_ref, pattern_ref, text_ref, q, *refs):
    sums, stats, passed, arrived, term, near, near_mate, side, side_mate = refs[:9]
    out = refs[-1]
    row = lax.axis_index("rows")
    across, core = row // 2, row % 2
    shard = near.shape[0] // 2
    half = 2 * PER_BLOCK
    heads = q.shape[1] // HEAD_DIM

    def far_part(block, head, which):
        slot = pattern_ref[block, 0, 0] + pattern_ref[block, 0, 1] - block - 2
        wanted = reads_ref[0, 0, slot]
        owner = wanted // 2
        mate_at = (wanted % 2) * PER_BLOCK + which * half
        far_at = jnp.where(owner % 2 == core, 0, PER_BLOCK) + which * half
        mate_rows = pl.ds(pl.multiple_of(mate_at, PER_BLOCK), PER_BLOCK)
        far_rows = pl.ds(pl.multiple_of(far_at, PER_BLOCK), PER_BLOCK)
        return jnp.where(
            owner // 2 == across,
            passed[mate_rows, lanes_of(first_head + head)],
            arrived[far_rows, lanes_of(head)],
        )

    def gathered(block, head, which):
        part = lanes_of(first_head + head)
        parts = []
        for turn in range(2):
            from_own, from_near = text_choice(text_ref[block, 0, turn])
            parts.append(
                jnp.where(
                    from_near,
                    pick(from_own, near, near_mate, shard, which, part),
                    pick(from_own, side, side_mate, shard, which, part),
                )
            )
        return jnp.concatenate(parts + [far_part(block, head, which)], axis=0)

    count = arrived.shape[1] // HEAD_DIM
    for group in grouped([(block, head) for head in range(count) for block in range(2)]):
        scores = [
            head_scores(q[rows_at(block), lanes_of(first_head + head)], gathered(block, head, 0))
            for block, head in group
        ]
        old_peaks = [
            stats[rows_at(block), first_head + head : first_head + head + 1]
            for block, head in group
        ]
        peaks = [
            jnp.maximum(old, jnp.max(s, axis=1, keepdims=True) * EXP2_SCALE)
            for s, old in zip(scores, old_peaks)
        ]
        weights = [
            jnp.exp2(s * EXP2_SCALE - peak).astype(jnp.bfloat16) for s, peak in zip(scores, peaks)
        ]
        factors = [jnp.exp2(old - peak) for old, peak in zip(old_peaks, peaks)]
        totals = [jnp.sum(w.astype(jnp.float32), axis=1, keepdims=True) for w in weights]
        products = [
            jnp.dot(w, gathered(block, head, 1), preferred_element_type=jnp.float32)
            for w, (block, head) in zip(weights, group)
        ]
        for product, total, factor, (block, head) in zip(products, totals, factors, group):
            rows, part, at = rows_at(block), lanes_of(first_head + head), heads + first_head + head
            total = stats[rows, at : at + 1] * factor + total
            summed = sums[rows, part] * factor + product
            out[rows, lanes_of(head)] = summed / total + term[rows, part]


def body(
    q_fresh, k_fresh, v_fresh, k_stale, v_stale, text_k, text_v, conv_w, reads, pattern, text_blocks
):
    rows_here, cols_here, width = q_fresh.shape
    tokens = rows_here * cols_here
    shard = text_k.shape[0]
    swap = [(r, (r + 2) % 4) for r in range(4)]
    mates = [(r, r ^ 1) for r in range(4)]
    in_vmem = pl.BlockSpec(memory_space=pltpu.VMEM)
    in_hbm = pl.BlockSpec(memory_space=pltpu.HBM)
    params = pltpu.CompilerParams(vmem_limit_bytes=VMEM_LIMIT)
    cost = pl.CostEstimate(flops=1 << 20, transcendentals=0, bytes_accessed=1 << 16)

    def after(value, *others):
        return lax.optimization_barrier((value, *others))[0]

    def flat(grid_values):
        return grid_values.reshape(tokens, width)

    def to_mate(values):
        return lax.ppermute(values, "rows", mates)

    def rows_of(*counts):
        shapes = tuple(jax.ShapeDtypeStruct((n, width), jnp.bfloat16) for n in counts)
        return shapes if len(shapes) > 1 else shapes[0]

    def local(kernel, name, shapes, *args, specs=None, scratch=()):
        many = isinstance(shapes, tuple)
        return pl.pallas_call(
            kernel,
            out_shape=shapes,
            in_specs=specs or [in_vmem] * len(args),
            out_specs=(in_vmem,) * len(shapes) if many else in_vmem,
            scratch_shapes=scratch,
            compiler_params=params,
            cost_estimate=cost,
            name=name,
        )(*args)

    chunks = tuple(
        jax.ShapeDtypeStruct((2 * tokens, n * HEAD_DIM), jnp.bfloat16) for n in CHUNK_HEADS
    )
    in_place = [
        pltpu.with_memory_space_constraint(value, pltpu.HBM)
        for value in (flat(k_stale), flat(v_stale), v_fresh, text_k, text_v)
    ]
    offer, beside, diagonal, text = local(
        pack_kernel,
        "pack",
        rows_of(2 * shard + 8, cols_here, cols_here, 2 * shard),
        reads,
        *in_place[2:],
        specs=[pl.BlockSpec(memory_space=pltpu.SMEM)] + [in_hbm] * 3,
        scratch=[pltpu.SemaphoreType.DMA((6,))],
    )
    stale = local(
        fetch_kernel,
        "fetch",
        rows_of(2 * tokens),
        *in_place[:2],
        text,
        specs=[in_hbm] * 2 + [in_vmem],
        scratch=[pltpu.SemaphoreType.DMA((2,))],
    )
    forward = [(i, (i + 1) % 4) for i in range(4)]
    backward = [(i, (i + 3) % 4) for i in range(4)]

    near_parts = [lax.ppermute(text, "cols", p) for p in (forward, backward)]
    beside = to_mate(beside)
    diagonal = lax.ppermute(diagonal, "rows", [(1, 2), (2, 1)])
    across = lax.ppermute(offer, "rows", swap)
    passed = to_mate(stale)
    packed = local(
        send_kernel, "send", chunks, after(across, diagonal), stale, passed
    )
    far = [lax.ppermute(chunk, "rows", swap) for chunk in packed]

    both, plus, minus = local(
        join_kernel,
        "join",
        rows_of(4 * shard, 2 * shard + 16, 2 * shard + 16),
        text,
        after(across, packed[0]),
        v_fresh,
        beside,
        diagonal,
    )
    left = lax.ppermute(plus, "cols", forward)
    right = lax.ppermute(minus, "cols", backward)
    early = local(bundle_kernel, "bundle", rows_of(4 * shard), *near_parts)
    early_mate, both_mate = to_mate(early), to_mate(both)
    near_parts[0] = after(near_parts[0], early_mate, both_mate)
    upper, lower = (
        local(bundle_kernel, "pair", rows_of(4 * shard), *pair)
        for pair in ((near_parts[0], left), (near_parts[1], right))
    )
    upper = lax.ppermute(upper, "cols", [(1, 2), (2, 3)])
    lower = lax.ppermute(lower, "cols", [(1, 0), (2, 1)])
    left_mate, right_mate = to_mate(left), to_mate(right)
    sums, stats = local(
        early_kernel,
        "early",
        (
            jax.ShapeDtypeStruct((tokens, width), jnp.float32),
            jax.ShapeDtypeStruct((tokens, HEAD_DIM), jnp.float32),
        ),
        text_blocks, flat(q_fresh), flat(k_fresh), flat(v_fresh),
        both, both_mate, early, early_mate, left, left_mate, right, right_mate,
        specs=[pl.BlockSpec(memory_space=pltpu.SMEM)] + [in_vmem] * 11,
    )
    upper, lower = after(upper, stats), after(lower, stats)
    far_side = local(choose_kernel, "choose", rows_of(2 * shard, 2 * shard), upper, lower)
    late = [part for side in far_side for part in (side, to_mate(side))]
    term = local(
        term_kernel,
        "term",
        jax.ShapeDtypeStruct((tokens, width), jnp.float32),
        v_fresh, beside, diagonal, left, right, conv_w,
    )

    out = None
    first_head = 0
    for chunk, head_count in enumerate(CHUNK_HEADS):
        if out is not None:
            far[chunk] = after(far[chunk], out)
        block = pl.BlockSpec(
            (pl.Element(tokens), pl.Element(head_count * HEAD_DIM)),
            lambda i, *_, at=first_head * HEAD_DIM: (0, at),
        )
        out = pl.pallas_call(
            functools.partial(late_kernel, first_head),
            out_shape=jax.ShapeDtypeStruct((tokens, width), jnp.float32),
            grid_spec=pltpu.PrefetchScalarGridSpec(
                num_scalar_prefetch=3,
                grid=(1,),
                in_specs=[in_vmem] * 10 + [in_hbm] * (out is not None),
                out_specs=block,
            ),
            input_output_aliases={13: 0} if out is not None else {},
            compiler_params=params,
            cost_estimate=cost,
            name=f"late{chunk}",
        )(
            reads, pattern, text_blocks, flat(q_fresh), sums, stats,
            passed, far[chunk], term, *late,
            *([out] if out is not None else []),
        )
        first_head += head_count
    return out.reshape(rows_here, cols_here, width)


def fits(mesh, reads, pattern, text_k):
    sizes = dict(mesh.shape)
    return (
        sizes["rows"] == 4
        and sizes["cols"] == 4
        and reads.shape[-1] == 2
        and pattern.shape[-1] == 2
        and pattern.shape[0] == 2 * sizes["groups"] * 4
        and text_k.shape[0] == sizes["groups"] * 4 * PER_BLOCK
    )


def solution(mesh):
    grid = P(("groups", "rows"), "cols", None)
    text = P(("groups", "rows", "cols"), None)
    in_specs = (grid, grid, grid, grid, grid, text, text, P(), grid, grid, grid)

    def program(*args):
        chosen = body if fits(mesh, args[8], args[9], args[5]) else general_body
        return jax.shard_map(
            chosen, mesh=mesh, in_specs=in_specs, out_specs=grid, check_vma=False
        )(*args)

    return program
```

```python
import functools
import math

import jax
import jax.numpy as jnp
from jax import lax
from jax.experimental import pallas as pl
from jax.experimental.pallas import tpu as pltpu
from jax.sharding import PartitionSpec as P

HEAD_DIM = 128
BLOCK_ROWS = 4
BLOCK_COLS = 32
PER_BLOCK = BLOCK_ROWS * BLOCK_COLS
SCORE_SCALE = 1.0 / math.sqrt(HEAD_DIM)
EXP2_SCALE = SCORE_SCALE * math.log2(math.e)
CHUNK_HEADS = (9, 3)
GROUP = 8
VMEM_LIMIT = 24 * 1024 * 1024


def extended(cells, sides, width):
    for axis, dim in sides:
        count = lax.axis_size(axis)
        ends = count - 1
        head = lax.slice_in_dim(cells, 0, width, axis=dim)
        tail = lax.slice_in_dim(cells, cells.shape[dim] - width, cells.shape[dim], axis=dim)
        cells = jnp.concatenate(
            [
                lax.ppermute(tail, axis, [(i, (i + 1) % count) for i in range(ends)]),
                cells,
                lax.ppermute(head, axis, [((i + 1) % count, i) for i in range(ends)]),
            ],
            axis=dim,
        )
    return cells


def position(v_fresh, conv_w):
    rows_here, cols_here, feature_width = v_fresh.shape
    rims = extended(v_fresh, (("rows", 0), ("cols", 1)), 1)
    position_term = jnp.zeros((rows_here, cols_here, feature_width), jnp.float32)
    for row_tap in range(3):
        for col_tap in range(3):
            position_term = position_term + conv_w[row_tap, col_tap] * rims[
                row_tap : row_tap + rows_here, col_tap : col_tap + cols_here
            ].astype(jnp.float32)
    return position_term


def split_heads(flat_rows):
    return flat_rows.reshape(flat_rows.shape[:-1] + (flat_rows.shape[-1] // HEAD_DIM, HEAD_DIM))


def attend(softmax_state, queries, key_blocks, value_blocks, allowed):
    old_peak, old_total, old_summed = softmax_state
    scores = (
        jnp.einsum(
            "bqhd,nkhd->bhqnk", queries, key_blocks, preferred_element_type=jnp.float32
        )
        * SCORE_SCALE
    )
    scores = jnp.where(allowed[:, None, None, :, None], scores, -1e30)
    new_peak = jnp.maximum(old_peak, jnp.max(scores, axis=(3, 4)))
    weights = jnp.exp(scores - new_peak[:, :, :, None, None]).astype(jnp.bfloat16)
    factor = jnp.exp(old_peak - new_peak)
    new_total = old_total * factor + jnp.sum(weights.astype(jnp.float32), axis=(3, 4))
    product = jnp.einsum(
        "bhqnk,nkhd->bqhd", weights, value_blocks, preferred_element_type=jnp.float32
    )
    new_summed = old_summed * jnp.transpose(factor, (0, 2, 1))[:, :, :, None] + product
    return (new_peak, new_total, new_summed)


def general_body(
    q_fresh, k_fresh, v_fresh, k_stale, v_stale, text_k, text_v, conv_w, reads, pattern, text_blocks
):
    rows_here, cols_here, feature_width = q_fresh.shape
    blocks_here = rows_here // BLOCK_ROWS
    head_count = feature_width // HEAD_DIM

    def as_blocks(grid_values):
        return split_heads(grid_values.reshape(blocks_here, PER_BLOCK, feature_width))

    queries = as_blocks(q_fresh)
    text_keys, text_values = (
        lax.all_gather(text_k, ("rows", "cols"), axis=0, tiled=True),
        lax.all_gather(text_v, ("rows", "cols"), axis=0, tiled=True),
    )
    text_count = text_keys.shape[0] // PER_BLOCK
    text_keys = split_heads(text_keys.reshape(text_count, PER_BLOCK, feature_width))
    text_values = split_heads(text_values.reshape(text_count, PER_BLOCK, feature_width))
    wanted = pattern[:, 0, :]
    fetch_rows = reads[0, 0, :]
    fetch_count = fetch_rows.shape[0]
    slot_count = blocks_here + fetch_count
    slot_mask = jnp.any(
        wanted[:, :, None] == jnp.arange(slot_count, dtype=jnp.int32)[None, None, :], axis=1
    )
    text_mask = jnp.any(
        text_blocks[:, 0, :, None] == jnp.arange(text_count, dtype=jnp.int32)[None, None, :], axis=1
    )
    softmax_state = (
        jnp.full((blocks_here, head_count, PER_BLOCK), -1e30, jnp.float32),
        jnp.zeros((blocks_here, head_count, PER_BLOCK), jnp.float32),
        jnp.zeros((blocks_here, PER_BLOCK, head_count, HEAD_DIM), jnp.float32),
    )
    softmax_state = attend(
        softmax_state,
        queries,
        jnp.concatenate([as_blocks(k_fresh), text_keys], axis=0),
        jnp.concatenate([as_blocks(v_fresh), text_values], axis=0),
        jnp.concatenate([slot_mask[:, :blocks_here], text_mask], axis=1),
    )
    chosen = jnp.where(
        wanted >= blocks_here, fetch_rows[jnp.clip(wanted - blocks_here, 0, fetch_count - 1)], -1
    )
    piece_keys = lax.all_gather(as_blocks(k_stale), "rows", axis=0, tiled=True)
    piece_values = lax.all_gather(as_blocks(v_stale), "rows", axis=0, tiled=True)
    block_rows = jnp.arange(piece_keys.shape[0], dtype=jnp.int32)
    piece_mask = jnp.any(chosen[:, :, None] == block_rows[None, None, :], axis=1)
    softmax_state = attend(softmax_state, queries, piece_keys, piece_values, piece_mask)
    _, final_total, final_summed = softmax_state
    mixed_rows = final_summed / jnp.transpose(final_total, (0, 2, 1))[:, :, :, None]
    attention = mixed_rows.reshape(rows_here, cols_here, feature_width)
    return attention + position(v_fresh, conv_w)


def head_scores(queries, keys):
    return lax.dot_general(
        queries, keys, (((1,), (1,)), ((), ())), preferred_element_type=jnp.float32
    )


def run_copies(copies, sems):
    copies = [pltpu.make_async_copy(*pair, sems.at[i]) for i, pair in enumerate(copies)]
    for copy in copies:
        copy.start()
    for copy in copies:
        copy.wait()


def pack_kernel(k_hbm, v_hbm, cells, text_k, text_v, stale, beside, diagonal, text, sems):
    tokens, shard = k_hbm.shape[0], text_k.shape[0]
    row = lax.axis_index("rows")
    end = cells.shape[0] - 1
    copies = []
    for which, source in enumerate((text_k, text_v)):
        copies.append((source, text.at[pl.ds(which * shard, shard)]))
    for which, source in enumerate((k_hbm, v_hbm)):
        copies.append((source, stale.at[pl.ds(which * tokens, tokens)]))
    copies.append((cells.at[jnp.where(row % 2 == 0, end, 0)], beside))
    copies.append((cells.at[jnp.where(row < 2, end, 0)], diagonal))
    run_copies(copies, sems)


def offer_kernel(reads_ref, text, out):
    both, width = text.shape
    partner = (lax.axis_index("rows") + 2) % 4

    def flag(owner):
        found = 0
        for turn in range(2):
            entry = reads_ref[0, 0, turn]
            found = jnp.where(entry // 2 == owner, entry % 2, found)
        return jnp.full((8, width // 2), found.astype(jnp.float32), jnp.float32)

    flags = [flag(owner) for owner in (partner, partner + 1 - 2 * (partner % 2))]
    out[pl.ds(0, both), :] = text[...]
    out[pl.ds(both, 8), :] = jnp.concatenate(flags, axis=1).astype(out.dtype)


def send_kernel(across, stale, passed, *outs):
    tokens, width = stale.shape[0] // 2, stale.shape[1]

    def block_of(slot):
        lanes = pl.ds(slot * (width // 2), HEAD_DIM)
        flag = jnp.max(across[pl.ds(across.shape[0] - 8, 8), lanes].astype(jnp.float32))
        return jnp.where(flag > 0.5, PER_BLOCK, 0)

    starts = block_of(0), block_of(1)
    first = 0
    for out in outs:
        part = pl.ds(first, out.shape[1])
        first += out.shape[1]
        for which in range(2):
            for slot, source in enumerate((stale, passed)):
                rows = pl.ds(pl.multiple_of(which * tokens + starts[slot], PER_BLOCK), PER_BLOCK)
                at = (2 * which + slot) * PER_BLOCK
                out[pl.ds(at, PER_BLOCK), :] = source[rows, part]


def bundle_kernel(*refs):
    out = refs[-1]
    at = 0
    for ref in refs[:-1]:
        count = ref.shape[0] - ref.shape[0] % 64
        out[pl.ds(at, count), :] = ref[pl.ds(0, count), :]
        at += count


def choose_kernel(upper, lower, first, second):
    upwards = lax.axis_index("cols") >= 2
    half = first.shape[0]
    for at, out in ((0, first), (half, second)):
        rows = pl.ds(at, half)
        out[...] = jnp.where(upwards, upper[rows, :], lower[rows, :])


def above_below(beside, diagonal):
    first_core = lax.axis_index("rows") % 2 == 0
    return (
        jnp.where(first_core, diagonal, beside),
        jnp.where(first_core, beside, diagonal),
    )


def join_kernel(text, across, cells, beside, diagonal, both, plus, minus):
    shard = text.shape[0] // 2
    rows_here, cols_here, width = cells.shape
    above, below = above_below(beside[...], diagonal[...])
    rows = [above] + [cells[i] for i in range(rows_here)] + [below]
    rows = [row.astype(jnp.float32) for row in rows]
    spare = jnp.zeros((16 - len(rows), width), jnp.float32)
    both[pl.ds(0, 2 * shard), :] = text[...]
    both[pl.ds(2 * shard, 2 * shard), :] = across[pl.ds(0, 2 * shard), :]
    for target in (plus, minus):
        target[pl.ds(0, 2 * shard), :] = across[pl.ds(0, 2 * shard), :]
    for target, at in ((plus, cols_here - 1), (minus, 0)):
        edge = jnp.concatenate([row[at : at + 1] for row in rows] + [spare], axis=0)
        target[pl.ds(2 * shard, 16), :] = edge.astype(target.dtype)


def term_kernel(cells, beside, diagonal, left, right, weights, out):
    rows_here, cols_here, width = cells.shape
    col = lax.axis_index("cols")
    edges = pl.ds(left.shape[0] - 16, 16)
    place = lax.broadcasted_iota(jnp.int32, (cols_here, HEAD_DIM), 0)
    for lane in range(width // HEAD_DIM):
        part = pl.ds(lane * HEAD_DIM, HEAD_DIM)
        above, below = above_below(beside[:, part], diagonal[:, part])
        lefts = left[edges, part].astype(jnp.float32)
        rights = right[edges, part].astype(jnp.float32)
        lefts = jnp.where(col > 0, lefts, 0.0)
        rights = jnp.where(col < 3, rights, 0.0)
        taps = []
        for row in range(rows_here + 2):
            if row == 0:
                centre = above
            elif row == rows_here + 1:
                centre = below
            else:
                centre = cells[row - 1, :, part]
            centre = centre.astype(jnp.float32)
            before = jnp.where(place == 0, lefts[row : row + 1], pltpu.roll(centre, 1, 0))
            after = jnp.where(
                place == cols_here - 1, rights[row : row + 1], pltpu.roll(centre, cols_here - 1, 0)
            )
            taps.append((before, centre, after))
        for row in range(rows_here):
            total = None
            for row_tap in range(3):
                for col_tap in range(3):
                    piece = weights[row_tap, col_tap : col_tap + 1, part] * taps[row + row_tap][col_tap]
                    total = piece if total is None else total + piece
            out[pl.ds(row * cols_here, cols_here), part] = total


def grouped(jobs):
    size = -(-len(jobs) // -(-len(jobs) // GROUP))
    return [jobs[at : at + size] for at in range(0, len(jobs), size)]


def lanes_of(head):
    return pl.ds(head * HEAD_DIM, HEAD_DIM)


def rows_at(block):
    return pl.ds(block * PER_BLOCK, PER_BLOCK)


def text_choice(chosen):
    row = lax.axis_index("rows")
    return chosen % 2 == row % 2, chosen // 2 == row // 2


def pick(from_own, own, other, shard, at, part):
    rows = pl.ds(at * shard, shard)
    return jnp.where(from_own, own[rows, part], other[rows, part])


def early_kernel(
    text_ref, q, k, v, both, both_mate, early, early_mate, left, left_mate, right, right_mate,
    sums, peaks_out, totals_out,
):
    shard = both.shape[0] // 4
    heads = q.shape[1] // HEAD_DIM

    def gathered(block, head, which):
        part = lanes_of(head)
        parts = [(k, v)[which][rows_at(block), part]]
        for turn in range(2):
            from_own, from_near = text_choice(text_ref[block, 0, turn])
            for near, side in (
                ((both, both_mate, which), (both, both_mate, 2 + which)),
                ((early, early_mate, which), (left, left_mate, which)),
                ((early, early_mate, 2 + which), (right, right_mate, which)),
            ):
                parts.append(
                    jnp.where(
                        from_near,
                        pick(from_own, near[0], near[1], shard, near[2], part),
                        pick(from_own, side[0], side[1], shard, side[2], part),
                    )
                )
        return jnp.concatenate(parts, axis=0)

    for group in grouped([(block, head) for head in range(heads) for block in range(2)]):
        scores = [
            head_scores(q[rows_at(block), lanes_of(head)], gathered(block, head, 0))
            for block, head in group
        ]
        peaks = [jnp.max(s, axis=1, keepdims=True) * EXP2_SCALE for s in scores]
        weights = [
            jnp.exp2(s * EXP2_SCALE - peak).astype(jnp.bfloat16) for s, peak in zip(scores, peaks)
        ]
        totals = [jnp.sum(w.astype(jnp.float32), axis=1, keepdims=True) for w in weights]
        for w, peak, total, (block, head) in zip(weights, peaks, totals, group):
            sums[rows_at(block), lanes_of(head)] = jnp.dot(
                w, gathered(block, head, 1), preferred_element_type=jnp.float32
            )
            spread = (PER_BLOCK, HEAD_DIM)
            peaks_out[rows_at(block), lanes_of(head)] = jnp.broadcast_to(peak, spread)
            totals_out[rows_at(block), lanes_of(head)] = jnp.broadcast_to(total, spread)


def late_kernel(first_head, reads_ref, pattern_ref, text_ref, q, *refs):
    sums, old_peaks, old_totals, passed, arrived, term = refs[:6]
    near, near_mate, side, side_mate = refs[6:10]
    out = refs[-1]
    row = lax.axis_index("rows")
    across, core = row // 2, row % 2
    shard = near.shape[0] // 2
    half = 2 * PER_BLOCK

    def far_part(block, head, which):
        slot = pattern_ref[block, 0, 0] + pattern_ref[block, 0, 1] - block - 2
        wanted = reads_ref[0, 0, slot]
        owner = wanted // 2
        mate_at = (wanted % 2) * PER_BLOCK + which * half
        far_at = jnp.where(owner % 2 == core, 0, PER_BLOCK) + which * half
        mate_rows = pl.ds(pl.multiple_of(mate_at, PER_BLOCK), PER_BLOCK)
        far_rows = pl.ds(pl.multiple_of(far_at, PER_BLOCK), PER_BLOCK)
        return jnp.where(
            owner // 2 == across,
            passed[mate_rows, lanes_of(first_head + head)],
            arrived[far_rows, lanes_of(head)],
        )

    def gathered(block, head, which):
        part = lanes_of(first_head + head)
        parts = [far_part(block, head, which)]
        for turn in range(2):
            from_own, from_near = text_choice(text_ref[block, 0, turn])
            parts.append(
                jnp.where(
                    from_near,
                    pick(from_own, near, near_mate, shard, which, part),
                    pick(from_own, side, side_mate, shard, which, part),
                )
            )
        return jnp.concatenate(parts, axis=0)

    count = arrived.shape[1] // HEAD_DIM
    for group in grouped([(block, head) for head in range(count) for block in range(2)]):
        scores = [
            head_scores(q[rows_at(block), lanes_of(first_head + head)], gathered(block, head, 0))
            for block, head in group
        ]
        olds = [old_peaks[rows_at(block), lanes_of(first_head + head)] for block, head in group]
        peaks = [
            jnp.maximum(old, jnp.max(s, axis=1, keepdims=True) * EXP2_SCALE)
            for s, old in zip(scores, olds)
        ]
        weights = []
        for s, peak in zip(scores, peaks):
            wide = jnp.concatenate([peak, peak[:, : s.shape[1] - HEAD_DIM]], axis=1)
            weights.append(jnp.exp2(s * EXP2_SCALE - wide).astype(jnp.bfloat16))
        totals = [jnp.sum(w.astype(jnp.float32), axis=1, keepdims=True) for w in weights]
        products = [
            jnp.dot(w, gathered(block, head, 1), preferred_element_type=jnp.float32)
            for w, (block, head) in zip(weights, group)
        ]
        for product, total, old, peak, (block, head) in zip(products, totals, olds, peaks, group):
            rows, part = rows_at(block), lanes_of(first_head + head)
            factor = jnp.exp2(old - peak)
            total = old_totals[rows, part] * factor + total
            summed = sums[rows, part] * factor + product
            out[rows, lanes_of(head)] = summed / total + term[rows, part]


def body(
    q_fresh, k_fresh, v_fresh, k_stale, v_stale, text_k, text_v, conv_w, reads, pattern, text_blocks
):
    rows_here, cols_here, width = q_fresh.shape
    tokens = rows_here * cols_here
    shard = text_k.shape[0]
    swap = [(r, (r + 2) % 4) for r in range(4)]
    mates = [(r, r ^ 1) for r in range(4)]
    in_vmem = pl.BlockSpec(memory_space=pltpu.VMEM)
    in_hbm = pl.BlockSpec(memory_space=pltpu.HBM)
    params = pltpu.CompilerParams(vmem_limit_bytes=VMEM_LIMIT)
    cost = pl.CostEstimate(flops=1 << 20, transcendentals=0, bytes_accessed=1 << 16)

    def after(value, *others):
        return lax.optimization_barrier((value, *others))[0]

    def flat(grid_values):
        return grid_values.reshape(tokens, width)

    def to_mate(values):
        return lax.ppermute(values, "rows", mates)

    def rows_of(*counts):
        shapes = tuple(jax.ShapeDtypeStruct((n, width), jnp.bfloat16) for n in counts)
        return shapes if len(shapes) > 1 else shapes[0]

    def local(kernel, name, shapes, *args, specs=None, scratch=()):
        many = isinstance(shapes, tuple)
        return pl.pallas_call(
            kernel,
            out_shape=shapes,
            in_specs=specs or [in_vmem] * len(args),
            out_specs=(in_vmem,) * len(shapes) if many else in_vmem,
            scratch_shapes=scratch,
            compiler_params=params,
            cost_estimate=cost,
            name=name,
        )(*args)

    chunks = tuple(
        jax.ShapeDtypeStruct((2 * tokens, n * HEAD_DIM), jnp.bfloat16) for n in CHUNK_HEADS
    )
    in_place = [
        pltpu.with_memory_space_constraint(value, pltpu.HBM)
        for value in (flat(k_stale), flat(v_stale), v_fresh, text_k, text_v)
    ]
    stale, beside, diagonal, text = local(
        pack_kernel,
        "pack",
        rows_of(2 * tokens, cols_here, cols_here, 2 * shard),
        *in_place,
        specs=[in_hbm] * 5,
        scratch=[pltpu.SemaphoreType.DMA((6,))],
    )
    forward = [(i, (i + 1) % 4) for i in range(4)]
    backward = [(i, (i + 3) % 4) for i in range(4)]

    near_parts = [lax.ppermute(text, "cols", p) for p in (forward, backward)]
    beside = to_mate(beside)
    diagonal = lax.ppermute(diagonal, "rows", [(1, 2), (2, 1)])
    offer = local(
        offer_kernel,
        "offer",
        rows_of(2 * shard + 8),
        reads,
        text,
        specs=[pl.BlockSpec(memory_space=pltpu.SMEM), in_vmem],
    )
    across = lax.ppermute(offer, "rows", swap)
    passed = to_mate(after(stale, beside))
    packed = local(
        send_kernel, "send", chunks, after(across, diagonal), stale, passed
    )
    far = [lax.ppermute(chunk, "rows", swap) for chunk in packed]

    both, plus, minus = local(
        join_kernel,
        "join",
        rows_of(4 * shard, 2 * shard + 16, 2 * shard + 16),
        text,
        after(across, packed[0]),
        v_fresh,
        beside,
        diagonal,
    )
    left = lax.ppermute(plus, "cols", forward)
    right = lax.ppermute(minus, "cols", backward)
    early = local(bundle_kernel, "bundle", rows_of(4 * shard), *near_parts)
    early_mate, both_mate = to_mate(early), to_mate(both)
    near_parts[0] = after(near_parts[0], early_mate, both_mate)
    upper, lower = (
        local(bundle_kernel, "pair", rows_of(4 * shard), *pair)
        for pair in ((near_parts[0], left), (near_parts[1], right))
    )
    upper = lax.ppermute(upper, "cols", [(1, 2), (2, 3)])
    lower = lax.ppermute(lower, "cols", [(1, 0), (2, 1)])
    left_mate, right_mate = to_mate(left), to_mate(right)
    sums, peaks, totals = local(
        early_kernel,
        "early",
        (jax.ShapeDtypeStruct((tokens, width), jnp.float32),) * 3,
        text_blocks, flat(q_fresh), flat(k_fresh), flat(v_fresh),
        both, both_mate, early, early_mate, left, left_mate, right, right_mate,
        specs=[pl.BlockSpec(memory_space=pltpu.SMEM)] + [in_vmem] * 11,
    )
    upper, lower = after(upper, sums), after(lower, sums)
    far_side = local(choose_kernel, "choose", rows_of(2 * shard, 2 * shard), upper, lower)
    late = [part for side in far_side for part in (side, to_mate(side))]
    term = local(
        term_kernel,
        "term",
        jax.ShapeDtypeStruct((tokens, width), jnp.float32),
        v_fresh, beside, diagonal, left, right, conv_w,
    )

    out = None
    first_head = 0
    for chunk, head_count in enumerate(CHUNK_HEADS):
        if out is not None:
            far[chunk] = after(far[chunk], out)
        block = pl.BlockSpec(
            (pl.Element(tokens), pl.Element(head_count * HEAD_DIM)),
            lambda i, *_, at=first_head * HEAD_DIM: (0, at),
        )
        out = pl.pallas_call(
            functools.partial(late_kernel, first_head),
            out_shape=jax.ShapeDtypeStruct((tokens, width), jnp.float32),
            grid_spec=pltpu.PrefetchScalarGridSpec(
                num_scalar_prefetch=3,
                grid=(1,),
                in_specs=[in_vmem] * 11 + [in_hbm] * (out is not None),
                out_specs=block,
            ),
            input_output_aliases={14: 0} if out is not None else {},
            compiler_params=params,
            cost_estimate=cost,
            name=f"late{chunk}",
        )(
            reads, pattern, text_blocks, flat(q_fresh), sums, peaks, totals,
            passed, far[chunk], term, *late,
            *([out] if out is not None else []),
        )
        first_head += head_count
    return out.reshape(rows_here, cols_here, width)


def fits(mesh, reads, pattern, text_k):
    sizes = dict(mesh.shape)
    return (
        sizes["rows"] == 4
        and sizes["cols"] == 4
        and reads.shape[-1] == 2
        and pattern.shape[-1] == 2
        and pattern.shape[0] == 2 * sizes["groups"] * 4
        and text_k.shape[0] == sizes["groups"] * 4 * PER_BLOCK
    )


def solution(mesh):
    grid = P(("groups", "rows"), "cols", None)
    text = P(("groups", "rows", "cols"), None)
    in_specs = (grid, grid, grid, grid, grid, text, text, P(), grid, grid, grid)

    def program(*args):
        chosen = body if fits(mesh, args[8], args[9], args[5]) else general_body
        return jax.shard_map(
            chosen, mesh=mesh, in_specs=in_specs, out_specs=grid, check_vma=False
        )(*args)

    return program
```

```python
import functools
import math

import jax
import jax.numpy as jnp
from jax import lax
from jax.experimental import pallas as pl
from jax.experimental.pallas import tpu as pltpu
from jax.sharding import PartitionSpec as P

HEAD_DIM = 128
BLOCK_ROWS = 4
BLOCK_COLS = 32
PER_BLOCK = BLOCK_ROWS * BLOCK_COLS
SCORE_SCALE = 1.0 / math.sqrt(HEAD_DIM)
EXP2_SCALE = SCORE_SCALE * math.log2(math.e)
CHUNK_HEADS = (10, 2)
GROUP = 8
VMEM_LIMIT = 24 * 1024 * 1024


def extended(cells, sides, width):
    for axis, dim in sides:
        count = lax.axis_size(axis)
        ends = count - 1
        head = lax.slice_in_dim(cells, 0, width, axis=dim)
        tail = lax.slice_in_dim(cells, cells.shape[dim] - width, cells.shape[dim], axis=dim)
        cells = jnp.concatenate(
            [
                lax.ppermute(tail, axis, [(i, (i + 1) % count) for i in range(ends)]),
                cells,
                lax.ppermute(head, axis, [((i + 1) % count, i) for i in range(ends)]),
            ],
            axis=dim,
        )
    return cells


def position(v_fresh, conv_w):
    rows_here, cols_here, feature_width = v_fresh.shape
    rims = extended(v_fresh, (("rows", 0), ("cols", 1)), 1)
    position_term = jnp.zeros((rows_here, cols_here, feature_width), jnp.float32)
    for row_tap in range(3):
        for col_tap in range(3):
            position_term = position_term + conv_w[row_tap, col_tap] * rims[
                row_tap : row_tap + rows_here, col_tap : col_tap + cols_here
            ].astype(jnp.float32)
    return position_term


def split_heads(flat_rows):
    return flat_rows.reshape(flat_rows.shape[:-1] + (flat_rows.shape[-1] // HEAD_DIM, HEAD_DIM))


def attend(softmax_state, queries, key_blocks, value_blocks, allowed):
    old_peak, old_total, old_summed = softmax_state
    scores = (
        jnp.einsum(
            "bqhd,nkhd->bhqnk", queries, key_blocks, preferred_element_type=jnp.float32
        )
        * SCORE_SCALE
    )
    scores = jnp.where(allowed[:, None, None, :, None], scores, -1e30)
    new_peak = jnp.maximum(old_peak, jnp.max(scores, axis=(3, 4)))
    weights = jnp.exp(scores - new_peak[:, :, :, None, None]).astype(jnp.bfloat16)
    factor = jnp.exp(old_peak - new_peak)
    new_total = old_total * factor + jnp.sum(weights.astype(jnp.float32), axis=(3, 4))
    product = jnp.einsum(
        "bhqnk,nkhd->bqhd", weights, value_blocks, preferred_element_type=jnp.float32
    )
    new_summed = old_summed * jnp.transpose(factor, (0, 2, 1))[:, :, :, None] + product
    return (new_peak, new_total, new_summed)


def general_body(
    q_fresh, k_fresh, v_fresh, k_stale, v_stale, text_k, text_v, conv_w, reads, pattern, text_blocks
):
    rows_here, cols_here, feature_width = q_fresh.shape
    blocks_here = rows_here // BLOCK_ROWS
    head_count = feature_width // HEAD_DIM

    def as_blocks(grid_values):
        return split_heads(grid_values.reshape(blocks_here, PER_BLOCK, feature_width))

    queries = as_blocks(q_fresh)
    text_keys, text_values = (
        lax.all_gather(text_k, ("rows", "cols"), axis=0, tiled=True),
        lax.all_gather(text_v, ("rows", "cols"), axis=0, tiled=True),
    )
    text_count = text_keys.shape[0] // PER_BLOCK
    text_keys = split_heads(text_keys.reshape(text_count, PER_BLOCK, feature_width))
    text_values = split_heads(text_values.reshape(text_count, PER_BLOCK, feature_width))
    wanted = pattern[:, 0, :]
    fetch_rows = reads[0, 0, :]
    fetch_count = fetch_rows.shape[0]
    slot_count = blocks_here + fetch_count
    slot_mask = jnp.any(
        wanted[:, :, None] == jnp.arange(slot_count, dtype=jnp.int32)[None, None, :], axis=1
    )
    text_mask = jnp.any(
        text_blocks[:, 0, :, None] == jnp.arange(text_count, dtype=jnp.int32)[None, None, :], axis=1
    )
    softmax_state = (
        jnp.full((blocks_here, head_count, PER_BLOCK), -1e30, jnp.float32),
        jnp.zeros((blocks_here, head_count, PER_BLOCK), jnp.float32),
        jnp.zeros((blocks_here, PER_BLOCK, head_count, HEAD_DIM), jnp.float32),
    )
    softmax_state = attend(
        softmax_state,
        queries,
        jnp.concatenate([as_blocks(k_fresh), text_keys], axis=0),
        jnp.concatenate([as_blocks(v_fresh), text_values], axis=0),
        jnp.concatenate([slot_mask[:, :blocks_here], text_mask], axis=1),
    )
    chosen = jnp.where(
        wanted >= blocks_here, fetch_rows[jnp.clip(wanted - blocks_here, 0, fetch_count - 1)], -1
    )
    piece_keys = lax.all_gather(as_blocks(k_stale), "rows", axis=0, tiled=True)
    piece_values = lax.all_gather(as_blocks(v_stale), "rows", axis=0, tiled=True)
    block_rows = jnp.arange(piece_keys.shape[0], dtype=jnp.int32)
    piece_mask = jnp.any(chosen[:, :, None] == block_rows[None, None, :], axis=1)
    softmax_state = attend(softmax_state, queries, piece_keys, piece_values, piece_mask)
    _, final_total, final_summed = softmax_state
    mixed_rows = final_summed / jnp.transpose(final_total, (0, 2, 1))[:, :, :, None]
    attention = mixed_rows.reshape(rows_here, cols_here, feature_width)
    return attention + position(v_fresh, conv_w)


def head_scores(queries, keys):
    return lax.dot_general(
        queries, keys, (((1,), (1,)), ((), ())), preferred_element_type=jnp.float32
    )


def run_copies(copies, sems):
    copies = [pltpu.make_async_copy(*pair, sems.at[i]) for i, pair in enumerate(copies)]
    for copy in copies:
        copy.start()
    for copy in copies:
        copy.wait()


def pack_kernel(k_hbm, v_hbm, cells, text_k, text_v, stale, beside, diagonal, text, sems):
    tokens, shard = k_hbm.shape[0], text_k.shape[0]
    row = lax.axis_index("rows")
    end = cells.shape[0] - 1
    copies = []
    for which, source in enumerate((text_k, text_v)):
        copies.append((source, text.at[pl.ds(which * shard, shard)]))
    for which, source in enumerate((k_hbm, v_hbm)):
        copies.append((source, stale.at[pl.ds(which * tokens, tokens)]))
    copies.append((cells.at[jnp.where(row % 2 == 0, end, 0)], beside))
    copies.append((cells.at[jnp.where(row < 2, end, 0)], diagonal))
    run_copies(copies, sems)


def offer_kernel(reads_ref, text, out):
    both, width = text.shape
    partner = (lax.axis_index("rows") + 2) % 4

    def flag(owner):
        found = 0
        for turn in range(2):
            entry = reads_ref[0, 0, turn]
            found = jnp.where(entry // 2 == owner, entry % 2, found)
        return jnp.full((8, width // 2), found.astype(jnp.float32), jnp.float32)

    flags = [flag(owner) for owner in (partner, partner + 1 - 2 * (partner % 2))]
    out[pl.ds(0, both), :] = text[...]
    out[pl.ds(both, 8), :] = jnp.concatenate(flags, axis=1).astype(out.dtype)


def send_kernel(across, stale, passed, *outs):
    tokens, width = stale.shape[0] // 2, stale.shape[1]

    def block_of(slot):
        lanes = pl.ds(slot * (width // 2), HEAD_DIM)
        flag = jnp.max(across[pl.ds(across.shape[0] - 8, 8), lanes].astype(jnp.float32))
        return jnp.where(flag > 0.5, PER_BLOCK, 0)

    starts = block_of(0), block_of(1)
    first = 0
    for out in outs:
        part = pl.ds(first, out.shape[1])
        first += out.shape[1]
        for which in range(2):
            for slot, source in enumerate((stale, passed)):
                rows = pl.ds(pl.multiple_of(which * tokens + starts[slot], PER_BLOCK), PER_BLOCK)
                at = (2 * which + slot) * PER_BLOCK
                out[pl.ds(at, PER_BLOCK), :] = source[rows, part]


def bundle_kernel(*refs):
    out = refs[-1]
    at = 0
    for ref in refs[:-1]:
        count = ref.shape[0] - ref.shape[0] % 64
        out[pl.ds(at, count), :] = ref[pl.ds(0, count), :]
        at += count


def choose_kernel(upper, lower, first, second):
    upwards = lax.axis_index("cols") >= 2
    half = first.shape[0]
    for at, out in ((0, first), (half, second)):
        rows = pl.ds(at, half)
        out[...] = jnp.where(upwards, upper[rows, :], lower[rows, :])


def above_below(beside, diagonal):
    first_core = lax.axis_index("rows") % 2 == 0
    return (
        jnp.where(first_core, diagonal, beside),
        jnp.where(first_core, beside, diagonal),
    )


def join_kernel(text, across, cells, beside, diagonal, both, plus, minus):
    shard = text.shape[0] // 2
    rows_here, cols_here, width = cells.shape
    above, below = above_below(beside[...], diagonal[...])
    rows = [above] + [cells[i] for i in range(rows_here)] + [below]
    rows = [row.astype(jnp.float32) for row in rows]
    spare = jnp.zeros((16 - len(rows), width), jnp.float32)
    both[pl.ds(0, 2 * shard), :] = text[...]
    both[pl.ds(2 * shard, 2 * shard), :] = across[pl.ds(0, 2 * shard), :]
    for target in (plus, minus):
        target[pl.ds(0, 2 * shard), :] = across[pl.ds(0, 2 * shard), :]
    for target, at in ((plus, cols_here - 1), (minus, 0)):
        edge = jnp.concatenate([row[at : at + 1] for row in rows] + [spare], axis=0)
        target[pl.ds(2 * shard, 16), :] = edge.astype(target.dtype)


def term_kernel(cells, beside, diagonal, left, right, weights, out):
    rows_here, cols_here, width = cells.shape
    col = lax.axis_index("cols")
    edges = pl.ds(left.shape[0] - 16, 16)
    place = lax.broadcasted_iota(jnp.int32, (cols_here, HEAD_DIM), 0)
    for lane in range(width // HEAD_DIM):
        part = pl.ds(lane * HEAD_DIM, HEAD_DIM)
        above, below = above_below(beside[:, part], diagonal[:, part])
        lefts = left[edges, part].astype(jnp.float32)
        rights = right[edges, part].astype(jnp.float32)
        lefts = jnp.where(col > 0, lefts, 0.0)
        rights = jnp.where(col < 3, rights, 0.0)
        taps = []
        for row in range(rows_here + 2):
            if row == 0:
                centre = above
            elif row == rows_here + 1:
                centre = below
            else:
                centre = cells[row - 1, :, part]
            centre = centre.astype(jnp.float32)
            before = jnp.where(place == 0, lefts[row : row + 1], pltpu.roll(centre, 1, 0))
            after = jnp.where(
                place == cols_here - 1, rights[row : row + 1], pltpu.roll(centre, cols_here - 1, 0)
            )
            taps.append((before, centre, after))
        for row in range(rows_here):
            total = None
            for row_tap in range(3):
                for col_tap in range(3):
                    piece = weights[row_tap, col_tap : col_tap + 1, part] * taps[row + row_tap][col_tap]
                    total = piece if total is None else total + piece
            out[pl.ds(row * cols_here, cols_here), part] = total


def grouped(jobs):
    size = -(-len(jobs) // -(-len(jobs) // GROUP))
    return [jobs[at : at + size] for at in range(0, len(jobs), size)]


def lanes_of(head):
    return pl.ds(head * HEAD_DIM, HEAD_DIM)


def rows_at(block):
    return pl.ds(block * PER_BLOCK, PER_BLOCK)


def text_choice(chosen):
    row = lax.axis_index("rows")
    return chosen % 2 == row % 2, chosen // 2 == row // 2


def pick(from_own, own, other, shard, at, part):
    rows = pl.ds(at * shard, shard)
    return jnp.where(from_own, own[rows, part], other[rows, part])


def early_kernel(
    text_ref, q, k, v, both, both_mate, early, early_mate, left, left_mate, right, right_mate,
    sums, peaks_out, totals_out,
):
    shard = both.shape[0] // 4
    heads = q.shape[1] // HEAD_DIM

    def gathered(block, head, which):
        part = lanes_of(head)
        parts = [(k, v)[which][rows_at(block), part]]
        for turn in range(2):
            from_own, from_near = text_choice(text_ref[block, 0, turn])
            for near, side in (
                ((both, both_mate, which), (both, both_mate, 2 + which)),
                ((early, early_mate, which), (left, left_mate, which)),
                ((early, early_mate, 2 + which), (right, right_mate, which)),
            ):
                parts.append(
                    jnp.where(
                        from_near,
                        pick(from_own, near[0], near[1], shard, near[2], part),
                        pick(from_own, side[0], side[1], shard, side[2], part),
                    )
                )
        return jnp.concatenate(parts, axis=0)

    for group in grouped([(block, head) for head in range(heads) for block in range(2)]):
        scores = [
            head_scores(q[rows_at(block), lanes_of(head)], gathered(block, head, 0))
            for block, head in group
        ]
        peaks = [jnp.max(s, axis=1, keepdims=True) * EXP2_SCALE for s in scores]
        weights = [
            jnp.exp2(s * EXP2_SCALE - peak).astype(jnp.bfloat16) for s, peak in zip(scores, peaks)
        ]
        totals = [jnp.sum(w.astype(jnp.float32), axis=1, keepdims=True) for w in weights]
        for w, peak, total, (block, head) in zip(weights, peaks, totals, group):
            sums[rows_at(block), lanes_of(head)] = jnp.dot(
                w, gathered(block, head, 1), preferred_element_type=jnp.float32
            )
            spread = (PER_BLOCK, HEAD_DIM)
            peaks_out[rows_at(block), lanes_of(head)] = jnp.broadcast_to(peak, spread)
            totals_out[rows_at(block), lanes_of(head)] = jnp.broadcast_to(total, spread)


def late_kernel(first_head, reads_ref, pattern_ref, text_ref, q, *refs):
    sums, old_peaks, old_totals, passed, arrived, term = refs[:6]
    near, near_mate, side, side_mate = refs[6:10]
    out = refs[-1]
    row = lax.axis_index("rows")
    across, core = row // 2, row % 2
    shard = near.shape[0] // 2
    half = 2 * PER_BLOCK

    def far_part(block, head, which):
        slot = pattern_ref[block, 0, 0] + pattern_ref[block, 0, 1] - block - 2
        wanted = reads_ref[0, 0, slot]
        owner = wanted // 2
        mate_at = (wanted % 2) * PER_BLOCK + which * half
        far_at = jnp.where(owner % 2 == core, 0, PER_BLOCK) + which * half
        mate_rows = pl.ds(pl.multiple_of(mate_at, PER_BLOCK), PER_BLOCK)
        far_rows = pl.ds(pl.multiple_of(far_at, PER_BLOCK), PER_BLOCK)
        return jnp.where(
            owner // 2 == across,
            passed[mate_rows, lanes_of(first_head + head)],
            arrived[far_rows, lanes_of(head)],
        )

    def gathered(block, head, which):
        part = lanes_of(first_head + head)
        parts = [far_part(block, head, which)]
        for turn in range(2):
            from_own, from_near = text_choice(text_ref[block, 0, turn])
            parts.append(
                jnp.where(
                    from_near,
                    pick(from_own, near, near_mate, shard, which, part),
                    pick(from_own, side, side_mate, shard, which, part),
                )
            )
        return jnp.concatenate(parts, axis=0)

    count = arrived.shape[1] // HEAD_DIM
    for group in grouped([(block, head) for head in range(count) for block in range(2)]):
        scores = [
            head_scores(q[rows_at(block), lanes_of(first_head + head)], gathered(block, head, 0))
            for block, head in group
        ]
        olds = [old_peaks[rows_at(block), lanes_of(first_head + head)] for block, head in group]
        peaks = [
            jnp.maximum(old, jnp.max(s, axis=1, keepdims=True) * EXP2_SCALE)
            for s, old in zip(scores, olds)
        ]
        weights = []
        for s, peak in zip(scores, peaks):
            wide = jnp.concatenate([peak, peak[:, : s.shape[1] - HEAD_DIM]], axis=1)
            weights.append(jnp.exp2(s * EXP2_SCALE - wide).astype(jnp.bfloat16))
        totals = [jnp.sum(w.astype(jnp.float32), axis=1, keepdims=True) for w in weights]
        products = [
            jnp.dot(w, gathered(block, head, 1), preferred_element_type=jnp.float32)
            for w, (block, head) in zip(weights, group)
        ]
        for product, total, old, peak, (block, head) in zip(products, totals, olds, peaks, group):
            rows, part = rows_at(block), lanes_of(first_head + head)
            factor = jnp.exp2(old - peak)
            total = old_totals[rows, part] * factor + total
            summed = sums[rows, part] * factor + product
            out[rows, lanes_of(head)] = summed / total + term[rows, part]


def body(
    q_fresh, k_fresh, v_fresh, k_stale, v_stale, text_k, text_v, conv_w, reads, pattern, text_blocks
):
    rows_here, cols_here, width = q_fresh.shape
    tokens = rows_here * cols_here
    shard = text_k.shape[0]
    swap = [(r, (r + 2) % 4) for r in range(4)]
    mates = [(r, r ^ 1) for r in range(4)]
    in_vmem = pl.BlockSpec(memory_space=pltpu.VMEM)
    in_hbm = pl.BlockSpec(memory_space=pltpu.HBM)
    params = pltpu.CompilerParams(vmem_limit_bytes=VMEM_LIMIT)
    cost = pl.CostEstimate(flops=1 << 20, transcendentals=0, bytes_accessed=1 << 16)

    def after(value, *others):
        return lax.optimization_barrier((value, *others))[0]

    def flat(grid_values):
        return grid_values.reshape(tokens, width)

    def to_mate(values):
        return lax.ppermute(values, "rows", mates)

    def rows_of(*counts):
        shapes = tuple(jax.ShapeDtypeStruct((n, width), jnp.bfloat16) for n in counts)
        return shapes if len(shapes) > 1 else shapes[0]

    def local(kernel, name, shapes, *args, specs=None, scratch=()):
        many = isinstance(shapes, tuple)
        return pl.pallas_call(
            kernel,
            out_shape=shapes,
            in_specs=specs or [in_vmem] * len(args),
            out_specs=(in_vmem,) * len(shapes) if many else in_vmem,
            scratch_shapes=scratch,
            compiler_params=params,
            cost_estimate=cost,
            name=name,
        )(*args)

    chunks = tuple(
        jax.ShapeDtypeStruct((2 * tokens, n * HEAD_DIM), jnp.bfloat16) for n in CHUNK_HEADS
    )
    in_place = [
        pltpu.with_memory_space_constraint(value, pltpu.HBM)
        for value in (flat(k_stale), flat(v_stale), v_fresh, text_k, text_v)
    ]
    stale, beside, diagonal, text = local(
        pack_kernel,
        "pack",
        rows_of(2 * tokens, cols_here, cols_here, 2 * shard),
        *in_place,
        specs=[in_hbm] * 5,
        scratch=[pltpu.SemaphoreType.DMA((6,))],
    )
    forward = [(i, (i + 1) % 4) for i in range(4)]
    backward = [(i, (i + 3) % 4) for i in range(4)]

    near_parts = [lax.ppermute(text, "cols", p) for p in (forward, backward)]
    beside = to_mate(beside)
    diagonal = lax.ppermute(diagonal, "rows", [(1, 2), (2, 1)])
    offer = local(
        offer_kernel,
        "offer",
        rows_of(2 * shard + 8),
        reads,
        text,
        specs=[pl.BlockSpec(memory_space=pltpu.SMEM), in_vmem],
    )
    across = lax.ppermute(offer, "rows", swap)
    passed = to_mate(stale)
    packed = local(
        send_kernel, "send", chunks, after(across, diagonal), stale, passed
    )
    far = [lax.ppermute(chunk, "rows", swap) for chunk in packed]

    both, plus, minus = local(
        join_kernel,
        "join",
        rows_of(4 * shard, 2 * shard + 16, 2 * shard + 16),
        text,
        after(across, packed[0]),
        v_fresh,
        beside,
        diagonal,
    )
    left = lax.ppermute(plus, "cols", forward)
    right = lax.ppermute(minus, "cols", backward)
    early = local(bundle_kernel, "bundle", rows_of(4 * shard), *near_parts)
    early_mate, both_mate = to_mate(early), to_mate(both)
    near_parts[0] = after(near_parts[0], early_mate, both_mate)
    upper, lower = (
        local(bundle_kernel, "pair", rows_of(4 * shard), *pair)
        for pair in ((near_parts[0], left), (near_parts[1], right))
    )
    upper = lax.ppermute(upper, "cols", [(1, 2), (2, 3)])
    lower = lax.ppermute(lower, "cols", [(1, 0), (2, 1)])
    left_mate, right_mate = to_mate(left), to_mate(right)
    sums, peaks, totals = local(
        early_kernel,
        "early",
        (jax.ShapeDtypeStruct((tokens, width), jnp.float32),) * 3,
        text_blocks, flat(q_fresh), flat(k_fresh), flat(v_fresh),
        both, both_mate, early, early_mate, left, left_mate, right, right_mate,
        specs=[pl.BlockSpec(memory_space=pltpu.SMEM)] + [in_vmem] * 11,
    )
    upper, lower = after(upper, sums), after(lower, sums)
    far_side = local(choose_kernel, "choose", rows_of(2 * shard, 2 * shard), upper, lower)
    late = [part for side in far_side for part in (side, to_mate(side))]
    term = local(
        term_kernel,
        "term",
        jax.ShapeDtypeStruct((tokens, width), jnp.float32),
        v_fresh, beside, diagonal, left, right, conv_w,
    )

    out = None
    first_head = 0
    for chunk, head_count in enumerate(CHUNK_HEADS):
        if out is not None:
            far[chunk] = after(far[chunk], out)
        block = pl.BlockSpec(
            (pl.Element(tokens), pl.Element(head_count * HEAD_DIM)),
            lambda i, *_, at=first_head * HEAD_DIM: (0, at),
        )
        out = pl.pallas_call(
            functools.partial(late_kernel, first_head),
            out_shape=jax.ShapeDtypeStruct((tokens, width), jnp.float32),
            grid_spec=pltpu.PrefetchScalarGridSpec(
                num_scalar_prefetch=3,
                grid=(1,),
                in_specs=[in_vmem] * 11 + [in_hbm] * (out is not None),
                out_specs=block,
            ),
            input_output_aliases={14: 0} if out is not None else {},
            compiler_params=params,
            cost_estimate=cost,
            name=f"late{chunk}",
        )(
            reads, pattern, text_blocks, flat(q_fresh), sums, peaks, totals,
            passed, far[chunk], term, *late,
            *([out] if out is not None else []),
        )
        first_head += head_count
    return out.reshape(rows_here, cols_here, width)


def fits(mesh, reads, pattern, text_k):
    sizes = dict(mesh.shape)
    return (
        sizes["rows"] == 4
        and sizes["cols"] == 4
        and reads.shape[-1] == 2
        and pattern.shape[-1] == 2
        and pattern.shape[0] == 2 * sizes["groups"] * 4
        and text_k.shape[0] == sizes["groups"] * 4 * PER_BLOCK
    )


def solution(mesh):
    grid = P(("groups", "rows"), "cols", None)
    text = P(("groups", "rows", "cols"), None)
    in_specs = (grid, grid, grid, grid, grid, text, text, P(), grid, grid, grid)

    def program(*args):
        chosen = body if fits(mesh, args[8], args[9], args[5]) else general_body
        return jax.shard_map(
            chosen, mesh=mesh, in_specs=in_specs, out_specs=grid, check_vma=False
        )(*args)

    return program
```

```python
import functools
import math

import jax
import jax.numpy as jnp
from jax import lax
from jax.experimental import pallas as pl
from jax.experimental.pallas import tpu as pltpu
from jax.sharding import PartitionSpec as P

HEAD_DIM = 128
BLOCK_ROWS = 4
BLOCK_COLS = 32
PER_BLOCK = BLOCK_ROWS * BLOCK_COLS
SCORE_SCALE = 1.0 / math.sqrt(HEAD_DIM)
EXP2_SCALE = SCORE_SCALE * math.log2(math.e)
CHUNK_HEADS = (9, 3)
GROUP = 8
VMEM_LIMIT = 24 * 1024 * 1024


def extended(cells, sides, width):
    for axis, dim in sides:
        count = lax.axis_size(axis)
        ends = count - 1
        head = lax.slice_in_dim(cells, 0, width, axis=dim)
        tail = lax.slice_in_dim(cells, cells.shape[dim] - width, cells.shape[dim], axis=dim)
        cells = jnp.concatenate(
            [
                lax.ppermute(tail, axis, [(i, (i + 1) % count) for i in range(ends)]),
                cells,
                lax.ppermute(head, axis, [((i + 1) % count, i) for i in range(ends)]),
            ],
            axis=dim,
        )
    return cells


def position(v_fresh, conv_w):
    rows_here, cols_here, feature_width = v_fresh.shape
    rims = extended(v_fresh, (("rows", 0), ("cols", 1)), 1)
    position_term = jnp.zeros((rows_here, cols_here, feature_width), jnp.float32)
    for row_tap in range(3):
        for col_tap in range(3):
            position_term = position_term + conv_w[row_tap, col_tap] * rims[
                row_tap : row_tap + rows_here, col_tap : col_tap + cols_here
            ].astype(jnp.float32)
    return position_term


def split_heads(flat_rows):
    return flat_rows.reshape(flat_rows.shape[:-1] + (flat_rows.shape[-1] // HEAD_DIM, HEAD_DIM))


def attend(softmax_state, queries, key_blocks, value_blocks, allowed):
    old_peak, old_total, old_summed = softmax_state
    scores = (
        jnp.einsum(
            "bqhd,nkhd->bhqnk", queries, key_blocks, preferred_element_type=jnp.float32
        )
        * SCORE_SCALE
    )
    scores = jnp.where(allowed[:, None, None, :, None], scores, -1e30)
    new_peak = jnp.maximum(old_peak, jnp.max(scores, axis=(3, 4)))
    weights = jnp.exp(scores - new_peak[:, :, :, None, None]).astype(jnp.bfloat16)
    factor = jnp.exp(old_peak - new_peak)
    new_total = old_total * factor + jnp.sum(weights.astype(jnp.float32), axis=(3, 4))
    product = jnp.einsum(
        "bhqnk,nkhd->bqhd", weights, value_blocks, preferred_element_type=jnp.float32
    )
    new_summed = old_summed * jnp.transpose(factor, (0, 2, 1))[:, :, :, None] + product
    return (new_peak, new_total, new_summed)


def general_body(
    q_fresh, k_fresh, v_fresh, k_stale, v_stale, text_k, text_v, conv_w, reads, pattern, text_blocks
):
    rows_here, cols_here, feature_width = q_fresh.shape
    blocks_here = rows_here // BLOCK_ROWS
    head_count = feature_width // HEAD_DIM

    def as_blocks(grid_values):
        return split_heads(grid_values.reshape(blocks_here, PER_BLOCK, feature_width))

    queries = as_blocks(q_fresh)
    text_keys, text_values = (
        lax.all_gather(text_k, ("rows", "cols"), axis=0, tiled=True),
        lax.all_gather(text_v, ("rows", "cols"), axis=0, tiled=True),
    )
    text_count = text_keys.shape[0] // PER_BLOCK
    text_keys = split_heads(text_keys.reshape(text_count, PER_BLOCK, feature_width))
    text_values = split_heads(text_values.reshape(text_count, PER_BLOCK, feature_width))
    wanted = pattern[:, 0, :]
    fetch_rows = reads[0, 0, :]
    fetch_count = fetch_rows.shape[0]
    slot_count = blocks_here + fetch_count
    slot_mask = jnp.any(
        wanted[:, :, None] == jnp.arange(slot_count, dtype=jnp.int32)[None, None, :], axis=1
    )
    text_mask = jnp.any(
        text_blocks[:, 0, :, None] == jnp.arange(text_count, dtype=jnp.int32)[None, None, :], axis=1
    )
    softmax_state = (
        jnp.full((blocks_here, head_count, PER_BLOCK), -1e30, jnp.float32),
        jnp.zeros((blocks_here, head_count, PER_BLOCK), jnp.float32),
        jnp.zeros((blocks_here, PER_BLOCK, head_count, HEAD_DIM), jnp.float32),
    )
    softmax_state = attend(
        softmax_state,
        queries,
        jnp.concatenate([as_blocks(k_fresh), text_keys], axis=0),
        jnp.concatenate([as_blocks(v_fresh), text_values], axis=0),
        jnp.concatenate([slot_mask[:, :blocks_here], text_mask], axis=1),
    )
    chosen = jnp.where(
        wanted >= blocks_here, fetch_rows[jnp.clip(wanted - blocks_here, 0, fetch_count - 1)], -1
    )
    piece_keys = lax.all_gather(as_blocks(k_stale), "rows", axis=0, tiled=True)
    piece_values = lax.all_gather(as_blocks(v_stale), "rows", axis=0, tiled=True)
    block_rows = jnp.arange(piece_keys.shape[0], dtype=jnp.int32)
    piece_mask = jnp.any(chosen[:, :, None] == block_rows[None, None, :], axis=1)
    softmax_state = attend(softmax_state, queries, piece_keys, piece_values, piece_mask)
    _, final_total, final_summed = softmax_state
    mixed_rows = final_summed / jnp.transpose(final_total, (0, 2, 1))[:, :, :, None]
    attention = mixed_rows.reshape(rows_here, cols_here, feature_width)
    return attention + position(v_fresh, conv_w)


def head_scores(queries, keys):
    return lax.dot_general(
        queries, keys, (((1,), (1,)), ((), ())), preferred_element_type=jnp.float32
    )


def run_copies(copies, sems):
    copies = [pltpu.make_async_copy(*pair, sems.at[i]) for i, pair in enumerate(copies)]
    for copy in copies:
        copy.start()
    for copy in copies:
        copy.wait()


def pack_kernel(k_hbm, v_hbm, cells, text_k, text_v, stale, beside, diagonal, text, sems):
    tokens, shard = k_hbm.shape[0], text_k.shape[0]
    row = lax.axis_index("rows")
    end = cells.shape[0] - 1
    copies = []
    for which, source in enumerate((text_k, text_v)):
        copies.append((source, text.at[pl.ds(which * shard, shard)]))
    for which, source in enumerate((k_hbm, v_hbm)):
        copies.append((source, stale.at[pl.ds(which * tokens, tokens)]))
    copies.append((cells.at[jnp.where(row % 2 == 0, end, 0)], beside))
    copies.append((cells.at[jnp.where(row < 2, end, 0)], diagonal))
    run_copies(copies, sems)


def offer_kernel(reads_ref, text, out):
    both, width = text.shape
    partner = (lax.axis_index("rows") + 2) % 4

    def flag(owner):
        found = 0
        for turn in range(2):
            entry = reads_ref[0, 0, turn]
            found = jnp.where(entry // 2 == owner, entry % 2, found)
        return jnp.full((8, width // 2), found.astype(jnp.float32), jnp.float32)

    flags = [flag(owner) for owner in (partner, partner + 1 - 2 * (partner % 2))]
    out[pl.ds(0, both), :] = text[...]
    out[pl.ds(both, 8), :] = jnp.concatenate(flags, axis=1).astype(out.dtype)


def send_kernel(across, stale, passed, *outs):
    tokens, width = stale.shape[0] // 2, stale.shape[1]

    def block_of(slot):
        lanes = pl.ds(slot * (width // 2), HEAD_DIM)
        flag = jnp.max(across[pl.ds(across.shape[0] - 8, 8), lanes].astype(jnp.float32))
        return jnp.where(flag > 0.5, PER_BLOCK, 0)

    starts = block_of(0), block_of(1)
    first = 0
    for out in outs:
        part = pl.ds(first, out.shape[1])
        first += out.shape[1]
        for which in range(2):
            for slot, source in enumerate((stale, passed)):
                rows = pl.ds(pl.multiple_of(which * tokens + starts[slot], PER_BLOCK), PER_BLOCK)
                at = (2 * which + slot) * PER_BLOCK
                out[pl.ds(at, PER_BLOCK), :] = source[rows, part]


def bundle_kernel(*refs):
    out = refs[-1]
    at = 0
    for ref in refs[:-1]:
        count = ref.shape[0] - ref.shape[0] % 64
        out[pl.ds(at, count), :] = ref[pl.ds(0, count), :]
        at += count


def choose_kernel(upper, lower, first, second):
    upwards = lax.axis_index("cols") >= 2
    half = first.shape[0]
    for at, out in ((0, first), (half, second)):
        rows = pl.ds(at, half)
        out[...] = jnp.where(upwards, upper[rows, :], lower[rows, :])


def above_below(beside, diagonal):
    first_core = lax.axis_index("rows") % 2 == 0
    return (
        jnp.where(first_core, diagonal, beside),
        jnp.where(first_core, beside, diagonal),
    )


def join_kernel(text, across, cells, beside, diagonal, both, plus, minus):
    shard = text.shape[0] // 2
    rows_here, cols_here, width = cells.shape
    above, below = above_below(beside[...], diagonal[...])
    rows = [above] + [cells[i] for i in range(rows_here)] + [below]
    rows = [row.astype(jnp.float32) for row in rows]
    spare = jnp.zeros((16 - len(rows), width), jnp.float32)
    both[pl.ds(0, 2 * shard), :] = text[...]
    both[pl.ds(2 * shard, 2 * shard), :] = across[pl.ds(0, 2 * shard), :]
    for target in (plus, minus):
        target[pl.ds(0, 2 * shard), :] = across[pl.ds(0, 2 * shard), :]
    for target, at in ((plus, cols_here - 1), (minus, 0)):
        edge = jnp.concatenate([row[at : at + 1] for row in rows] + [spare], axis=0)
        target[pl.ds(2 * shard, 16), :] = edge.astype(target.dtype)


def term_kernel(cells, beside, diagonal, left, right, weights, out):
    rows_here, cols_here, width = cells.shape
    col = lax.axis_index("cols")
    edges = pl.ds(left.shape[0] - 16, 16)
    place = lax.broadcasted_iota(jnp.int32, (cols_here, HEAD_DIM), 0)
    for lane in range(width // HEAD_DIM):
        part = pl.ds(lane * HEAD_DIM, HEAD_DIM)
        above, below = above_below(beside[:, part], diagonal[:, part])
        lefts = left[edges, part].astype(jnp.float32)
        rights = right[edges, part].astype(jnp.float32)
        lefts = jnp.where(col > 0, lefts, 0.0)
        rights = jnp.where(col < 3, rights, 0.0)
        taps = []
        for row in range(rows_here + 2):
            if row == 0:
                centre = above
            elif row == rows_here + 1:
                centre = below
            else:
                centre = cells[row - 1, :, part]
            centre = centre.astype(jnp.float32)
            before = jnp.where(place == 0, lefts[row : row + 1], pltpu.roll(centre, 1, 0))
            after = jnp.where(
                place == cols_here - 1, rights[row : row + 1], pltpu.roll(centre, cols_here - 1, 0)
            )
            taps.append((before, centre, after))
        for row in range(rows_here):
            total = None
            for row_tap in range(3):
                for col_tap in range(3):
                    piece = weights[row_tap, col_tap : col_tap + 1, part] * taps[row + row_tap][col_tap]
                    total = piece if total is None else total + piece
            out[pl.ds(row * cols_here, cols_here), part] = total


def grouped(jobs):
    size = -(-len(jobs) // -(-len(jobs) // GROUP))
    return [jobs[at : at + size] for at in range(0, len(jobs), size)]


def lanes_of(head):
    return pl.ds(head * HEAD_DIM, HEAD_DIM)


def rows_at(block):
    return pl.ds(block * PER_BLOCK, PER_BLOCK)


def text_choice(chosen):
    row = lax.axis_index("rows")
    return chosen % 2 == row % 2, chosen // 2 == row // 2


def pick(from_own, own, other, shard, at, part):
    rows = pl.ds(at * shard, shard)
    return jnp.where(from_own, own[rows, part], other[rows, part])


def early_kernel(
    text_ref, q, k, v, both, both_mate, early, early_mate, left, left_mate, right, right_mate,
    sums, peaks_out, totals_out,
):
    shard = both.shape[0] // 4
    heads = q.shape[1] // HEAD_DIM

    def gathered(block, head, which):
        part = lanes_of(head)
        parts = [(k, v)[which][rows_at(block), part]]
        for turn in range(2):
            from_own, from_near = text_choice(text_ref[block, 0, turn])
            for near, side in (
                ((both, both_mate, which), (both, both_mate, 2 + which)),
                ((early, early_mate, which), (left, left_mate, which)),
                ((early, early_mate, 2 + which), (right, right_mate, which)),
            ):
                parts.append(
                    jnp.where(
                        from_near,
                        pick(from_own, near[0], near[1], shard, near[2], part),
                        pick(from_own, side[0], side[1], shard, side[2], part),
                    )
                )
        return jnp.concatenate(parts, axis=0)

    for group in grouped([(block, head) for head in range(heads) for block in range(2)]):
        scores = [
            head_scores(q[rows_at(block), lanes_of(head)], gathered(block, head, 0))
            for block, head in group
        ]
        peaks = [jnp.max(s, axis=1, keepdims=True) * EXP2_SCALE for s in scores]
        weights = [
            jnp.exp2(s * EXP2_SCALE - peak).astype(jnp.bfloat16) for s, peak in zip(scores, peaks)
        ]
        totals = [jnp.sum(w.astype(jnp.float32), axis=1, keepdims=True) for w in weights]
        for w, peak, total, (block, head) in zip(weights, peaks, totals, group):
            sums[rows_at(block), lanes_of(head)] = jnp.dot(
                w, gathered(block, head, 1), preferred_element_type=jnp.float32
            )
            spread = (PER_BLOCK, HEAD_DIM)
            peaks_out[rows_at(block), lanes_of(head)] = jnp.broadcast_to(peak, spread)
            totals_out[rows_at(block), lanes_of(head)] = jnp.broadcast_to(total, spread)


def late_kernel(first_head, reads_ref, pattern_ref, text_ref, q, *refs):
    sums, old_peaks, old_totals, passed, arrived, term = refs[:6]
    near, near_mate, side, side_mate = refs[6:10]
    out = refs[-1]
    row = lax.axis_index("rows")
    across, core = row // 2, row % 2
    shard = near.shape[0] // 2
    half = 2 * PER_BLOCK

    def far_part(block, head, which):
        slot = pattern_ref[block, 0, 0] + pattern_ref[block, 0, 1] - block - 2
        wanted = reads_ref[0, 0, slot]
        owner = wanted // 2
        mate_at = (wanted % 2) * PER_BLOCK + which * half
        far_at = jnp.where(owner % 2 == core, 0, PER_BLOCK) + which * half
        mate_rows = pl.ds(pl.multiple_of(mate_at, PER_BLOCK), PER_BLOCK)
        far_rows = pl.ds(pl.multiple_of(far_at, PER_BLOCK), PER_BLOCK)
        return jnp.where(
            owner // 2 == across,
            passed[mate_rows, lanes_of(first_head + head)],
            arrived[far_rows, lanes_of(head)],
        )

    def gathered(block, head, which):
        part = lanes_of(first_head + head)
        parts = [far_part(block, head, which)]
        for turn in range(2):
            from_own, from_near = text_choice(text_ref[block, 0, turn])
            parts.append(
                jnp.where(
                    from_near,
                    pick(from_own, near, near_mate, shard, which, part),
                    pick(from_own, side, side_mate, shard, which, part),
                )
            )
        return jnp.concatenate(parts, axis=0)

    count = arrived.shape[1] // HEAD_DIM
    for group in grouped([(block, head) for head in range(count) for block in range(2)]):
        scores = [
            head_scores(q[rows_at(block), lanes_of(first_head + head)], gathered(block, head, 0))
            for block, head in group
        ]
        olds = [old_peaks[rows_at(block), lanes_of(first_head + head)] for block, head in group]
        peaks = [
            jnp.maximum(old, jnp.max(s, axis=1, keepdims=True) * EXP2_SCALE)
            for s, old in zip(scores, olds)
        ]
        weights = []
        for s, peak in zip(scores, peaks):
            wide = jnp.concatenate([peak, peak[:, : s.shape[1] - HEAD_DIM]], axis=1)
            weights.append(jnp.exp2(s * EXP2_SCALE - wide).astype(jnp.bfloat16))
        totals = [jnp.sum(w.astype(jnp.float32), axis=1, keepdims=True) for w in weights]
        products = [
            jnp.dot(w, gathered(block, head, 1), preferred_element_type=jnp.float32)
            for w, (block, head) in zip(weights, group)
        ]
        for product, total, old, peak, (block, head) in zip(products, totals, olds, peaks, group):
            rows, part = rows_at(block), lanes_of(first_head + head)
            factor = jnp.exp2(old - peak)
            total = old_totals[rows, part] * factor + total
            summed = sums[rows, part] * factor + product
            out[rows, lanes_of(head)] = summed / total + term[rows, part]


def body(
    q_fresh, k_fresh, v_fresh, k_stale, v_stale, text_k, text_v, conv_w, reads, pattern, text_blocks
):
    rows_here, cols_here, width = q_fresh.shape
    tokens = rows_here * cols_here
    shard = text_k.shape[0]
    swap = [(r, (r + 2) % 4) for r in range(4)]
    mates = [(r, r ^ 1) for r in range(4)]
    in_vmem = pl.BlockSpec(memory_space=pltpu.VMEM)
    in_hbm = pl.BlockSpec(memory_space=pltpu.HBM)
    params = pltpu.CompilerParams(vmem_limit_bytes=VMEM_LIMIT)
    cost = pl.CostEstimate(flops=1 << 20, transcendentals=0, bytes_accessed=1 << 16)

    def after(value, *others):
        return lax.optimization_barrier((value, *others))[0]

    def flat(grid_values):
        return grid_values.reshape(tokens, width)

    def to_mate(values):
        return lax.ppermute(values, "rows", mates)

    def rows_of(*counts):
        shapes = tuple(jax.ShapeDtypeStruct((n, width), jnp.bfloat16) for n in counts)
        return shapes if len(shapes) > 1 else shapes[0]

    def local(kernel, name, shapes, *args, specs=None, scratch=()):
        many = isinstance(shapes, tuple)
        return pl.pallas_call(
            kernel,
            out_shape=shapes,
            in_specs=specs or [in_vmem] * len(args),
            out_specs=(in_vmem,) * len(shapes) if many else in_vmem,
            scratch_shapes=scratch,
            compiler_params=params,
            cost_estimate=cost,
            name=name,
        )(*args)

    chunks = tuple(
        jax.ShapeDtypeStruct((2 * tokens, n * HEAD_DIM), jnp.bfloat16) for n in CHUNK_HEADS
    )
    in_place = [
        pltpu.with_memory_space_constraint(value, pltpu.HBM)
        for value in (flat(k_stale), flat(v_stale), v_fresh, text_k, text_v)
    ]
    stale, beside, diagonal, text = local(
        pack_kernel,
        "pack",
        rows_of(2 * tokens, cols_here, cols_here, 2 * shard),
        *in_place,
        specs=[in_hbm] * 5,
        scratch=[pltpu.SemaphoreType.DMA((6,))],
    )
    forward = [(i, (i + 1) % 4) for i in range(4)]
    backward = [(i, (i + 3) % 4) for i in range(4)]

    near_parts = [lax.ppermute(text, "cols", p) for p in (forward, backward)]
    beside = to_mate(beside)
    diagonal = lax.ppermute(diagonal, "rows", [(1, 2), (2, 1)])
    offer = local(
        offer_kernel,
        "offer",
        rows_of(2 * shard + 8),
        reads,
        text,
        specs=[pl.BlockSpec(memory_space=pltpu.SMEM), in_vmem],
    )
    across = lax.ppermute(offer, "rows", swap)
    passed = to_mate(stale)
    packed = local(
        send_kernel, "send", chunks, after(across, diagonal), stale, passed
    )
    far = [lax.ppermute(chunk, "rows", swap) for chunk in packed]

    both, plus, minus = local(
        join_kernel,
        "join",
        rows_of(4 * shard, 2 * shard + 16, 2 * shard + 16),
        text,
        after(across, packed[0]),
        v_fresh,
        beside,
        diagonal,
    )
    left = lax.ppermute(plus, "cols", forward)
    right = lax.ppermute(minus, "cols", backward)
    early = local(bundle_kernel, "bundle", rows_of(4 * shard), *near_parts)
    early_mate, both_mate = to_mate(early), to_mate(both)
    near_parts[0] = after(near_parts[0], early_mate, both_mate)
    upper, lower = (
        local(bundle_kernel, "pair", rows_of(4 * shard), *pair)
        for pair in ((near_parts[0], left), (near_parts[1], right))
    )
    upper = lax.ppermute(upper, "cols", [(1, 2), (2, 3)])
    lower = lax.ppermute(lower, "cols", [(1, 0), (2, 1)])
    left_mate, right_mate = to_mate(left), to_mate(right)
    sums, peaks, totals = local(
        early_kernel,
        "early",
        (jax.ShapeDtypeStruct((tokens, width), jnp.float32),) * 3,
        text_blocks, flat(q_fresh), flat(k_fresh), flat(v_fresh),
        both, both_mate, early, early_mate, left, left_mate, right, right_mate,
        specs=[pl.BlockSpec(memory_space=pltpu.SMEM)] + [in_vmem] * 11,
    )
    upper, lower = after(upper, sums), after(lower, sums)
    far_side = local(choose_kernel, "choose", rows_of(2 * shard, 2 * shard), upper, lower)
    late = [part for side in far_side for part in (side, to_mate(side))]
    term = local(
        term_kernel,
        "term",
        jax.ShapeDtypeStruct((tokens, width), jnp.float32),
        v_fresh, beside, diagonal, left, right, conv_w,
    )

    out = None
    first_head = 0
    for chunk, head_count in enumerate(CHUNK_HEADS):
        if out is not None:
            far[chunk] = after(far[chunk], out)
        block = pl.BlockSpec(
            (pl.Element(tokens), pl.Element(head_count * HEAD_DIM)),
            lambda i, *_, at=first_head * HEAD_DIM: (0, at),
        )
        out = pl.pallas_call(
            functools.partial(late_kernel, first_head),
            out_shape=jax.ShapeDtypeStruct((tokens, width), jnp.float32),
            grid_spec=pltpu.PrefetchScalarGridSpec(
                num_scalar_prefetch=3,
                grid=(1,),
                in_specs=[in_vmem] * 11 + [in_hbm] * (out is not None),
                out_specs=block,
            ),
            input_output_aliases={14: 0} if out is not None else {},
            compiler_params=params,
            cost_estimate=cost,
            name=f"late{chunk}",
        )(
            reads, pattern, text_blocks, flat(q_fresh), sums, peaks, totals,
            passed, far[chunk], term, *late,
            *([out] if out is not None else []),
        )
        first_head += head_count
    return out.reshape(rows_here, cols_here, width)


def fits(mesh, reads, pattern, text_k):
    sizes = dict(mesh.shape)
    return (
        sizes["rows"] == 4
        and sizes["cols"] == 4
        and reads.shape[-1] == 2
        and pattern.shape[-1] == 2
        and pattern.shape[0] == 2 * sizes["groups"] * 4
        and text_k.shape[0] == sizes["groups"] * 4 * PER_BLOCK
    )


def solution(mesh):
    grid = P(("groups", "rows"), "cols", None)
    text = P(("groups", "rows", "cols"), None)
    in_specs = (grid, grid, grid, grid, grid, text, text, P(), grid, grid, grid)

    def program(*args):
        chosen = body if fits(mesh, args[8], args[9], args[5]) else general_body
        return jax.shard_map(
            chosen, mesh=mesh, in_specs=in_specs, out_specs=grid, check_vma=False
        )(*args)

    return program
```

```python
import functools
import math

import jax
import jax.numpy as jnp
from jax import lax
from jax.experimental import pallas as pl
from jax.experimental.pallas import tpu as pltpu
from jax.sharding import PartitionSpec as P

HEAD_DIM = 128
BLOCK_ROWS = 4
BLOCK_COLS = 32
PER_BLOCK = BLOCK_ROWS * BLOCK_COLS
SCORE_SCALE = 1.0 / math.sqrt(HEAD_DIM)
EXP2_SCALE = SCORE_SCALE * math.log2(math.e)
CHUNK_HEADS = (9, 3)
GROUP = 8
VMEM_LIMIT = 24 * 1024 * 1024


def extended(cells, sides, width):
    for axis, dim in sides:
        count = lax.axis_size(axis)
        ends = count - 1
        head = lax.slice_in_dim(cells, 0, width, axis=dim)
        tail = lax.slice_in_dim(cells, cells.shape[dim] - width, cells.shape[dim], axis=dim)
        cells = jnp.concatenate(
            [
                lax.ppermute(tail, axis, [(i, (i + 1) % count) for i in range(ends)]),
                cells,
                lax.ppermute(head, axis, [((i + 1) % count, i) for i in range(ends)]),
            ],
            axis=dim,
        )
    return cells


def position(v_fresh, conv_w):
    rows_here, cols_here, feature_width = v_fresh.shape
    rims = extended(v_fresh, (("rows", 0), ("cols", 1)), 1)
    position_term = jnp.zeros((rows_here, cols_here, feature_width), jnp.float32)
    for row_tap in range(3):
        for col_tap in range(3):
            position_term = position_term + conv_w[row_tap, col_tap] * rims[
                row_tap : row_tap + rows_here, col_tap : col_tap + cols_here
            ].astype(jnp.float32)
    return position_term


def split_heads(flat_rows):
    return flat_rows.reshape(flat_rows.shape[:-1] + (flat_rows.shape[-1] // HEAD_DIM, HEAD_DIM))


def attend(softmax_state, queries, key_blocks, value_blocks, allowed):
    old_peak, old_total, old_summed = softmax_state
    scores = (
        jnp.einsum(
            "bqhd,nkhd->bhqnk", queries, key_blocks, preferred_element_type=jnp.float32
        )
        * SCORE_SCALE
    )
    scores = jnp.where(allowed[:, None, None, :, None], scores, -1e30)
    new_peak = jnp.maximum(old_peak, jnp.max(scores, axis=(3, 4)))
    weights = jnp.exp(scores - new_peak[:, :, :, None, None]).astype(jnp.bfloat16)
    factor = jnp.exp(old_peak - new_peak)
    new_total = old_total * factor + jnp.sum(weights.astype(jnp.float32), axis=(3, 4))
    product = jnp.einsum(
        "bhqnk,nkhd->bqhd", weights, value_blocks, preferred_element_type=jnp.float32
    )
    new_summed = old_summed * jnp.transpose(factor, (0, 2, 1))[:, :, :, None] + product
    return (new_peak, new_total, new_summed)


def general_body(
    q_fresh, k_fresh, v_fresh, k_stale, v_stale, text_k, text_v, conv_w, reads, pattern, text_blocks
):
    rows_here, cols_here, feature_width = q_fresh.shape
    blocks_here = rows_here // BLOCK_ROWS
    head_count = feature_width // HEAD_DIM

    def as_blocks(grid_values):
        return split_heads(grid_values.reshape(blocks_here, PER_BLOCK, feature_width))

    queries = as_blocks(q_fresh)
    text_keys, text_values = (
        lax.all_gather(text_k, ("rows", "cols"), axis=0, tiled=True),
        lax.all_gather(text_v, ("rows", "cols"), axis=0, tiled=True),
    )
    text_count = text_keys.shape[0] // PER_BLOCK
    text_keys = split_heads(text_keys.reshape(text_count, PER_BLOCK, feature_width))
    text_values = split_heads(text_values.reshape(text_count, PER_BLOCK, feature_width))
    wanted = pattern[:, 0, :]
    fetch_rows = reads[0, 0, :]
    fetch_count = fetch_rows.shape[0]
    slot_count = blocks_here + fetch_count
    slot_mask = jnp.any(
        wanted[:, :, None] == jnp.arange(slot_count, dtype=jnp.int32)[None, None, :], axis=1
    )
    text_mask = jnp.any(
        text_blocks[:, 0, :, None] == jnp.arange(text_count, dtype=jnp.int32)[None, None, :], axis=1
    )
    softmax_state = (
        jnp.full((blocks_here, head_count, PER_BLOCK), -1e30, jnp.float32),
        jnp.zeros((blocks_here, head_count, PER_BLOCK), jnp.float32),
        jnp.zeros((blocks_here, PER_BLOCK, head_count, HEAD_DIM), jnp.float32),
    )
    softmax_state = attend(
        softmax_state,
        queries,
        jnp.concatenate([as_blocks(k_fresh), text_keys], axis=0),
        jnp.concatenate([as_blocks(v_fresh), text_values], axis=0),
        jnp.concatenate([slot_mask[:, :blocks_here], text_mask], axis=1),
    )
    chosen = jnp.where(
        wanted >= blocks_here, fetch_rows[jnp.clip(wanted - blocks_here, 0, fetch_count - 1)], -1
    )
    piece_keys = lax.all_gather(as_blocks(k_stale), "rows", axis=0, tiled=True)
    piece_values = lax.all_gather(as_blocks(v_stale), "rows", axis=0, tiled=True)
    block_rows = jnp.arange(piece_keys.shape[0], dtype=jnp.int32)
    piece_mask = jnp.any(chosen[:, :, None] == block_rows[None, None, :], axis=1)
    softmax_state = attend(softmax_state, queries, piece_keys, piece_values, piece_mask)
    _, final_total, final_summed = softmax_state
    mixed_rows = final_summed / jnp.transpose(final_total, (0, 2, 1))[:, :, :, None]
    attention = mixed_rows.reshape(rows_here, cols_here, feature_width)
    return attention + position(v_fresh, conv_w)


def head_scores(queries, keys):
    return lax.dot_general(
        queries, keys, (((1,), (1,)), ((), ())), preferred_element_type=jnp.float32
    )


def run_copies(copies, sems):
    copies = [pltpu.make_async_copy(*pair, sems.at[i]) for i, pair in enumerate(copies)]
    for copy in copies:
        copy.start()
    for copy in copies:
        copy.wait()


def pack_kernel(k_hbm, v_hbm, cells, text_k, text_v, stale, beside, diagonal, text, sems):
    tokens, shard = k_hbm.shape[0], text_k.shape[0]
    row = lax.axis_index("rows")
    end = cells.shape[0] - 1
    copies = []
    for which, source in enumerate((text_k, text_v)):
        copies.append((source, text.at[pl.ds(which * shard, shard)]))
    for which, source in enumerate((k_hbm, v_hbm)):
        copies.append((source, stale.at[pl.ds(which * tokens, tokens)]))
    copies.append((cells.at[jnp.where(row % 2 == 0, end, 0)], beside))
    copies.append((cells.at[jnp.where(row < 2, end, 0)], diagonal))
    run_copies(copies, sems)


def offer_kernel(reads_ref, text, out):
    both, width = text.shape
    partner = (lax.axis_index("rows") + 2) % 4

    def flag(owner):
        found = 0
        for turn in range(2):
            entry = reads_ref[0, 0, turn]
            found = jnp.where(entry // 2 == owner, entry % 2, found)
        return jnp.full((8, width // 2), found.astype(jnp.float32), jnp.float32)

    flags = [flag(owner) for owner in (partner, partner + 1 - 2 * (partner % 2))]
    out[pl.ds(0, both), :] = text[...]
    out[pl.ds(both, 8), :] = jnp.concatenate(flags, axis=1).astype(out.dtype)


def send_kernel(across, stale, passed, *outs):
    tokens, width = stale.shape[0] // 2, stale.shape[1]

    def block_of(slot):
        lanes = pl.ds(slot * (width // 2), HEAD_DIM)
        flag = jnp.max(across[pl.ds(across.shape[0] - 8, 8), lanes].astype(jnp.float32))
        return jnp.where(flag > 0.5, PER_BLOCK, 0)

    starts = block_of(0), block_of(1)
    first = 0
    for out in outs:
        part = pl.ds(first, out.shape[1])
        first += out.shape[1]
        for which in range(2):
            for slot, source in enumerate((stale, passed)):
                rows = pl.ds(pl.multiple_of(which * tokens + starts[slot], PER_BLOCK), PER_BLOCK)
                at = (2 * which + slot) * PER_BLOCK
                out[pl.ds(at, PER_BLOCK), :] = source[rows, part]


def bundle_kernel(*refs):
    out = refs[-1]
    at = 0
    for ref in refs[:-1]:
        count = ref.shape[0] - ref.shape[0] % 64
        out[pl.ds(at, count), :] = ref[pl.ds(0, count), :]
        at += count


def choose_kernel(upper, lower, first, second):
    upwards = lax.axis_index("cols") >= 2
    half = first.shape[0]
    for at, out in ((0, first), (half, second)):
        rows = pl.ds(at, half)
        out[...] = jnp.where(upwards, upper[rows, :], lower[rows, :])


def above_below(beside, diagonal):
    first_core = lax.axis_index("rows") % 2 == 0
    return (
        jnp.where(first_core, diagonal, beside),
        jnp.where(first_core, beside, diagonal),
    )


def join_kernel(text, across, cells, beside, diagonal, both, plus, minus):
    shard = text.shape[0] // 2
    rows_here, cols_here, width = cells.shape
    above, below = above_below(beside[...], diagonal[...])
    rows = [above] + [cells[i] for i in range(rows_here)] + [below]
    rows = [row.astype(jnp.float32) for row in rows]
    spare = jnp.zeros((16 - len(rows), width), jnp.float32)
    both[pl.ds(0, 2 * shard), :] = text[...]
    both[pl.ds(2 * shard, 2 * shard), :] = across[pl.ds(0, 2 * shard), :]
    for target in (plus, minus):
        target[pl.ds(0, 2 * shard), :] = across[pl.ds(0, 2 * shard), :]
    for target, at in ((plus, cols_here - 1), (minus, 0)):
        edge = jnp.concatenate([row[at : at + 1] for row in rows] + [spare], axis=0)
        target[pl.ds(2 * shard, 16), :] = edge.astype(target.dtype)


def term_kernel(cells, beside, diagonal, left, right, weights, out):
    rows_here, cols_here, width = cells.shape
    col = lax.axis_index("cols")
    edges = pl.ds(left.shape[0] - 16, 16)
    place = lax.broadcasted_iota(jnp.int32, (cols_here, HEAD_DIM), 0)
    for lane in range(width // HEAD_DIM):
        part = pl.ds(lane * HEAD_DIM, HEAD_DIM)
        above, below = above_below(beside[:, part], diagonal[:, part])
        lefts = left[edges, part].astype(jnp.float32)
        rights = right[edges, part].astype(jnp.float32)
        lefts = jnp.where(col > 0, lefts, 0.0)
        rights = jnp.where(col < 3, rights, 0.0)
        taps = []
        for row in range(rows_here + 2):
            if row == 0:
                centre = above
            elif row == rows_here + 1:
                centre = below
            else:
                centre = cells[row - 1, :, part]
            centre = centre.astype(jnp.float32)
            before = jnp.where(place == 0, lefts[row : row + 1], pltpu.roll(centre, 1, 0))
            after = jnp.where(
                place == cols_here - 1, rights[row : row + 1], pltpu.roll(centre, cols_here - 1, 0)
            )
            taps.append((before, centre, after))
        for row in range(rows_here):
            total = None
            for row_tap in range(3):
                for col_tap in range(3):
                    piece = weights[row_tap, col_tap : col_tap + 1, part] * taps[row + row_tap][col_tap]
                    total = piece if total is None else total + piece
            out[pl.ds(row * cols_here, cols_here), part] = total


def grouped(jobs):
    size = -(-len(jobs) // -(-len(jobs) // GROUP))
    return [jobs[at : at + size] for at in range(0, len(jobs), size)]


def lanes_of(head):
    return pl.ds(head * HEAD_DIM, HEAD_DIM)


def rows_at(block):
    return pl.ds(block * PER_BLOCK, PER_BLOCK)


def text_choice(chosen):
    row = lax.axis_index("rows")
    return chosen % 2 == row % 2, chosen // 2 == row // 2


def pick(from_own, own, other, shard, at, part):
    rows = pl.ds(at * shard, shard)
    return jnp.where(from_own, own[rows, part], other[rows, part])


def early_kernel(
    text_ref, q, k, v, both, both_mate, early, early_mate, left, left_mate, right, right_mate,
    sums, peaks_out, totals_out,
):
    shard = both.shape[0] // 4
    heads = q.shape[1] // HEAD_DIM

    def gathered(block, head, which):
        part = lanes_of(head)
        parts = [(k, v)[which][rows_at(block), part]]
        for turn in range(2):
            from_own, from_near = text_choice(text_ref[block, 0, turn])
            for near, side in (
                ((both, both_mate, which), (both, both_mate, 2 + which)),
                ((early, early_mate, which), (left, left_mate, which)),
                ((early, early_mate, 2 + which), (right, right_mate, which)),
            ):
                parts.append(
                    jnp.where(
                        from_near,
                        pick(from_own, near[0], near[1], shard, near[2], part),
                        pick(from_own, side[0], side[1], shard, side[2], part),
                    )
                )
        return jnp.concatenate(parts, axis=0)

    for group in grouped([(block, head) for head in range(heads) for block in range(2)]):
        scores = [
            head_scores(q[rows_at(block), lanes_of(head)], gathered(block, head, 0))
            for block, head in group
        ]
        peaks = [jnp.max(s, axis=1, keepdims=True) * EXP2_SCALE for s in scores]
        weights = [
            jnp.exp2(s * EXP2_SCALE - peak).astype(jnp.bfloat16) for s, peak in zip(scores, peaks)
        ]
        totals = [jnp.sum(w.astype(jnp.float32), axis=1, keepdims=True) for w in weights]
        for w, peak, total, (block, head) in zip(weights, peaks, totals, group):
            sums[rows_at(block), lanes_of(head)] = jnp.dot(
                w, gathered(block, head, 1), preferred_element_type=jnp.float32
            )
            spread = (PER_BLOCK, HEAD_DIM)
            peaks_out[rows_at(block), lanes_of(head)] = jnp.broadcast_to(peak, spread)
            totals_out[rows_at(block), lanes_of(head)] = jnp.broadcast_to(total, spread)


def late_kernel(first_head, reads_ref, pattern_ref, text_ref, q, *refs):
    sums, old_peaks, old_totals, passed, arrived, term = refs[:6]
    near, near_mate, side, side_mate = refs[6:10]
    target, out, sems = refs[-3:]
    copies = []
    row = lax.axis_index("rows")
    across, core = row // 2, row % 2
    shard = near.shape[0] // 2
    half = 2 * PER_BLOCK

    def far_part(block, head, which):
        slot = pattern_ref[block, 0, 0] + pattern_ref[block, 0, 1] - block - 2
        wanted = reads_ref[0, 0, slot]
        owner = wanted // 2
        mate_at = (wanted % 2) * PER_BLOCK + which * half
        far_at = jnp.where(owner % 2 == core, 0, PER_BLOCK) + which * half
        mate_rows = pl.ds(pl.multiple_of(mate_at, PER_BLOCK), PER_BLOCK)
        far_rows = pl.ds(pl.multiple_of(far_at, PER_BLOCK), PER_BLOCK)
        return jnp.where(
            owner // 2 == across,
            passed[mate_rows, lanes_of(first_head + head)],
            arrived[far_rows, lanes_of(head)],
        )

    def gathered(block, head, which):
        part = lanes_of(first_head + head)
        parts = [far_part(block, head, which)]
        for turn in range(2):
            from_own, from_near = text_choice(text_ref[block, 0, turn])
            parts.append(
                jnp.where(
                    from_near,
                    pick(from_own, near, near_mate, shard, which, part),
                    pick(from_own, side, side_mate, shard, which, part),
                )
            )
        return jnp.concatenate(parts, axis=0)

    count = arrived.shape[1] // HEAD_DIM
    for group in grouped([(block, head) for head in range(count) for block in range(2)]):
        scores = [
            head_scores(q[rows_at(block), lanes_of(first_head + head)], gathered(block, head, 0))
            for block, head in group
        ]
        olds = [old_peaks[rows_at(block), lanes_of(first_head + head)] for block, head in group]
        peaks = [
            jnp.maximum(old, jnp.max(s, axis=1, keepdims=True) * EXP2_SCALE)
            for s, old in zip(scores, olds)
        ]
        weights = []
        for s, peak in zip(scores, peaks):
            wide = jnp.concatenate([peak, peak[:, : s.shape[1] - HEAD_DIM]], axis=1)
            weights.append(jnp.exp2(s * EXP2_SCALE - wide).astype(jnp.bfloat16))
        totals = [jnp.sum(w.astype(jnp.float32), axis=1, keepdims=True) for w in weights]
        products = [
            jnp.dot(w, gathered(block, head, 1), preferred_element_type=jnp.float32)
            for w, (block, head) in zip(weights, group)
        ]
        for product, total, old, peak, (block, head) in zip(products, totals, olds, peaks, group):
            rows, part = rows_at(block), lanes_of(first_head + head)
            factor = jnp.exp2(old - peak)
            total = old_totals[rows, part] * factor + total
            summed = sums[rows, part] * factor + product
            out[rows, lanes_of(head)] = summed / total + term[rows, part]
        first, width = group[0][1], (group[-1][1] + 1 - group[0][1]) * HEAD_DIM
        copies.append(
            pltpu.make_async_copy(
                out.at[:, pl.ds(first * HEAD_DIM, width)],
                target.at[:, pl.ds((first_head + first) * HEAD_DIM, width)],
                sems.at[len(copies)],
            )
        )
        copies[-1].start()
    for copy in copies:
        copy.wait()


def body(
    q_fresh, k_fresh, v_fresh, k_stale, v_stale, text_k, text_v, conv_w, reads, pattern, text_blocks
):
    rows_here, cols_here, width = q_fresh.shape
    tokens = rows_here * cols_here
    shard = text_k.shape[0]
    swap = [(r, (r + 2) % 4) for r in range(4)]
    mates = [(r, r ^ 1) for r in range(4)]
    in_vmem = pl.BlockSpec(memory_space=pltpu.VMEM)
    in_hbm = pl.BlockSpec(memory_space=pltpu.HBM)
    params = pltpu.CompilerParams(vmem_limit_bytes=VMEM_LIMIT)
    cost = pl.CostEstimate(flops=1 << 20, transcendentals=0, bytes_accessed=1 << 16)

    def after(value, *others):
        return lax.optimization_barrier((value, *others))[0]

    def flat(grid_values):
        return grid_values.reshape(tokens, width)

    def to_mate(values):
        return lax.ppermute(values, "rows", mates)

    def rows_of(*counts):
        shapes = tuple(jax.ShapeDtypeStruct((n, width), jnp.bfloat16) for n in counts)
        return shapes if len(shapes) > 1 else shapes[0]

    def local(kernel, name, shapes, *args, specs=None, scratch=()):
        many = isinstance(shapes, tuple)
        return pl.pallas_call(
            kernel,
            out_shape=shapes,
            in_specs=specs or [in_vmem] * len(args),
            out_specs=(in_vmem,) * len(shapes) if many else in_vmem,
            scratch_shapes=scratch,
            compiler_params=params,
            cost_estimate=cost,
            name=name,
        )(*args)

    chunks = tuple(
        jax.ShapeDtypeStruct((2 * tokens, n * HEAD_DIM), jnp.bfloat16) for n in CHUNK_HEADS
    )
    in_place = [
        pltpu.with_memory_space_constraint(value, pltpu.HBM)
        for value in (flat(k_stale), flat(v_stale), v_fresh, text_k, text_v)
    ]
    stale, beside, diagonal, text = local(
        pack_kernel,
        "pack",
        rows_of(2 * tokens, cols_here, cols_here, 2 * shard),
        *in_place,
        specs=[in_hbm] * 5,
        scratch=[pltpu.SemaphoreType.DMA((6,))],
    )
    forward = [(i, (i + 1) % 4) for i in range(4)]
    backward = [(i, (i + 3) % 4) for i in range(4)]

    near_parts = [lax.ppermute(text, "cols", p) for p in (forward, backward)]
    beside = to_mate(beside)
    diagonal = lax.ppermute(diagonal, "rows", [(1, 2), (2, 1)])
    offer = local(
        offer_kernel,
        "offer",
        rows_of(2 * shard + 8),
        reads,
        text,
        specs=[pl.BlockSpec(memory_space=pltpu.SMEM), in_vmem],
    )
    across = lax.ppermute(offer, "rows", swap)
    passed = to_mate(stale)
    packed = local(
        send_kernel, "send", chunks, after(across, diagonal), stale, passed
    )
    far = [lax.ppermute(chunk, "rows", swap) for chunk in packed]

    both, plus, minus = local(
        join_kernel,
        "join",
        rows_of(4 * shard, 2 * shard + 16, 2 * shard + 16),
        text,
        after(across, packed[0]),
        v_fresh,
        beside,
        diagonal,
    )
    left = lax.ppermute(plus, "cols", forward)
    right = lax.ppermute(minus, "cols", backward)
    early = local(bundle_kernel, "bundle", rows_of(4 * shard), *near_parts)
    early_mate, both_mate = to_mate(early), to_mate(both)
    near_parts[0] = after(near_parts[0], early_mate, both_mate)
    upper, lower = (
        local(bundle_kernel, "pair", rows_of(4 * shard), *pair)
        for pair in ((near_parts[0], left), (near_parts[1], right))
    )
    upper = lax.ppermute(upper, "cols", [(1, 2), (2, 3)])
    lower = lax.ppermute(lower, "cols", [(1, 0), (2, 1)])
    left_mate, right_mate = to_mate(left), to_mate(right)
    sums, peaks, totals = local(
        early_kernel,
        "early",
        (jax.ShapeDtypeStruct((tokens, width), jnp.float32),) * 3,
        text_blocks, flat(q_fresh), flat(k_fresh), flat(v_fresh),
        both, both_mate, early, early_mate, left, left_mate, right, right_mate,
        specs=[pl.BlockSpec(memory_space=pltpu.SMEM)] + [in_vmem] * 11,
    )
    upper, lower = after(upper, sums), after(lower, sums)
    far_side = local(choose_kernel, "choose", rows_of(2 * shard, 2 * shard), upper, lower)
    late = [part for side in far_side for part in (side, to_mate(side))]
    term = local(
        term_kernel,
        "term",
        jax.ShapeDtypeStruct((tokens, width), jnp.float32),
        v_fresh, beside, diagonal, left, right, conv_w,
    )

    out = None
    first_head = 0
    for chunk, head_count in enumerate(CHUNK_HEADS):
        if out is not None:
            far[chunk] = after(far[chunk], out)
        out = pl.pallas_call(
            functools.partial(late_kernel, first_head),
            out_shape=jax.ShapeDtypeStruct((tokens, width), jnp.float32),
            grid_spec=pltpu.PrefetchScalarGridSpec(
                num_scalar_prefetch=3,
                grid=(1,),
                in_specs=[in_vmem] * 11 + [in_hbm] * (out is not None),
                out_specs=in_hbm,
                scratch_shapes=[
                    pltpu.VMEM((tokens, head_count * HEAD_DIM), jnp.float32),
                    pltpu.SemaphoreType.DMA((4,)),
                ],
            ),
            input_output_aliases={14: 0} if out is not None else {},
            compiler_params=params,
            cost_estimate=cost,
            name=f"late{chunk}",
        )(
            reads, pattern, text_blocks, flat(q_fresh), sums, peaks, totals,
            passed, far[chunk], term, *late,
            *([out] if out is not None else []),
        )
        first_head += head_count
    return out.reshape(rows_here, cols_here, width)


def fits(mesh, reads, pattern, text_k):
    sizes = dict(mesh.shape)
    return (
        sizes["rows"] == 4
        and sizes["cols"] == 4
        and reads.shape[-1] == 2
        and pattern.shape[-1] == 2
        and pattern.shape[0] == 2 * sizes["groups"] * 4
        and text_k.shape[0] == sizes["groups"] * 4 * PER_BLOCK
    )


def solution(mesh):
    grid = P(("groups", "rows"), "cols", None)
    text = P(("groups", "rows", "cols"), None)
    in_specs = (grid, grid, grid, grid, grid, text, text, P(), grid, grid, grid)

    def program(*args):
        chosen = body if fits(mesh, args[8], args[9], args[5]) else general_body
        return jax.shard_map(
            chosen, mesh=mesh, in_specs=in_specs, out_specs=grid, check_vma=False
        )(*args)

    return program
```

```python
import functools
import math

import jax
import jax.numpy as jnp
from jax import lax
from jax.experimental import pallas as pl
from jax.experimental.pallas import tpu as pltpu
from jax.sharding import PartitionSpec as P

HEAD_DIM = 128
BLOCK_ROWS = 4
BLOCK_COLS = 32
PER_BLOCK = BLOCK_ROWS * BLOCK_COLS
SCORE_SCALE = 1.0 / math.sqrt(HEAD_DIM)
EXP2_SCALE = SCORE_SCALE * math.log2(math.e)
CHUNK_HEADS = (9, 3)
GROUP = 20
VMEM_LIMIT = 24 * 1024 * 1024


def extended(cells, sides, width):
    for axis, dim in sides:
        count = lax.axis_size(axis)
        ends = count - 1
        head = lax.slice_in_dim(cells, 0, width, axis=dim)
        tail = lax.slice_in_dim(cells, cells.shape[dim] - width, cells.shape[dim], axis=dim)
        cells = jnp.concatenate(
            [
                lax.ppermute(tail, axis, [(i, (i + 1) % count) for i in range(ends)]),
                cells,
                lax.ppermute(head, axis, [((i + 1) % count, i) for i in range(ends)]),
            ],
            axis=dim,
        )
    return cells


def position(v_fresh, conv_w):
    rows_here, cols_here, feature_width = v_fresh.shape
    rims = extended(v_fresh, (("rows", 0), ("cols", 1)), 1)
    position_term = jnp.zeros((rows_here, cols_here, feature_width), jnp.float32)
    for row_tap in range(3):
        for col_tap in range(3):
            position_term = position_term + conv_w[row_tap, col_tap] * rims[
                row_tap : row_tap + rows_here, col_tap : col_tap + cols_here
            ].astype(jnp.float32)
    return position_term


def split_heads(flat_rows):
    return flat_rows.reshape(flat_rows.shape[:-1] + (flat_rows.shape[-1] // HEAD_DIM, HEAD_DIM))


def attend(softmax_state, queries, key_blocks, value_blocks, allowed):
    old_peak, old_total, old_summed = softmax_state
    scores = (
        jnp.einsum(
            "bqhd,nkhd->bhqnk", queries, key_blocks, preferred_element_type=jnp.float32
        )
        * SCORE_SCALE
    )
    scores = jnp.where(allowed[:, None, None, :, None], scores, -1e30)
    new_peak = jnp.maximum(old_peak, jnp.max(scores, axis=(3, 4)))
    weights = jnp.exp(scores - new_peak[:, :, :, None, None]).astype(jnp.bfloat16)
    factor = jnp.exp(old_peak - new_peak)
    new_total = old_total * factor + jnp.sum(weights.astype(jnp.float32), axis=(3, 4))
    product = jnp.einsum(
        "bhqnk,nkhd->bqhd", weights, value_blocks, preferred_element_type=jnp.float32
    )
    new_summed = old_summed * jnp.transpose(factor, (0, 2, 1))[:, :, :, None] + product
    return (new_peak, new_total, new_summed)


def general_body(
    q_fresh, k_fresh, v_fresh, k_stale, v_stale, text_k, text_v, conv_w, reads, pattern, text_blocks
):
    rows_here, cols_here, feature_width = q_fresh.shape
    blocks_here = rows_here // BLOCK_ROWS
    head_count = feature_width // HEAD_DIM

    def as_blocks(grid_values):
        return split_heads(grid_values.reshape(blocks_here, PER_BLOCK, feature_width))

    queries = as_blocks(q_fresh)
    text_keys, text_values = (
        lax.all_gather(text_k, ("rows", "cols"), axis=0, tiled=True),
        lax.all_gather(text_v, ("rows", "cols"), axis=0, tiled=True),
    )
    text_count = text_keys.shape[0] // PER_BLOCK
    text_keys = split_heads(text_keys.reshape(text_count, PER_BLOCK, feature_width))
    text_values = split_heads(text_values.reshape(text_count, PER_BLOCK, feature_width))
    wanted = pattern[:, 0, :]
    fetch_rows = reads[0, 0, :]
    fetch_count = fetch_rows.shape[0]
    slot_count = blocks_here + fetch_count
    slot_mask = jnp.any(
        wanted[:, :, None] == jnp.arange(slot_count, dtype=jnp.int32)[None, None, :], axis=1
    )
    text_mask = jnp.any(
        text_blocks[:, 0, :, None] == jnp.arange(text_count, dtype=jnp.int32)[None, None, :], axis=1
    )
    softmax_state = (
        jnp.full((blocks_here, head_count, PER_BLOCK), -1e30, jnp.float32),
        jnp.zeros((blocks_here, head_count, PER_BLOCK), jnp.float32),
        jnp.zeros((blocks_here, PER_BLOCK, head_count, HEAD_DIM), jnp.float32),
    )
    softmax_state = attend(
        softmax_state,
        queries,
        jnp.concatenate([as_blocks(k_fresh), text_keys], axis=0),
        jnp.concatenate([as_blocks(v_fresh), text_values], axis=0),
        jnp.concatenate([slot_mask[:, :blocks_here], text_mask], axis=1),
    )
    chosen = jnp.where(
        wanted >= blocks_here, fetch_rows[jnp.clip(wanted - blocks_here, 0, fetch_count - 1)], -1
    )
    piece_keys = lax.all_gather(as_blocks(k_stale), "rows", axis=0, tiled=True)
    piece_values = lax.all_gather(as_blocks(v_stale), "rows", axis=0, tiled=True)
    block_rows = jnp.arange(piece_keys.shape[0], dtype=jnp.int32)
    piece_mask = jnp.any(chosen[:, :, None] == block_rows[None, None, :], axis=1)
    softmax_state = attend(softmax_state, queries, piece_keys, piece_values, piece_mask)
    _, final_total, final_summed = softmax_state
    mixed_rows = final_summed / jnp.transpose(final_total, (0, 2, 1))[:, :, :, None]
    attention = mixed_rows.reshape(rows_here, cols_here, feature_width)
    return attention + position(v_fresh, conv_w)


def head_scores(queries, keys):
    return lax.dot_general(
        queries, keys, (((1,), (1,)), ((), ())), preferred_element_type=jnp.float32
    )


def run_copies(copies, sems):
    copies = [pltpu.make_async_copy(*pair, sems.at[i]) for i, pair in enumerate(copies)]
    for copy in copies:
        copy.start()
    for copy in copies:
        copy.wait()


def pack_kernel(k_hbm, v_hbm, cells, text_k, text_v, stale, beside, diagonal, text, sems):
    tokens, shard = k_hbm.shape[0], text_k.shape[0]
    row = lax.axis_index("rows")
    end = cells.shape[0] - 1
    copies = []
    for which, source in enumerate((text_k, text_v)):
        copies.append((source, text.at[pl.ds(which * shard, shard)]))
    for which, source in enumerate((k_hbm, v_hbm)):
        copies.append((source, stale.at[pl.ds(which * tokens, tokens)]))
    copies.append((cells.at[jnp.where(row % 2 == 0, end, 0)], beside))
    copies.append((cells.at[jnp.where(row < 2, end, 0)], diagonal))
    run_copies(copies, sems)


def offer_kernel(reads_ref, text, out):
    both, width = text.shape
    partner = (lax.axis_index("rows") + 2) % 4

    def flag(owner):
        found = 0
        for turn in range(2):
            entry = reads_ref[0, 0, turn]
            found = jnp.where(entry // 2 == owner, entry % 2, found)
        return jnp.full((8, width // 2), found.astype(jnp.float32), jnp.float32)

    flags = [flag(owner) for owner in (partner, partner + 1 - 2 * (partner % 2))]
    out[pl.ds(0, both), :] = text[...]
    out[pl.ds(both, 8), :] = jnp.concatenate(flags, axis=1).astype(out.dtype)


def send_kernel(across, stale, passed, *outs):
    tokens, width = stale.shape[0] // 2, stale.shape[1]

    def block_of(slot):
        lanes = pl.ds(slot * (width // 2), HEAD_DIM)
        flag = jnp.max(across[pl.ds(across.shape[0] - 8, 8), lanes].astype(jnp.float32))
        return jnp.where(flag > 0.5, PER_BLOCK, 0)

    starts = block_of(0), block_of(1)
    first = 0
    for out in outs:
        part = pl.ds(first, out.shape[1])
        first += out.shape[1]
        for which in range(2):
            for slot, source in enumerate((stale, passed)):
                rows = pl.ds(pl.multiple_of(which * tokens + starts[slot], PER_BLOCK), PER_BLOCK)
                at = (2 * which + slot) * PER_BLOCK
                out[pl.ds(at, PER_BLOCK), :] = source[rows, part]


def bundle_kernel(*refs):
    out = refs[-1]
    at = 0
    for ref in refs[:-1]:
        count = ref.shape[0] - ref.shape[0] % 64
        out[pl.ds(at, count), :] = ref[pl.ds(0, count), :]
        at += count


def choose_kernel(upper, lower, first, second):
    upwards = lax.axis_index("cols") >= 2
    half = first.shape[0]
    for at, out in ((0, first), (half, second)):
        rows = pl.ds(at, half)
        out[...] = jnp.where(upwards, upper[rows, :], lower[rows, :])


def above_below(beside, diagonal):
    first_core = lax.axis_index("rows") % 2 == 0
    return (
        jnp.where(first_core, diagonal, beside),
        jnp.where(first_core, beside, diagonal),
    )


def join_kernel(text, across, cells, beside, diagonal, both, plus, minus):
    shard = text.shape[0] // 2
    rows_here, cols_here, width = cells.shape
    above, below = above_below(beside[...], diagonal[...])
    rows = [above] + [cells[i] for i in range(rows_here)] + [below]
    rows = [row.astype(jnp.float32) for row in rows]
    spare = jnp.zeros((16 - len(rows), width), jnp.float32)
    both[pl.ds(0, 2 * shard), :] = text[...]
    both[pl.ds(2 * shard, 2 * shard), :] = across[pl.ds(0, 2 * shard), :]
    for target in (plus, minus):
        target[pl.ds(0, 2 * shard), :] = across[pl.ds(0, 2 * shard), :]
    for target, at in ((plus, cols_here - 1), (minus, 0)):
        edge = jnp.concatenate([row[at : at + 1] for row in rows] + [spare], axis=0)
        target[pl.ds(2 * shard, 16), :] = edge.astype(target.dtype)


def term_kernel(cells, beside, diagonal, left, right, weights, out):
    rows_here, cols_here, width = cells.shape
    col = lax.axis_index("cols")
    edges = pl.ds(left.shape[0] - 16, 16)
    place = lax.broadcasted_iota(jnp.int32, (cols_here, HEAD_DIM), 0)
    for lane in range(width // HEAD_DIM):
        part = pl.ds(lane * HEAD_DIM, HEAD_DIM)
        above, below = above_below(beside[:, part], diagonal[:, part])
        lefts = left[edges, part].astype(jnp.float32)
        rights = right[edges, part].astype(jnp.float32)
        lefts = jnp.where(col > 0, lefts, 0.0)
        rights = jnp.where(col < 3, rights, 0.0)
        taps = []
        for row in range(rows_here + 2):
            if row == 0:
                centre = above
            elif row == rows_here + 1:
                centre = below
            else:
                centre = cells[row - 1, :, part]
            centre = centre.astype(jnp.float32)
            before = jnp.where(place == 0, lefts[row : row + 1], pltpu.roll(centre, 1, 0))
            after = jnp.where(
                place == cols_here - 1, rights[row : row + 1], pltpu.roll(centre, cols_here - 1, 0)
            )
            taps.append((before, centre, after))
        for row in range(rows_here):
            total = None
            for row_tap in range(3):
                for col_tap in range(3):
                    piece = weights[row_tap, col_tap : col_tap + 1, part] * taps[row + row_tap][col_tap]
                    total = piece if total is None else total + piece
            out[pl.ds(row * cols_here, cols_here), part] = total


def grouped(jobs):
    size = -(-len(jobs) // -(-len(jobs) // GROUP))
    return [jobs[at : at + size] for at in range(0, len(jobs), size)]


def lanes_of(head):
    return pl.ds(head * HEAD_DIM, HEAD_DIM)


def rows_at(block):
    return pl.ds(block * PER_BLOCK, PER_BLOCK)


def text_choice(chosen):
    row = lax.axis_index("rows")
    return chosen % 2 == row % 2, chosen // 2 == row // 2


def pick(from_own, own, other, shard, at, part):
    rows = pl.ds(at * shard, shard)
    return jnp.where(from_own, own[rows, part], other[rows, part])


def early_kernel(
    text_ref, q, k, v, both, both_mate, early, early_mate, left, left_mate, right, right_mate,
    sums, peaks_out, totals_out,
):
    shard = both.shape[0] // 4
    heads = q.shape[1] // HEAD_DIM

    def gathered(block, head, which):
        part = lanes_of(head)
        parts = [(k, v)[which][rows_at(block), part]]
        for turn in range(2):
            from_own, from_near = text_choice(text_ref[block, 0, turn])
            for near, side in (
                ((both, both_mate, which), (both, both_mate, 2 + which)),
                ((early, early_mate, which), (left, left_mate, which)),
                ((early, early_mate, 2 + which), (right, right_mate, which)),
            ):
                parts.append(
                    jnp.where(
                        from_near,
                        pick(from_own, near[0], near[1], shard, near[2], part),
                        pick(from_own, side[0], side[1], shard, side[2], part),
                    )
                )
        return jnp.concatenate(parts, axis=0)

    for group in grouped([(block, head) for head in range(heads) for block in range(2)]):
        scores = [
            head_scores(q[rows_at(block), lanes_of(head)], gathered(block, head, 0))
            for block, head in group
        ]
        peaks = [jnp.max(s, axis=1, keepdims=True) * EXP2_SCALE for s in scores]
        weights = [
            jnp.exp2(s * EXP2_SCALE - peak).astype(jnp.bfloat16) for s, peak in zip(scores, peaks)
        ]
        totals = [jnp.sum(w.astype(jnp.float32), axis=1, keepdims=True) for w in weights]
        for w, peak, total, (block, head) in zip(weights, peaks, totals, group):
            sums[rows_at(block), lanes_of(head)] = jnp.dot(
                w, gathered(block, head, 1), preferred_element_type=jnp.float32
            )
            spread = (PER_BLOCK, HEAD_DIM)
            peaks_out[rows_at(block), lanes_of(head)] = jnp.broadcast_to(peak, spread)
            totals_out[rows_at(block), lanes_of(head)] = jnp.broadcast_to(total, spread)


def late_kernel(first_head, reads_ref, pattern_ref, text_ref, q, *refs):
    sums, old_peaks, old_totals, passed, arrived, term = refs[:6]
    near, near_mate, side, side_mate = refs[6:10]
    target, out, sems = refs[-3:]
    copies = []
    row = lax.axis_index("rows")
    across, core = row // 2, row % 2
    shard = near.shape[0] // 2
    half = 2 * PER_BLOCK

    def far_part(block, head, which):
        slot = pattern_ref[block, 0, 0] + pattern_ref[block, 0, 1] - block - 2
        wanted = reads_ref[0, 0, slot]
        owner = wanted // 2
        mate_at = (wanted % 2) * PER_BLOCK + which * half
        far_at = jnp.where(owner % 2 == core, 0, PER_BLOCK) + which * half
        mate_rows = pl.ds(pl.multiple_of(mate_at, PER_BLOCK), PER_BLOCK)
        far_rows = pl.ds(pl.multiple_of(far_at, PER_BLOCK), PER_BLOCK)
        return jnp.where(
            owner // 2 == across,
            passed[mate_rows, lanes_of(first_head + head)],
            arrived[far_rows, lanes_of(head)],
        )

    def gathered(block, head, which):
        part = lanes_of(first_head + head)
        parts = [far_part(block, head, which)]
        for turn in range(2):
            from_own, from_near = text_choice(text_ref[block, 0, turn])
            parts.append(
                jnp.where(
                    from_near,
                    pick(from_own, near, near_mate, shard, which, part),
                    pick(from_own, side, side_mate, shard, which, part),
                )
            )
        return jnp.concatenate(parts, axis=0)

    count = arrived.shape[1] // HEAD_DIM
    for group in grouped([(block, head) for head in range(count) for block in range(2)]):
        scores = [
            head_scores(q[rows_at(block), lanes_of(first_head + head)], gathered(block, head, 0))
            for block, head in group
        ]
        olds = [old_peaks[rows_at(block), lanes_of(first_head + head)] for block, head in group]
        peaks = [
            jnp.maximum(old, jnp.max(s, axis=1, keepdims=True) * EXP2_SCALE)
            for s, old in zip(scores, olds)
        ]
        weights = []
        for s, peak in zip(scores, peaks):
            wide = jnp.concatenate([peak, peak[:, : s.shape[1] - HEAD_DIM]], axis=1)
            weights.append(jnp.exp2(s * EXP2_SCALE - wide).astype(jnp.bfloat16))
        totals = [jnp.sum(w.astype(jnp.float32), axis=1, keepdims=True) for w in weights]
        products = [
            jnp.dot(w, gathered(block, head, 1), preferred_element_type=jnp.float32)
            for w, (block, head) in zip(weights, group)
        ]
        for product, total, old, peak, (block, head) in zip(products, totals, olds, peaks, group):
            rows, part = rows_at(block), lanes_of(first_head + head)
            factor = jnp.exp2(old - peak)
            total = old_totals[rows, part] * factor + total
            summed = sums[rows, part] * factor + product
            out[rows, lanes_of(head)] = summed / total + term[rows, part]
        first, width = group[0][1], (group[-1][1] + 1 - group[0][1]) * HEAD_DIM
        copies.append(
            pltpu.make_async_copy(
                out.at[:, pl.ds(first * HEAD_DIM, width)],
                target.at[:, pl.ds((first_head + first) * HEAD_DIM, width)],
                sems.at[len(copies)],
            )
        )
        copies[-1].start()
    for copy in copies:
        copy.wait()


def body(
    q_fresh, k_fresh, v_fresh, k_stale, v_stale, text_k, text_v, conv_w, reads, pattern, text_blocks
):
    rows_here, cols_here, width = q_fresh.shape
    tokens = rows_here * cols_here
    shard = text_k.shape[0]
    swap = [(r, (r + 2) % 4) for r in range(4)]
    mates = [(r, r ^ 1) for r in range(4)]
    in_vmem = pl.BlockSpec(memory_space=pltpu.VMEM)
    in_hbm = pl.BlockSpec(memory_space=pltpu.HBM)
    params = pltpu.CompilerParams(vmem_limit_bytes=VMEM_LIMIT)
    cost = pl.CostEstimate(flops=1 << 20, transcendentals=0, bytes_accessed=1 << 16)

    def after(value, *others):
        return lax.optimization_barrier((value, *others))[0]

    def flat(grid_values):
        return grid_values.reshape(tokens, width)

    def to_mate(values):
        return lax.ppermute(values, "rows", mates)

    def rows_of(*counts):
        shapes = tuple(jax.ShapeDtypeStruct((n, width), jnp.bfloat16) for n in counts)
        return shapes if len(shapes) > 1 else shapes[0]

    def local(kernel, name, shapes, *args, specs=None, scratch=()):
        many = isinstance(shapes, tuple)
        return pl.pallas_call(
            kernel,
            out_shape=shapes,
            in_specs=specs or [in_vmem] * len(args),
            out_specs=(in_vmem,) * len(shapes) if many else in_vmem,
            scratch_shapes=scratch,
            compiler_params=params,
            cost_estimate=cost,
            name=name,
        )(*args)

    chunks = tuple(
        jax.ShapeDtypeStruct((2 * tokens, n * HEAD_DIM), jnp.bfloat16) for n in CHUNK_HEADS
    )
    in_place = [
        pltpu.with_memory_space_constraint(value, pltpu.HBM)
        for value in (flat(k_stale), flat(v_stale), v_fresh, text_k, text_v)
    ]
    stale, beside, diagonal, text = local(
        pack_kernel,
        "pack",
        rows_of(2 * tokens, cols_here, cols_here, 2 * shard),
        *in_place,
        specs=[in_hbm] * 5,
        scratch=[pltpu.SemaphoreType.DMA((6,))],
    )
    forward = [(i, (i + 1) % 4) for i in range(4)]
    backward = [(i, (i + 3) % 4) for i in range(4)]

    near_parts = [lax.ppermute(text, "cols", p) for p in (forward, backward)]
    beside = to_mate(beside)
    diagonal = lax.ppermute(diagonal, "rows", [(1, 2), (2, 1)])
    offer = local(
        offer_kernel,
        "offer",
        rows_of(2 * shard + 8),
        reads,
        text,
        specs=[pl.BlockSpec(memory_space=pltpu.SMEM), in_vmem],
    )
    across = lax.ppermute(offer, "rows", swap)
    passed = to_mate(stale)
    packed = local(
        send_kernel, "send", chunks, after(across, diagonal), stale, passed
    )
    far = [lax.ppermute(chunk, "rows", swap) for chunk in packed]

    both, plus, minus = local(
        join_kernel,
        "join",
        rows_of(4 * shard, 2 * shard + 16, 2 * shard + 16),
        text,
        after(across, packed[0]),
        v_fresh,
        beside,
        diagonal,
    )
    left = lax.ppermute(plus, "cols", forward)
    right = lax.ppermute(minus, "cols", backward)
    early = local(bundle_kernel, "bundle", rows_of(4 * shard), *near_parts)
    early_mate, both_mate = to_mate(early), to_mate(both)
    near_parts[0] = after(near_parts[0], early_mate, both_mate)
    upper, lower = (
        local(bundle_kernel, "pair", rows_of(4 * shard), *pair)
        for pair in ((near_parts[0], left), (near_parts[1], right))
    )
    upper = lax.ppermute(upper, "cols", [(1, 2), (2, 3)])
    lower = lax.ppermute(lower, "cols", [(1, 0), (2, 1)])
    left_mate, right_mate = to_mate(left), to_mate(right)
    sums, peaks, totals = local(
        early_kernel,
        "early",
        (jax.ShapeDtypeStruct((tokens, width), jnp.float32),) * 3,
        text_blocks, flat(q_fresh), flat(k_fresh), flat(v_fresh),
        both, both_mate, early, early_mate, left, left_mate, right, right_mate,
        specs=[pl.BlockSpec(memory_space=pltpu.SMEM)] + [in_vmem] * 11,
    )
    upper, lower = after(upper, sums), after(lower, sums)
    far_side = local(choose_kernel, "choose", rows_of(2 * shard, 2 * shard), upper, lower)
    late = [part for side in far_side for part in (side, to_mate(side))]
    term = local(
        term_kernel,
        "term",
        jax.ShapeDtypeStruct((tokens, width), jnp.float32),
        v_fresh, beside, diagonal, left, right, conv_w,
    )

    out = None
    first_head = 0
    for chunk, head_count in enumerate(CHUNK_HEADS):
        if out is not None:
            far[chunk] = after(far[chunk], out)
        out = pl.pallas_call(
            functools.partial(late_kernel, first_head),
            out_shape=jax.ShapeDtypeStruct((tokens, width), jnp.float32),
            grid_spec=pltpu.PrefetchScalarGridSpec(
                num_scalar_prefetch=3,
                grid=(1,),
                in_specs=[in_vmem] * 11 + [in_hbm] * (out is not None),
                out_specs=in_hbm,
                scratch_shapes=[
                    pltpu.VMEM((tokens, head_count * HEAD_DIM), jnp.float32),
                    pltpu.SemaphoreType.DMA((4,)),
                ],
            ),
            input_output_aliases={14: 0} if out is not None else {},
            compiler_params=params,
            cost_estimate=cost,
            name=f"late{chunk}",
        )(
            reads, pattern, text_blocks, flat(q_fresh), sums, peaks, totals,
            passed, far[chunk], term, *late,
            *([out] if out is not None else []),
        )
        first_head += head_count
    return out.reshape(rows_here, cols_here, width)


def fits(mesh, reads, pattern, text_k):
    sizes = dict(mesh.shape)
    return (
        sizes["rows"] == 4
        and sizes["cols"] == 4
        and reads.shape[-1] == 2
        and pattern.shape[-1] == 2
        and pattern.shape[0] == 2 * sizes["groups"] * 4
        and text_k.shape[0] == sizes["groups"] * 4 * PER_BLOCK
    )


def solution(mesh):
    grid = P(("groups", "rows"), "cols", None)
    text = P(("groups", "rows", "cols"), None)
    in_specs = (grid, grid, grid, grid, grid, text, text, P(), grid, grid, grid)

    def program(*args):
        chosen = body if fits(mesh, args[8], args[9], args[5]) else general_body
        return jax.shard_map(
            chosen, mesh=mesh, in_specs=in_specs, out_specs=grid, check_vma=False
        )(*args)

    return program
```

```python
import functools
import math

import jax
import jax.numpy as jnp
from jax import lax
from jax.experimental import pallas as pl
from jax.experimental.pallas import tpu as pltpu
from jax.sharding import PartitionSpec as P

HEAD_DIM = 128
BLOCK_ROWS = 4
BLOCK_COLS = 32
PER_BLOCK = BLOCK_ROWS * BLOCK_COLS
SCORE_SCALE = 1.0 / math.sqrt(HEAD_DIM)
EXP2_SCALE = SCORE_SCALE * math.log2(math.e)
CHUNK_HEADS = (9, 3)
GROUP = 8
VMEM_LIMIT = 24 * 1024 * 1024


def extended(cells, sides, width):
    for axis, dim in sides:
        count = lax.axis_size(axis)
        ends = count - 1
        head = lax.slice_in_dim(cells, 0, width, axis=dim)
        tail = lax.slice_in_dim(cells, cells.shape[dim] - width, cells.shape[dim], axis=dim)
        cells = jnp.concatenate(
            [
                lax.ppermute(tail, axis, [(i, (i + 1) % count) for i in range(ends)]),
                cells,
                lax.ppermute(head, axis, [((i + 1) % count, i) for i in range(ends)]),
            ],
            axis=dim,
        )
    return cells


def position(v_fresh, conv_w):
    rows_here, cols_here, feature_width = v_fresh.shape
    rims = extended(v_fresh, (("rows", 0), ("cols", 1)), 1)
    position_term = jnp.zeros((rows_here, cols_here, feature_width), jnp.float32)
    for row_tap in range(3):
        for col_tap in range(3):
            position_term = position_term + conv_w[row_tap, col_tap] * rims[
                row_tap : row_tap + rows_here, col_tap : col_tap + cols_here
            ].astype(jnp.float32)
    return position_term


def split_heads(flat_rows):
    return flat_rows.reshape(flat_rows.shape[:-1] + (flat_rows.shape[-1] // HEAD_DIM, HEAD_DIM))


def attend(softmax_state, queries, key_blocks, value_blocks, allowed):
    old_peak, old_total, old_summed = softmax_state
    scores = (
        jnp.einsum(
            "bqhd,nkhd->bhqnk", queries, key_blocks, preferred_element_type=jnp.float32
        )
        * SCORE_SCALE
    )
    scores = jnp.where(allowed[:, None, None, :, None], scores, -1e30)
    new_peak = jnp.maximum(old_peak, jnp.max(scores, axis=(3, 4)))
    weights = jnp.exp(scores - new_peak[:, :, :, None, None]).astype(jnp.bfloat16)
    factor = jnp.exp(old_peak - new_peak)
    new_total = old_total * factor + jnp.sum(weights.astype(jnp.float32), axis=(3, 4))
    product = jnp.einsum(
        "bhqnk,nkhd->bqhd", weights, value_blocks, preferred_element_type=jnp.float32
    )
    new_summed = old_summed * jnp.transpose(factor, (0, 2, 1))[:, :, :, None] + product
    return (new_peak, new_total, new_summed)


def general_body(
    q_fresh, k_fresh, v_fresh, k_stale, v_stale, text_k, text_v, conv_w, reads, pattern, text_blocks
):
    rows_here, cols_here, feature_width = q_fresh.shape
    blocks_here = rows_here // BLOCK_ROWS
    head_count = feature_width // HEAD_DIM

    def as_blocks(grid_values):
        return split_heads(grid_values.reshape(blocks_here, PER_BLOCK, feature_width))

    queries = as_blocks(q_fresh)
    text_keys, text_values = (
        lax.all_gather(text_k, ("rows", "cols"), axis=0, tiled=True),
        lax.all_gather(text_v, ("rows", "cols"), axis=0, tiled=True),
    )
    text_count = text_keys.shape[0] // PER_BLOCK
    text_keys = split_heads(text_keys.reshape(text_count, PER_BLOCK, feature_width))
    text_values = split_heads(text_values.reshape(text_count, PER_BLOCK, feature_width))
    wanted = pattern[:, 0, :]
    fetch_rows = reads[0, 0, :]
    fetch_count = fetch_rows.shape[0]
    slot_count = blocks_here + fetch_count
    slot_mask = jnp.any(
        wanted[:, :, None] == jnp.arange(slot_count, dtype=jnp.int32)[None, None, :], axis=1
    )
    text_mask = jnp.any(
        text_blocks[:, 0, :, None] == jnp.arange(text_count, dtype=jnp.int32)[None, None, :], axis=1
    )
    softmax_state = (
        jnp.full((blocks_here, head_count, PER_BLOCK), -1e30, jnp.float32),
        jnp.zeros((blocks_here, head_count, PER_BLOCK), jnp.float32),
        jnp.zeros((blocks_here, PER_BLOCK, head_count, HEAD_DIM), jnp.float32),
    )
    softmax_state = attend(
        softmax_state,
        queries,
        jnp.concatenate([as_blocks(k_fresh), text_keys], axis=0),
        jnp.concatenate([as_blocks(v_fresh), text_values], axis=0),
        jnp.concatenate([slot_mask[:, :blocks_here], text_mask], axis=1),
    )
    chosen = jnp.where(
        wanted >= blocks_here, fetch_rows[jnp.clip(wanted - blocks_here, 0, fetch_count - 1)], -1
    )
    piece_keys = lax.all_gather(as_blocks(k_stale), "rows", axis=0, tiled=True)
    piece_values = lax.all_gather(as_blocks(v_stale), "rows", axis=0, tiled=True)
    block_rows = jnp.arange(piece_keys.shape[0], dtype=jnp.int32)
    piece_mask = jnp.any(chosen[:, :, None] == block_rows[None, None, :], axis=1)
    softmax_state = attend(softmax_state, queries, piece_keys, piece_values, piece_mask)
    _, final_total, final_summed = softmax_state
    mixed_rows = final_summed / jnp.transpose(final_total, (0, 2, 1))[:, :, :, None]
    attention = mixed_rows.reshape(rows_here, cols_here, feature_width)
    return attention + position(v_fresh, conv_w)


def head_scores(queries, keys):
    return lax.dot_general(
        queries, keys, (((1,), (1,)), ((), ())), preferred_element_type=jnp.float32
    )


def run_copies(copies, sems):
    copies = [pltpu.make_async_copy(*pair, sems.at[i]) for i, pair in enumerate(copies)]
    for copy in copies:
        copy.start()
    for copy in copies:
        copy.wait()


def pack_kernel(k_hbm, v_hbm, cells, text_k, text_v, stale, beside, diagonal, text, sems):
    tokens, shard = k_hbm.shape[0], text_k.shape[0]
    row = lax.axis_index("rows")
    end = cells.shape[0] - 1
    copies = []
    for which, source in enumerate((text_k, text_v)):
        copies.append((source, text.at[pl.ds(which * shard, shard)]))
    for which, source in enumerate((k_hbm, v_hbm)):
        copies.append((source, stale.at[pl.ds(which * tokens, tokens)]))
    copies.append((cells.at[jnp.where(row % 2 == 0, end, 0)], beside))
    copies.append((cells.at[jnp.where(row < 2, end, 0)], diagonal))
    run_copies(copies, sems)


def offer_kernel(reads_ref, text, out):
    both, width = text.shape
    partner = (lax.axis_index("rows") + 2) % 4

    def flag(owner):
        found = 0
        for turn in range(2):
            entry = reads_ref[0, 0, turn]
            found = jnp.where(entry // 2 == owner, entry % 2, found)
        return jnp.full((8, width // 2), found.astype(jnp.float32), jnp.float32)

    flags = [flag(owner) for owner in (partner, partner + 1 - 2 * (partner % 2))]
    out[pl.ds(0, both), :] = text[...]
    out[pl.ds(both, 8), :] = jnp.concatenate(flags, axis=1).astype(out.dtype)


def send_kernel(across, stale, passed, *outs):
    tokens, width = stale.shape[0] // 2, stale.shape[1]

    def block_of(slot):
        lanes = pl.ds(slot * (width // 2), HEAD_DIM)
        flag = jnp.max(across[pl.ds(across.shape[0] - 8, 8), lanes].astype(jnp.float32))
        return jnp.where(flag > 0.5, PER_BLOCK, 0)

    starts = block_of(0), block_of(1)
    first = 0
    for out in outs:
        part = pl.ds(first, out.shape[1])
        first += out.shape[1]
        for which in range(2):
            for slot, source in enumerate((stale, passed)):
                rows = pl.ds(pl.multiple_of(which * tokens + starts[slot], PER_BLOCK), PER_BLOCK)
                at = (2 * which + slot) * PER_BLOCK
                out[pl.ds(at, PER_BLOCK), :] = source[rows, part]


def bundle_kernel(*refs):
    out = refs[-1]
    at = 0
    for ref in refs[:-1]:
        count = ref.shape[0] - ref.shape[0] % 64
        out[pl.ds(at, count), :] = ref[pl.ds(0, count), :]
        at += count


def choose_kernel(upper, lower, first, second):
    upwards = lax.axis_index("cols") >= 2
    half = first.shape[0]
    for at, out in ((0, first), (half, second)):
        rows = pl.ds(at, half)
        out[...] = jnp.where(upwards, upper[rows, :], lower[rows, :])


def above_below(beside, diagonal):
    first_core = lax.axis_index("rows") % 2 == 0
    return (
        jnp.where(first_core, diagonal, beside),
        jnp.where(first_core, beside, diagonal),
    )


def join_kernel(text, across, cells, beside, diagonal, both, plus, minus):
    shard = text.shape[0] // 2
    rows_here, cols_here, width = cells.shape
    above, below = above_below(beside[...], diagonal[...])
    rows = [above] + [cells[i] for i in range(rows_here)] + [below]
    rows = [row.astype(jnp.float32) for row in rows]
    spare = jnp.zeros((16 - len(rows), width), jnp.float32)
    both[pl.ds(0, 2 * shard), :] = text[...]
    both[pl.ds(2 * shard, 2 * shard), :] = across[pl.ds(0, 2 * shard), :]
    for target in (plus, minus):
        target[pl.ds(0, 2 * shard), :] = across[pl.ds(0, 2 * shard), :]
    for target, at in ((plus, cols_here - 1), (minus, 0)):
        edge = jnp.concatenate([row[at : at + 1] for row in rows] + [spare], axis=0)
        target[pl.ds(2 * shard, 16), :] = edge.astype(target.dtype)


def term_kernel(cells, beside, diagonal, left, right, weights, out):
    rows_here, cols_here, width = cells.shape
    col = lax.axis_index("cols")
    edges = pl.ds(left.shape[0] - 16, 16)
    place = lax.broadcasted_iota(jnp.int32, (cols_here, HEAD_DIM), 0)
    for lane in range(width // HEAD_DIM):
        part = pl.ds(lane * HEAD_DIM, HEAD_DIM)
        above, below = above_below(beside[:, part], diagonal[:, part])
        lefts = left[edges, part].astype(jnp.float32)
        rights = right[edges, part].astype(jnp.float32)
        lefts = jnp.where(col > 0, lefts, 0.0)
        rights = jnp.where(col < 3, rights, 0.0)
        taps = []
        for row in range(rows_here + 2):
            if row == 0:
                centre = above
            elif row == rows_here + 1:
                centre = below
            else:
                centre = cells[row - 1, :, part]
            centre = centre.astype(jnp.float32)
            before = jnp.where(place == 0, lefts[row : row + 1], pltpu.roll(centre, 1, 0))
            after = jnp.where(
                place == cols_here - 1, rights[row : row + 1], pltpu.roll(centre, cols_here - 1, 0)
            )
            taps.append((before, centre, after))
        for row in range(rows_here):
            total = None
            for row_tap in range(3):
                for col_tap in range(3):
                    piece = weights[row_tap, col_tap : col_tap + 1, part] * taps[row + row_tap][col_tap]
                    total = piece if total is None else total + piece
            out[pl.ds(row * cols_here, cols_here), part] = total


def grouped(jobs):
    size = -(-len(jobs) // -(-len(jobs) // GROUP))
    return [jobs[at : at + size] for at in range(0, len(jobs), size)]


def lanes_of(head):
    return pl.ds(head * HEAD_DIM, HEAD_DIM)


def rows_at(block):
    return pl.ds(block * PER_BLOCK, PER_BLOCK)


def text_choice(chosen):
    row = lax.axis_index("rows")
    return chosen % 2 == row % 2, chosen // 2 == row // 2


def pick(from_own, own, other, shard, at, part):
    rows = pl.ds(at * shard, shard)
    return jnp.where(from_own, own[rows, part], other[rows, part])


def early_kernel(
    text_ref, q, k, v, both, both_mate, early, early_mate, left, left_mate, right, right_mate,
    sums, peaks_out, totals_out,
):
    shard = both.shape[0] // 4
    heads = q.shape[1] // HEAD_DIM

    def gathered(block, head, which):
        part = lanes_of(head)
        parts = [(k, v)[which][rows_at(block), part]]
        for turn in range(2):
            from_own, from_near = text_choice(text_ref[block, 0, turn])
            for near, side in (
                ((both, both_mate, which), (both, both_mate, 2 + which)),
                ((early, early_mate, which), (left, left_mate, which)),
                ((early, early_mate, 2 + which), (right, right_mate, which)),
            ):
                parts.append(
                    jnp.where(
                        from_near,
                        pick(from_own, near[0], near[1], shard, near[2], part),
                        pick(from_own, side[0], side[1], shard, side[2], part),
                    )
                )
        return jnp.concatenate(parts, axis=0)

    for group in grouped([(block, head) for head in range(heads) for block in range(2)]):
        scores = [
            head_scores(q[rows_at(block), lanes_of(head)], gathered(block, head, 0))
            for block, head in group
        ]
        peaks = [jnp.max(s, axis=1, keepdims=True) * EXP2_SCALE for s in scores]
        weights = [
            jnp.exp2(s * EXP2_SCALE - peak).astype(jnp.bfloat16) for s, peak in zip(scores, peaks)
        ]
        totals = [jnp.sum(w.astype(jnp.float32), axis=1, keepdims=True) for w in weights]
        for w, peak, total, (block, head) in zip(weights, peaks, totals, group):
            sums[rows_at(block), lanes_of(head)] = jnp.dot(
                w, gathered(block, head, 1), preferred_element_type=jnp.float32
            )
            spread = (PER_BLOCK, HEAD_DIM)
            peaks_out[rows_at(block), lanes_of(head)] = jnp.broadcast_to(peak, spread)
            totals_out[rows_at(block), lanes_of(head)] = jnp.broadcast_to(total, spread)


def late_kernel(first_head, reads_ref, pattern_ref, text_ref, q, *refs):
    sums, old_peaks, old_totals, passed, arrived, term = refs[:6]
    near, near_mate, side, side_mate = refs[6:10]
    target, out, sems = refs[-3:]
    copies = []
    row = lax.axis_index("rows")
    across, core = row // 2, row % 2
    shard = near.shape[0] // 2
    half = 2 * PER_BLOCK

    def far_part(block, head, which):
        slot = pattern_ref[block, 0, 0] + pattern_ref[block, 0, 1] - block - 2
        wanted = reads_ref[0, 0, slot]
        owner = wanted // 2
        mate_at = (wanted % 2) * PER_BLOCK + which * half
        far_at = jnp.where(owner % 2 == core, 0, PER_BLOCK) + which * half
        mate_rows = pl.ds(pl.multiple_of(mate_at, PER_BLOCK), PER_BLOCK)
        far_rows = pl.ds(pl.multiple_of(far_at, PER_BLOCK), PER_BLOCK)
        return jnp.where(
            owner // 2 == across,
            passed[mate_rows, lanes_of(first_head + head)],
            arrived[far_rows, lanes_of(head)],
        )

    def gathered(block, head, which):
        part = lanes_of(first_head + head)
        parts = [far_part(block, head, which)]
        for turn in range(2):
            from_own, from_near = text_choice(text_ref[block, 0, turn])
            parts.append(
                jnp.where(
                    from_near,
                    pick(from_own, near, near_mate, shard, which, part),
                    pick(from_own, side, side_mate, shard, which, part),
                )
            )
        return jnp.concatenate(parts, axis=0)

    count = arrived.shape[1] // HEAD_DIM
    for group in grouped([(block, head) for head in range(count) for block in range(2)]):
        scores = [
            head_scores(q[rows_at(block), lanes_of(first_head + head)], gathered(block, head, 0))
            for block, head in group
        ]
        olds = [old_peaks[rows_at(block), lanes_of(first_head + head)] for block, head in group]
        peaks = [
            jnp.maximum(old, jnp.max(s, axis=1, keepdims=True) * EXP2_SCALE)
            for s, old in zip(scores, olds)
        ]
        weights = []
        for s, peak in zip(scores, peaks):
            wide = jnp.concatenate([peak, peak[:, : s.shape[1] - HEAD_DIM]], axis=1)
            weights.append(jnp.exp2(s * EXP2_SCALE - wide).astype(jnp.bfloat16))
        totals = [jnp.sum(w.astype(jnp.float32), axis=1, keepdims=True) for w in weights]
        products = [
            jnp.dot(w, gathered(block, head, 1), preferred_element_type=jnp.float32)
            for w, (block, head) in zip(weights, group)
        ]
        for product, total, old, peak, (block, head) in zip(products, totals, olds, peaks, group):
            rows, part = rows_at(block), lanes_of(first_head + head)
            factor = jnp.exp2(old - peak)
            total = old_totals[rows, part] * factor + total
            summed = sums[rows, part] * factor + product
            out[rows, lanes_of(head)] = summed / total + term[rows, part]
        first, width = group[0][1], (group[-1][1] + 1 - group[0][1]) * HEAD_DIM
        copies.append(
            pltpu.make_async_copy(
                out.at[:, pl.ds(first * HEAD_DIM, width)],
                target.at[:, pl.ds((first_head + first) * HEAD_DIM, width)],
                sems.at[len(copies)],
            )
        )
        copies[-1].start()
    for copy in copies:
        copy.wait()


def body(
    q_fresh, k_fresh, v_fresh, k_stale, v_stale, text_k, text_v, conv_w, reads, pattern, text_blocks
):
    rows_here, cols_here, width = q_fresh.shape
    tokens = rows_here * cols_here
    shard = text_k.shape[0]
    swap = [(r, (r + 2) % 4) for r in range(4)]
    mates = [(r, r ^ 1) for r in range(4)]
    in_vmem = pl.BlockSpec(memory_space=pltpu.VMEM)
    in_hbm = pl.BlockSpec(memory_space=pltpu.HBM)
    params = pltpu.CompilerParams(vmem_limit_bytes=VMEM_LIMIT)
    cost = pl.CostEstimate(flops=1 << 20, transcendentals=0, bytes_accessed=1 << 16)

    def after(value, *others):
        return lax.optimization_barrier((value, *others))[0]

    def flat(grid_values):
        return grid_values.reshape(tokens, width)

    def to_mate(values):
        return lax.ppermute(values, "rows", mates)

    def rows_of(*counts):
        shapes = tuple(jax.ShapeDtypeStruct((n, width), jnp.bfloat16) for n in counts)
        return shapes if len(shapes) > 1 else shapes[0]

    def local(kernel, name, shapes, *args, specs=None, scratch=()):
        many = isinstance(shapes, tuple)
        return pl.pallas_call(
            kernel,
            out_shape=shapes,
            in_specs=specs or [in_vmem] * len(args),
            out_specs=(in_vmem,) * len(shapes) if many else in_vmem,
            scratch_shapes=scratch,
            compiler_params=params,
            cost_estimate=cost,
            name=name,
        )(*args)

    chunks = tuple(
        jax.ShapeDtypeStruct((2 * tokens, n * HEAD_DIM), jnp.bfloat16) for n in CHUNK_HEADS
    )
    in_place = [
        pltpu.with_memory_space_constraint(value, pltpu.HBM)
        for value in (flat(k_stale), flat(v_stale), v_fresh, text_k, text_v)
    ]
    stale, beside, diagonal, text = local(
        pack_kernel,
        "pack",
        rows_of(2 * tokens, cols_here, cols_here, 2 * shard),
        *in_place,
        specs=[in_hbm] * 5,
        scratch=[pltpu.SemaphoreType.DMA((6,))],
    )
    forward = [(i, (i + 1) % 4) for i in range(4)]
    backward = [(i, (i + 3) % 4) for i in range(4)]

    near_parts = [lax.ppermute(text, "cols", p) for p in (forward, backward)]
    beside = to_mate(beside)
    diagonal = lax.ppermute(diagonal, "rows", [(1, 2), (2, 1)])
    offer = local(
        offer_kernel,
        "offer",
        rows_of(2 * shard + 8),
        reads,
        text,
        specs=[pl.BlockSpec(memory_space=pltpu.SMEM), in_vmem],
    )
    across = lax.ppermute(offer, "rows", swap)
    passed = to_mate(stale)
    packed = local(
        send_kernel, "send", chunks, after(across, diagonal), stale, passed
    )
    far = [lax.ppermute(chunk, "rows", swap) for chunk in packed]

    both, plus, minus = local(
        join_kernel,
        "join",
        rows_of(4 * shard, 2 * shard + 16, 2 * shard + 16),
        text,
        after(across, packed[0]),
        v_fresh,
        beside,
        diagonal,
    )
    left = lax.ppermute(plus, "cols", forward)
    right = lax.ppermute(minus, "cols", backward)
    early = local(bundle_kernel, "bundle", rows_of(4 * shard), *near_parts)
    early_mate, both_mate = to_mate(early), to_mate(both)
    near_parts[0] = after(near_parts[0], early_mate, both_mate)
    upper, lower = (
        local(bundle_kernel, "pair", rows_of(4 * shard), *pair)
        for pair in ((near_parts[0], left), (near_parts[1], right))
    )
    upper = lax.ppermute(upper, "cols", [(1, 2), (2, 3)])
    lower = lax.ppermute(lower, "cols", [(1, 0), (2, 1)])
    left_mate, right_mate = to_mate(left), to_mate(right)
    sums, peaks, totals = local(
        early_kernel,
        "early",
        (jax.ShapeDtypeStruct((tokens, width), jnp.float32),) * 3,
        text_blocks, flat(q_fresh), flat(k_fresh), flat(v_fresh),
        both, both_mate, early, early_mate, left, left_mate, right, right_mate,
        specs=[pl.BlockSpec(memory_space=pltpu.SMEM)] + [in_vmem] * 11,
    )
    term = local(
        term_kernel,
        "term",
        jax.ShapeDtypeStruct((tokens, width), jnp.float32),
        v_fresh, beside, diagonal, left, right, conv_w,
    )
    upper, lower = after(upper, sums, term), after(lower, sums, term)
    far_side = local(choose_kernel, "choose", rows_of(2 * shard, 2 * shard), upper, lower)
    late = [part for side in far_side for part in (side, to_mate(side))]

    out = None
    first_head = 0
    for chunk, head_count in enumerate(CHUNK_HEADS):
        if out is not None:
            far[chunk] = after(far[chunk], out)
        out = pl.pallas_call(
            functools.partial(late_kernel, first_head),
            out_shape=jax.ShapeDtypeStruct((tokens, width), jnp.float32),
            grid_spec=pltpu.PrefetchScalarGridSpec(
                num_scalar_prefetch=3,
                grid=(1,),
                in_specs=[in_vmem] * 11 + [in_hbm] * (out is not None),
                out_specs=in_hbm,
                scratch_shapes=[
                    pltpu.VMEM((tokens, head_count * HEAD_DIM), jnp.float32),
                    pltpu.SemaphoreType.DMA((4,)),
                ],
            ),
            input_output_aliases={14: 0} if out is not None else {},
            compiler_params=params,
            cost_estimate=cost,
            name=f"late{chunk}",
        )(
            reads, pattern, text_blocks, flat(q_fresh), sums, peaks, totals,
            passed, far[chunk], term, *late,
            *([out] if out is not None else []),
        )
        first_head += head_count
    return out.reshape(rows_here, cols_here, width)


def fits(mesh, reads, pattern, text_k):
    sizes = dict(mesh.shape)
    return (
        sizes["rows"] == 4
        and sizes["cols"] == 4
        and reads.shape[-1] == 2
        and pattern.shape[-1] == 2
        and pattern.shape[0] == 2 * sizes["groups"] * 4
        and text_k.shape[0] == sizes["groups"] * 4 * PER_BLOCK
    )


def solution(mesh):
    grid = P(("groups", "rows"), "cols", None)
    text = P(("groups", "rows", "cols"), None)
    in_specs = (grid, grid, grid, grid, grid, text, text, P(), grid, grid, grid)

    def program(*args):
        chosen = body if fits(mesh, args[8], args[9], args[5]) else general_body
        return jax.shard_map(
            chosen, mesh=mesh, in_specs=in_specs, out_specs=grid, check_vma=False
        )(*args)

    return program
```
